32 devices in a mesh: stream: 2 (over x), mp: 4 (over z), dp: 4 (over y, core).
Axes of the slice: x: 2, y: 2, z: 4, core: 2. Of those that a mesh axis runs over, the one named last changes fastest.
Arguments:
- hidden: bfloat16 [2, 4096, 1024], P('stream', 'dp'), may hold values from -6 to 6
- cotangent: bfloat16 [2, 4096, 1024], P('stream', 'dp'), may hold values from -6 to 6
- segments: int32 [2, 32, 128], P(None, 'dp'), may hold values from 0 to 3, never falling along the last dimension, each value on 1 to 36 neighbouring positions
- cross_in: bfloat16 [2, 1024, 3, 1024], P('stream', None, None, 'mp'), may hold values from -0.1875 to 0.1875
- cross_bias: bfloat16 [2, 2, 1024], P('stream', None, 'mp'), may hold values from -3 to 3
- cross_out: bfloat16 [2, 1024, 1024], P('stream', 'mp'), may hold values from -1 to 1
- up_weight: bfloat16 [2, 1024, 3072], P('stream', None, 'mp'), may hold values from -0.1875 to 0.1875
- up_bias: bfloat16 [2, 3072], P('stream', 'mp'), may hold values from -3 to 3
- down_weight: bfloat16 [2, 3072, 1024], P('stream', 'mp'), may hold values from -0.1875 to 0.1875
- attend_in: bfloat16 [2, 1024, 3, 1024], P('stream', None, None, 'mp'), may hold values from -0.1875 to 0.1875
- attend_bias: bfloat16 [2, 2, 1024], P('stream', None, 'mp'), may hold values from -3 to 3
- attend_out: bfloat16 [2, 1024, 1024], P('stream', 'mp'), may hold values from -1 to 1
- out_bias: bfloat16 [2, 3, 1024], P('stream'), may hold values from -3 to 3
- norm_gains: bfloat16 [2, 3, 1024], P('stream'), may hold values from 0.5 to 1.5
- norm_shifts: bfloat16 [2, 3, 1024], P('stream'), may hold values from -3 to 3
Outputs:
- layer_out: bfloat16 [2, 4096, 1024], P('stream', 'dp')
- hidden_grad: bfloat16 [2, 4096, 1024], P('stream', 'dp')
- cross_in_grad: float32 [2, 1024, 3, 1024], P('stream', 'dp', None, 'mp')
- cross_bias_grad: float32 [2, 2, 1024], P('stream', None, ('mp', 'dp'))
- cross_out_grad: float32 [2, 1024, 1024], P('stream', 'mp', 'dp')
- up_weight_grad: float32 [2, 1024, 3072], P('stream', 'dp', 'mp')
- up_bias_grad: float32 [2, 3072], P('stream', ('mp', 'dp'))
- down_weight_grad: float32 [2, 3072, 1024], P('stream', 'mp', 'dp')
- attend_in_grad: float32 [2, 1024, 3, 1024], P('stream', 'dp', None, 'mp')
- attend_bias_grad: float32 [2, 2, 1024], P('stream', None, ('mp', 'dp'))
- attend_out_grad: float32 [2, 1024, 1024], P('stream', 'mp', 'dp')
- out_bias_grad: float32 [2, 3, 1024], P('stream', None, 'dp')
- norm_gains_grad: float32 [2, 3, 1024], P('stream', None, 'dp')
- norm_shifts_grad: float32 [2, 3, 1024], P('stream', None, 'dp')
The draws below stay inside these ranges and needn't reach their ends.
Inputs may be any that keep to these rules, and one draw needn't show every extreme that they name: `segments`: along each row of 128 positions the numbers never fall; each of the 4 numbers covers 1 to 36 positions, one of them exactly 36; caption k of a text row belongs with image k of the same image row.
All inputs are finite; a program needn't handle non-finite values.
Results may differ from the reference program's by a relative error of at most 0.02.
Values may be sent and summed in bfloat16 or wider, within the bound.
A program may use at most 192 MiB of HBM per device.

```python
import math
import jax
import jax.numpy as jnp
import numpy as np
from jax import lax

TEXT_WIDTH = 768
TEXT_HEADS = 12
TEXT_FF = 3072
IMAGE_WIDTH = 1024
IMAGE_HEADS = 8
IMAGE_FF = 1024
CO_WIDTH = 1024
CO_HEADS = 8
GROUPS = 4
LENGTH = 128
PAIRS = 4
MOST = 36
ROWS_DEV = 8
ROWS = 32
TOKENS = 4096
N_DP = 4


def raised(array, key, source, target, shards_of, factor):
    def block_of(position):
        return (jnp.arange(array.shape[position]) // (array.shape[position] // shards_of)).reshape((-1,) + (1,) * (array.ndim - 1 - position))

    first = jax.random.permutation(key, shards_of)[block_of(target)]
    far = (block_of(target) + shards_of // 2) % shards_of
    return jnp.where((block_of(source) == first) | (block_of(source) == far), factor * array, array)


def levels(key, extent, shards, smallest, top_value):
    gain = 1.0
    for position, parts in shards:
        draws = jax.random.uniform(jax.random.fold_in(jax.random.fold_in(key, 6), position), (parts,), jnp.float32, smallest / len(shards), top_value / len(shards))
        gain = gain * jnp.repeat(jnp.exp(draws), extent[position] // parts).reshape((-1,) + (1,) * (len(extent) - 1 - position))
    return gain


def length_profile(count, total, most, skew):
    portions = [(1 << 20) // math.isqrt(rank ** skew) + 1 for rank in range(2, count + 1)]
    surplus, holding = total - most - (count - 1), [1] * (count - 1)
    while surplus > 0:
        candidates = [i for i in range(count - 1) if holding[i] < most]
        whole, budget = sum([portions[i] for i in candidates]), surplus
        for i in candidates:
            addition = min(most - holding[i], max(1, budget * portions[i] // whole), surplus)
            holding[i] = holding[i] + addition
            surplus = surplus - addition
    return np.array([most] + holding)


def ragged_sizes(own_key, amount, total, reach, skew):
    if amount == 2:
        one = jax.random.randint(own_key, (), max(1, total - reach), min(reach, total - 1) + 1)
        return jnp.stack([one, total - one])
    tallies = jnp.asarray(length_profile(amount, total, reach, skew), jnp.int32)
    pairs = (amount - 1) // 2
    donor, taker = tallies[1:1 + 2 * pairs:2], tallies[2:2 + 2 * pairs:2]
    margin = jnp.minimum(donor - 1, reach - taker)
    moved = jax.random.randint(jax.random.fold_in(own_key, 1), (pairs,), 0, 1 << 20) % (margin + 1)
    tallies = tallies.at[1:1 + 2 * pairs:2].set(donor - moved).at[2:2 + 2 * pairs:2].set(taker + moved)
    return tallies[jax.random.permutation(jax.random.fold_in(own_key, 2), amount)]


def bell_draw(rng, dims, scale, most, cuts=(), held_as=jnp.bfloat16):
    factor_of = levels(rng, dims, cuts, -0.22, 0.18) if cuts else 1.0
    drawn = jax.random.normal(rng, dims, jnp.float32) * scale * factor_of
    return jnp.minimum(jnp.maximum(drawn, -most), most).astype(held_as)


def noise_with(key, extent, width, reach, cuts, heavy, kind=jnp.bfloat16):
    values = width * jax.random.normal(key, extent, jnp.float32)
    if cuts:
        values = values * levels(key, extent, cuts, -0.22, 0.18)
    return jnp.clip(raised(values, jax.random.fold_in(key, 3), *heavy), -reach, reach).astype(kind)


def setup_inputs(seed: int = 0) -> dict:
    keys = jax.random.split(jax.random.key(seed), 16)
    return {
        "hidden": bell_draw(keys[0], (2, TOKENS, IMAGE_WIDTH), 1.0, 6.0, ((0, 2), (1, 4))),
        "cotangent": noise_with(keys[1], (2, TOKENS, IMAGE_WIDTH), 1.0, 6.0, ((0, 2), (1, 4)), (1, 2, 4, 2.0)),
        "segments": jax.vmap(lambda own: jnp.searchsorted(jnp.cumsum(ragged_sizes(own, PAIRS, LENGTH, MOST, 2)), jnp.arange(LENGTH), side="right"))(jax.random.split(keys[2], 2 * ROWS)).reshape((2, ROWS, LENGTH)).astype(jnp.int32),
        "cross_in": bell_draw(keys[3], (2, IMAGE_WIDTH, 3, CO_WIDTH), IMAGE_WIDTH ** -0.5, 0.1875, ((0, 2), (3, 4))),
        "cross_bias": bell_draw(keys[4], (2, 2, CO_WIDTH), 0.5, 3.0, ((0, 2), (2, 4))),
        "cross_out": bell_draw(keys[5], (2, CO_WIDTH, IMAGE_WIDTH), (CO_WIDTH // MOST) ** -0.5, 1.0, ((0, 2), (1, 4))),
        "up_weight": bell_draw(keys[6], (2, IMAGE_WIDTH, TEXT_FF), IMAGE_WIDTH ** -0.5, 0.1875, ((0, 2), (2, 4))),
        "up_bias": bell_draw(keys[7], (2, TEXT_FF), 0.5, 3.0, ((0, 2), (1, 4))),
        "down_weight": bell_draw(keys[8], (2, TEXT_FF, IMAGE_WIDTH), IMAGE_FF ** -0.5, 0.1875, ((0, 2), (1, 4))),
        "attend_in": bell_draw(keys[9], (2, IMAGE_WIDTH, 3, IMAGE_WIDTH), IMAGE_WIDTH ** -0.5, 0.1875, ((0, 2), (3, 4))),
        "attend_bias": bell_draw(keys[10], (2, 2, IMAGE_WIDTH), 0.5, 3.0, ((0, 2), (2, 4))),
        "attend_out": bell_draw(keys[11], (2, IMAGE_WIDTH, IMAGE_WIDTH), (IMAGE_WIDTH // MOST) ** -0.5, 1.0, ((0, 2), (1, 4))),
        "out_bias": bell_draw(keys[12], (2, 3, IMAGE_WIDTH), 0.5, 3.0, ((0, 2),)),
        "norm_gains": jnp.clip(1.0 + 0.1 * jax.random.normal(keys[13], (2, 3, IMAGE_WIDTH), jnp.float32), 0.5, 1.5).astype(jnp.bfloat16),
        "norm_shifts": bell_draw(keys[14], (2, 3, IMAGE_WIDTH), 0.5, 3.0, ((0, 2),)),
    }


@jax.custom_vjp
def low(v):
    return lax.optimization_barrier(v.astype(jnp.bfloat16)).astype(jnp.float32)

@jax.custom_vjp
def low_back(v):
    return v

def low_keep(v):
    return (low(v), None)

def low_pass(kept, grad):
    return (grad,)

def back_keep(v):
    return (v, None)

def back_low(kept, grad):
    return (low(grad),)
low.defvjp(low_keep, low_pass)
low_back.defvjp(back_keep, back_low)
highest = lax.Precision.HIGHEST
norm_eps = 1e-12
masked_score = -1000000000.0

def rounded(value_in):
    return low(low_back(value_in))

def matmul(left, right):
    return jnp.dot(left, right, precision=highest)

def normalize(value_in, gain_row, shift_row):
    row_mean = lax.optimization_barrier(jnp.mean(value_in, axis=-1, keepdims=True))
    centred = value_in - row_mean
    spread = lax.optimization_barrier(jnp.mean(centred * centred, axis=-1, keepdims=True))
    return centred * lax.rsqrt(spread + norm_eps) * gain_row + shift_row

def attention(queries, key_rows, value_rows, allowed, head_count):
    row_count = allowed.shape[0]
    length = allowed.shape[1]
    head_dim = queries.shape[1] // head_count
    head_shape = (row_count, length, head_count, head_dim)
    scores = jnp.einsum('rqhd,rkhd->rhqk', queries.reshape(head_shape), key_rows.reshape(head_shape), precision=highest)
    scores = low_back(scores * (1.0 / math.sqrt(head_dim)))
    scores = jnp.where(allowed[:, None], scores, masked_score)
    weights = low(jax.nn.softmax(scores, axis=-1))
    context = jnp.einsum('rhqk,rkhd->rqhd', weights, value_rows.reshape(head_shape), precision=highest)
    return rounded(context.reshape(row_count * length, head_count * head_dim))

def stream_view(params, side_index, width_real, head_total, hidden_total):
    cross_in, cross_bias, cross_out, up_weight, up_bias, down_weight, attend_in, attend_bias, attend_out = params[:9]
    padded = cross_in.shape[1]
    group_units = up_weight.shape[2] // GROUPS
    used_units = hidden_total // GROUPS
    group_lanes = padded // GROUPS
    used_lanes = width_real // GROUPS
    cross_view = cross_in[side_index, :width_real]
    up_view = up_weight[side_index, :width_real].reshape(width_real, GROUPS, group_units)[:, :, :used_units].reshape(width_real, hidden_total)
    up_shift = up_bias[side_index].reshape(GROUPS, group_units)[:, :used_units].reshape(hidden_total)
    down_view = down_weight[side_index].reshape(GROUPS, group_units, padded)[:, :used_units, :width_real].reshape(hidden_total, width_real)
    attend_view = attend_in[side_index, :width_real].reshape(width_real, 3, GROUPS, group_lanes)[:, :, :, :used_lanes].reshape(width_real, 3, width_real)
    attend_shift = attend_bias[side_index].reshape(2, GROUPS, group_lanes)[:, :, :used_lanes].reshape(2, width_real)
    attend_back = attend_out[side_index].reshape(GROUPS, group_lanes, padded)[:, :used_lanes, :width_real].reshape(width_real, width_real)
    return (cross_view, cross_bias[side_index], cross_out[side_index, :, :width_real], up_view, up_shift, down_view, attend_view, attend_shift, attend_back)

def layer(params, inputs, block_segments):
    out_bias, norm_gains, norm_shifts = (params[9], params[10], params[11])
    setups = ((TEXT_WIDTH, TEXT_HEADS, TEXT_FF), (IMAGE_WIDTH, IMAGE_HEADS, IMAGE_FF))
    views = [stream_view(params, side_index, setups[side_index][0], setups[side_index][1], setups[side_index][2]) for side_index in range(2)]
    streams_in = [inputs[side_index, :, :setups[side_index][0]] for side_index in range(2)]
    projected = []
    for side_index in range(2):
        cross_view, cross_shift = (views[side_index][0], views[side_index][1])
        queries = rounded(matmul(streams_in[side_index], cross_view[:, 0]) + cross_shift[0])
        key_rows = rounded(matmul(streams_in[side_index], cross_view[:, 1]))
        value_rows = rounded(matmul(streams_in[side_index], cross_view[:, 2]) + cross_shift[1])
        projected.append((queries, key_rows, value_rows))
    results = []
    for side_index in range(2):
        other_index = 1 - side_index
        width_real, head_total = (setups[side_index][0], setups[side_index][1])
        stream_parts = views[side_index]
        own_rows = block_segments[side_index]
        allowed = own_rows[:, :, None] == block_segments[other_index][:, None, :]
        context = attention(projected[side_index][0], projected[other_index][1], projected[other_index][2], allowed, CO_HEADS)
        branch = low_back(matmul(context, stream_parts[2]) + out_bias[side_index, 0, :width_real])
        first_norm = normalize(streams_in[side_index] + branch, norm_gains[side_index, 0, :width_real], norm_shifts[side_index, 0, :width_real])
        inner_rows = low_back(matmul(low(first_norm), stream_parts[3]) + stream_parts[4])
        activated = low(jax.nn.gelu(inner_rows, approximate=False))
        feed_rows = low_back(matmul(activated, stream_parts[5]) + out_bias[side_index, 1, :width_real])
        second_norm = normalize(first_norm + feed_rows, norm_gains[side_index, 1, :width_real], norm_shifts[side_index, 1, :width_real])
        second_low = low(second_norm)
        self_queries = rounded(matmul(second_low, stream_parts[6][:, 0]) + stream_parts[7][0])
        self_keys = rounded(matmul(second_low, stream_parts[6][:, 1]))
        self_values = rounded(matmul(second_low, stream_parts[6][:, 2]) + stream_parts[7][1])
        own_mask = own_rows[:, :, None] == own_rows[:, None, :]
        self_context = attention(self_queries, self_keys, self_values, own_mask, head_total)
        branch_two = low_back(matmul(self_context, stream_parts[8]) + out_bias[side_index, 2, :width_real])
        final_rows = normalize(second_norm + branch_two, norm_gains[side_index, 2, :width_real], norm_shifts[side_index, 2, :width_real])
        results.append(final_rows)
    padding = IMAGE_WIDTH - TEXT_WIDTH
    return jnp.stack([jnp.pad(results[0], ((0, 0), (0, padding))), results[1]])

def reference(hidden, cotangent, segments, cross_in, cross_bias, cross_out, up_weight, up_bias, down_weight, attend_in, attend_bias, attend_out, out_bias, norm_gains, norm_shifts):
    params = tuple((weight.astype(jnp.float32) for weight in (cross_in, cross_bias, cross_out, up_weight, up_bias, down_weight, attend_in, attend_bias, attend_out, out_bias, norm_gains, norm_shifts)))
    block_size = ROWS_DEV * LENGTH

    def block_step(totals, block_index):
        inputs = lax.dynamic_slice_in_dim(hidden, (block_index * block_size).astype(jnp.int32), block_size, 1).astype(jnp.float32)
        incoming = lax.dynamic_slice_in_dim(cotangent, (block_index * block_size).astype(jnp.int32), block_size, 1).astype(jnp.float32)
        block_segments = lax.dynamic_slice_in_dim(segments, (block_index * ROWS_DEV).astype(jnp.int32), ROWS_DEV, 1)
        result, pullback = jax.vjp(lambda weights, activations: layer(weights, activations, block_segments), params, inputs)
        weight_grads, input_grads = pullback(incoming)
        totals = jax.tree.map(jnp.add, totals, weight_grads)
        return (totals, (result.astype(jnp.bfloat16), input_grads.astype(jnp.bfloat16)))
    zero_grads = jax.tree.map(jnp.zeros_like, params)
    totals, outputs = lax.scan(block_step, zero_grads, jnp.arange(N_DP, dtype=jnp.int32))
    width_pad = hidden.shape[2]
    layer_out = outputs[0].transpose(1, 0, 2, 3).reshape(2, -1, width_pad)
    hidden_grad = outputs[1].transpose(1, 0, 2, 3).reshape(2, -1, width_pad)
    return (layer_out, hidden_grad, totals[0], totals[1], totals[2], totals[3], totals[4], totals[5], totals[6], totals[7], totals[8], totals[9], totals[10], totals[11])
```

```python
import math
from functools import partial

import jax
import jax.numpy as jnp
from jax import lax
from jax.experimental import pallas as pl
from jax.experimental.pallas import tpu as pltpu
from jax.sharding import PartitionSpec as P

TEXT_WIDTH = 768
TEXT_HEADS = 12
TEXT_FF = 3072
IMAGE_WIDTH = 1024
IMAGE_HEADS = 8
IMAGE_FF = 1024
CO_HEADS = 8

norm_eps = 1e-12
masked_score = -1000000000.0
low = jnp.bfloat16
wide = jnp.float32
ANY = pl.BlockSpec(memory_space=pl.ANY)
VMEM = pl.BlockSpec(memory_space=pltpu.VMEM)
MESH = pl.DeviceIdType.MESH
VMEM_LIMIT = 64000 * 1024
TILE = 256


def dot(left, right):
    return jnp.dot(left, right, preferred_element_type=wide)


def dot_nt(left, right):
    return lax.dot_general(left, right, (((1,), (1,)), ((), ())), preferred_element_type=wide)


def dot_tn(left, right):
    return lax.dot_general(left, right, (((0,), (0,)), ((), ())), preferred_element_type=wide)


class Setting:
    def __init__(self, width, count, units, groups):
        self.width = width
        self.head = width // count
        self.units = units // groups
        self.lanes = width // groups
        self.parts = width // TILE
        self.per_group = count // groups


class Layout:
    def __init__(self, s, inner):
        self.attend_out = 0
        self.attend_in = inner
        self.down = 4 * inner
        self.up = 4 * inner + s.units
        self.cross_out = 4 * inner + 2 * s.units
        self.total = 5 * inner + 2 * s.units


def lane(start, size=TILE):
    return pl.ds(pl.multiple_of(start, 128), size)


def ring_gather(groups, stride, pieces, z, copy, sems):
    send_z, recv_z, send_y, recv_y, send_c, recv_c = sems
    quarter = lax.rem(copy // stride, 4)
    to_y = (quarter ^ 2) * stride + lax.rem(copy, stride)
    to_c = (quarter ^ 1) * stride + lax.rem(copy, stride)
    count = len(pieces)

    def z_copy(p, way, hop):
        step = 1 - 2 * way
        origin = z - hop * step
        source, full, cut = pieces[p]
        src = cut(source, quarter) if hop == 0 else cut(full.at[origin], quarter)
        return pltpu.make_async_remote_copy(
            src, cut(full.at[origin], quarter), send_z.at[p, way, hop], recv_z.at[p, way, hop],
            device_id={"mp": z + step}, device_id_type=MESH)

    def z_arrival(p, way, hop):
        step = 1 - 2 * way
        origin = z - (hop + 1) * step
        source, full, cut = pieces[p]
        block = cut(full.at[origin], quarter)
        return pltpu.make_async_remote_copy(
            block, block, send_z.at[p, way, hop], recv_z.at[p, way, hop],
            device_id={"mp": z - step}, device_id_type=MESH)

    def y_copy(p, way, hop):
        origin = z - (hop + 1) * (1 - 2 * way)
        source, full, cut = pieces[p]
        block = cut(full.at[origin], quarter)
        return pltpu.make_async_remote_copy(
            block, block, send_y.at[p, way, hop], recv_y.at[p, way, hop],
            device_id={"dp": to_y}, device_id_type=MESH)

    def y_arrival(p, way, hop):
        origin = z - (hop + 1) * (1 - 2 * way)
        source, full, cut = pieces[p]
        block = cut(full.at[origin], quarter ^ 2)
        return pltpu.make_async_remote_copy(
            block, block, send_y.at[p, way, hop], recv_y.at[p, way, hop],
            device_id={"dp": to_y}, device_id_type=MESH)

    def c_copy(p, way, hop, which, mine=True):
        origin = z - (hop + 1) * (1 - 2 * way)
        source, full, cut = pieces[p]
        whose = (quarter if mine else quarter ^ 1) ^ (2 * which)
        block = cut(full.at[origin], whose)
        return pltpu.make_async_remote_copy(
            block, block, send_c.at[p, way, hop, which], recv_c.at[p, way, hop, which],
            device_id={"dp": to_c}, device_id_type=MESH)

    def sends(way, hop):
        if way == 0:
            return jnp.logical_and(z >= hop, z < groups - 1)
        return jnp.logical_and(z <= groups - 1 - hop, z > 0)

    def arrives(way, hop):
        return z >= hop + 1 if way == 0 else z <= groups - 2 - hop

    at_end = jnp.logical_or(z == 0, z == groups - 1)
    ahead = 2

    def own(p):
        for way in range(2):
            @pl.when(sends(way, 0))
            def _():
                z_copy(p, way, 0).start()

    def received(p):
        for hop in range(groups - 1):
            for way in range(2):
                @pl.when(arrives(way, hop))
                def _():
                    z_arrival(p, way, hop).wait_recv()
                    if hop + 1 < groups - 1:
                        @pl.when(sends(way, hop + 1))
                        def _():
                            z_copy(p, way, hop + 1).start()
                    y_copy(p, way, hop).start()
                    c_copy(p, way, hop, 0).start()

    def shared(p):
        for hop in range(groups - 1):
            for way in range(2):
                @pl.when(arrives(way, hop))
                def _():
                    y_arrival(p, way, hop).wait_recv()
                    c_copy(p, way, hop, 1).start()

    def settled(p):
        for hop in range(groups - 1):
            for way in range(2):
                @pl.when(arrives(way, hop))
                def _():
                    for which in range(2):
                        c_copy(p, way, hop, which, mine=False).wait_recv()

    def drained(p):
        for hop in range(groups - 1):
            for way in range(2):
                @pl.when(sends(way, hop))
                def _():
                    z_copy(p, way, hop).wait_send()

                @pl.when(arrives(way, hop))
                def _():
                    y_copy(p, way, hop).wait_send()
                    for which in range(2):
                        c_copy(p, way, hop, which).wait_send()

    for p in range(min(ahead, count)):
        own(p)
    for p in range(ahead, count):
        pl.when(at_end)(partial(own, p))
    for p in range(count):
        received(p)
        if p + ahead < count:
            pl.when(jnp.logical_not(at_end))(partial(own, p + ahead))
        if p:
            shared(p - 1)
    shared(count - 1)
    for p in range(count):
        settled(p)
    for p in range(count):
        drained(p)


def greet(groups, z, partners):
    barrier = pltpu.get_barrier_semaphore()
    for step in (-1, 1):
        @pl.when(jnp.logical_and(z + step >= 0, z + step < groups))
        def _():
            pl.semaphore_signal(barrier, inc=1, device_id={"mp": z + step}, device_id_type=MESH)
    for peer in partners:
        pl.semaphore_signal(barrier, inc=1, device_id=peer, device_id_type=MESH)
    at_end = jnp.logical_or(z == 0, z == groups - 1)

    @pl.when(at_end)
    def _():
        pl.semaphore_wait(barrier, 1 + len(partners))

    @pl.when(jnp.logical_not(at_end))
    def _():
        pl.semaphore_wait(barrier, 2 + len(partners))


def gather_kernel(settings, groups, stride, cross_in, cross_out, up, down, attend_in, attend_out,
                  f_cross_in, f_cross_out, f_up, f_down, f_attend_in, f_attend_out,
                  send_z, recv_z, send_y, recv_y, send_c, recv_c, local):
    z = lax.axis_index("mp")
    copy = lax.axis_index("dp")
    side = lax.axis_index("stream")
    quarter = lax.rem(copy // stride, 4)
    to_y = (quarter ^ 2) * stride + lax.rem(copy, stride)
    to_c = (quarter ^ 1) * stride + lax.rem(copy, stride)
    greet(groups, z, [{"dp": to_y}, {"dp": to_c}])
    inner = cross_out.shape[0]

    def run(s):
        w, u = s.width, s.units

        def projection(ref, part):
            return ref.at[:, pl.ds(part * (w // 4), w // 4), :]

        def leave(ref, part):
            return ref.at[pl.ds(part * (inner // 4), inner // 4), pl.ds(0, w)]

        def enter(ref, part):
            return ref.at[pl.ds(part * (w // 4), w // 4), pl.ds(0, u)]

        def fall(ref, part):
            return ref.at[pl.ds(part * (u // 4), u // 4), pl.ds(0, w)]

        pieces = [
            (cross_in, f_cross_in, projection),
            (cross_out, f_cross_out, leave),
            (up, f_up, enter),
            (down, f_down, fall),
            (attend_in, f_attend_in, projection),
            (attend_out, f_attend_out, leave),
        ]
        mine = []
        for p, (source, full, cut) in enumerate(pieces):
            if cut is projection:
                pair = [ref.at[:, pl.ds(0, w), :] for ref in (source, full.at[z])]
            elif cut is enter:
                pair = [ref.at[pl.ds(0, w), pl.ds(0, u)] for ref in (source, full.at[z])]
            else:
                rows = inner if cut is leave else u
                pair = [ref.at[pl.ds(0, rows), pl.ds(0, w)] for ref in (source, full.at[z])]
            mine.append(pltpu.make_async_copy(pair[0], pair[1], local.at[p]))
        for item in mine:
            item.start()
        ring_gather(groups, stride, pieces, z, copy,
                    (send_z, recv_z, send_y, recv_y, send_c, recv_c))
        for item in mine:
            item.wait()

    for which, s in enumerate(settings):
        pl.when(side == which)(partial(run, s))


def project_kernel(s, groups, x, bias, full, q, k, v, held, sems):
    w = s.width
    inner = held.shape[3]
    loads = [
        pltpu.make_async_copy(full.at[z, :, pl.ds(0, w), :], held.at[z, :, pl.ds(0, w), :],
                              sems.at[z]) for z in range(groups)]
    for load in loads:
        load.start()
    for z in range(groups):
        loads[z].wait()
        cols = slice(z * inner, (z + 1) * inner)
        own = x[:, :w]
        k[:, cols] = dot(own, held[z, 1, :w]).astype(low)
        v[:, cols] = (dot(own, held[z, 2, :w]) + bias[1:2, cols]).astype(low)
        q[:, cols] = (dot(own, held[z, 0, :w]) + bias[0:1, cols]).astype(low)


def softmax(scores, allowed):
    scores = jnp.where(allowed, scores, masked_score)
    exponent = jnp.exp(scores - jnp.max(scores, axis=-1, keepdims=True))
    return exponent / jnp.sum(exponent, axis=-1, keepdims=True)


def norm_into(summed_ref, normal_ref, inverse_ref, w):
    summed = summed_ref[...]
    mean = jnp.sum(summed, axis=-1, keepdims=True) * (1.0 / w)
    centred = summed - mean
    inverse = lax.rsqrt(jnp.sum(centred * centred, axis=-1, keepdims=True) * (1.0 / w) + norm_eps)
    normal_ref[...] = centred * inverse
    inverse_ref[...] = inverse


def norm_back(normal, inverse, gain, incoming, w):
    scaled = incoming * gain
    first = jnp.sum(scaled, axis=-1, keepdims=True) * (1.0 / w)
    second = jnp.sum(scaled * normal, axis=-1, keepdims=True) * (1.0 / w)
    return inverse * (scaled - first - normal * second)


def down_sum(value):
    return jnp.sum(value, axis=0, keepdims=True)


def cross_forward(length, rows, q, k, v, allowed, prob, context):
    scale = 1.0 / math.sqrt(128)

    @pl.loop(0, CO_HEADS)
    def _(h):
        cols = lane(h * 128, 128)
        for r in range(rows):
            at = slice(r * length, (r + 1) * length)
            p = softmax(dot_nt(q[at, cols], k[at, cols]) * scale, allowed[at, :] > 0)
            prob[h * rows + r] = p
            context[at, cols] = dot(p.astype(low), v[at, cols]).astype(low)


def score_grad(p, grad):
    return (p * (grad - jnp.sum(grad * p, axis=-1, keepdims=True))).astype(low)


def cross_backward(length, rows, q, k, v, prob, grad_context, dq, dk, dv):
    scale = 1.0 / math.sqrt(128)

    @pl.loop(0, CO_HEADS)
    def _(h):
        cols = lane(h * 128, 128)
        for r in range(rows):
            at = slice(r * length, (r + 1) * length)
            p = prob[h * rows + r]
            dc = grad_context[at, cols]
            ds = score_grad(p, dot_nt(dc, v[at, cols]))
            dv[at, cols] = dot_tn(p.astype(low), dc).astype(low)
            dq[at, cols] = (dot(ds, k[at, cols]) * scale).astype(low)
            dk[at, cols] = (dot_tn(ds, q[at, cols]) * scale).astype(low)


def head_slots(s, groups):
    if s.head == 128:
        return [(b, None) for b in range(s.per_group)]
    return [(h // 2, h % 2) for h in range(s.per_group)]


def half(value, which):
    if which is None:
        return value
    index = lax.broadcasted_iota(jnp.int32, value.shape, 1)
    keep = index < 64 if which == 0 else index >= 64
    return jnp.where(keep, value, jnp.zeros_like(value))


def self_forward(s, groups, length, rows, q, k, v, allowed, prob, context):
    scale = 1.0 / math.sqrt(s.head)
    inner = q.shape[1] // groups
    slots = head_slots(s, groups)

    @pl.loop(0, groups)
    def _(z):
        for b in range(inner // 128):
            cols = lane(z * inner + b * 128, 128)
            for r in range(rows):
                at = slice(r * length, (r + 1) * length)
                out = jnp.zeros((length, 128), wide)
                for i, (block, part) in enumerate(slots):
                    if block != b:
                        continue
                    qh = half(q[at, cols], part)
                    p = softmax(dot_nt(qh, k[at, cols]) * scale, allowed[at, :] > 0)
                    prob[(z * len(slots) + i) * rows + r] = p
                    out = out + half(dot(p.astype(low), v[at, cols]), part)
                context[at, cols] = out.astype(low)


def self_backward(s, groups, length, rows, q, k, v, prob, grad_context, dq, dk, dv):
    scale = 1.0 / math.sqrt(s.head)
    inner = q.shape[1] // groups
    slots = head_slots(s, groups)

    @pl.loop(0, groups)
    def _(z):
        for b in range(inner // 128):
            cols = lane(z * inner + b * 128, 128)
            for r in range(rows):
                at = slice(r * length, (r + 1) * length)
                sums = [jnp.zeros((length, 128), wide)] * 3
                for i, (block, part) in enumerate(slots):
                    if block != b:
                        continue
                    p = prob[(z * len(slots) + i) * rows + r]
                    dc = half(grad_context[at, cols], part)
                    ds = score_grad(p, dot_nt(dc, v[at, cols]))
                    sums = [
                        sums[0] + half(dot(ds, k[at, cols]) * scale, part),
                        sums[1] + half(dot_tn(ds, q[at, cols]) * scale, part),
                        sums[2] + dot_tn(p.astype(low), dc),
                    ]
                dq[at, cols] = sums[0].astype(low)
                dk[at, cols] = sums[1].astype(low)
                dv[at, cols] = sums[2].astype(low)


def middle_kernel(s, layout, groups, length,
                  x, grad_out, q, k, v, cross_allowed, self_allowed, up_bias, attend_bias,
                  out_bias, gains, shifts, f_cross_out, f_up, f_down, f_attend_in, f_attend_out,
                  layer_out, entry, dq, dk, dv, grads, vectors, up_sums, attend_sums,
                  w_cross_out, w_up, w_down, w_attend_in, w_attend_out, staged,
                  context, cross_prob, acc, n1, n2, n3, r1, r2, r3, h1, h2, slope, active,
                  q2, k2, v2, self_prob, context2, low_grad, grad_context, dq2, dk2, dv2, dz,
                  load_sem, store_sem):
    w, u = s.width, s.units
    inner = f_cross_out.shape[1]
    rows = x.shape[0] // length
    loads = {}
    number = 0

    def load(name, src, dst):
        nonlocal number
        item = pltpu.make_async_copy(src, dst, load_sem.at[number])
        number += 1
        item.start()
        loads.setdefault(name, []).append(item)

    for z in range(groups):
        load("co", f_cross_out.at[z, :, pl.ds(0, w)], w_cross_out.at[pl.ds(z * inner, inner)])
    for z in range(groups):
        load("up", f_up.at[z, pl.ds(0, w), pl.ds(0, u)], w_up.at[z])
    for z in range(groups):
        load("down", f_down.at[z, pl.ds(0, u), pl.ds(0, w)], w_down.at[pl.ds(z * u, u)])
    for z in range(groups):
        load("ai", f_attend_in.at[z, :, pl.ds(0, w)], w_attend_in.at[z])
    for z in range(groups):
        load("ao", f_attend_out.at[z, :, pl.ds(0, w)], w_attend_out.at[pl.ds(z * inner, inner)])

    def ready(name):
        for item in loads[name]:
            item.wait()

    cross_forward(length, rows, q, k, v, cross_allowed, cross_prob, context)
    ready("co")

    def leave(source, weight, residual, line):
        @pl.loop(0, s.parts)
        def _(j):
            cols = lane(j * TILE)
            acc[:, cols] = (dot(source[...], weight[:, cols]) + residual(cols)
                            + out_bias[line : line + 1, cols])

    def scaled(normal, line, cols):
        return normal[:, cols] * gains[line : line + 1, cols] + shifts[line : line + 1, cols]

    leave(context, w_cross_out, lambda cols: x[:, cols].astype(wide), 0)
    norm_into(acc, n1, r1, w)
    h1[...] = scaled(n1, 0, slice(0, w)).astype(low)
    ready("up")

    @pl.loop(0, groups)
    def _(z):
        for j in range(u // TILE):
            cols = lane(z * u + j * TILE)
            value = dot(h1[...], w_up[z, :, j * TILE : (j + 1) * TILE]) + up_bias[0:1, cols]
            bell = 0.5 * (1.0 + lax.erf(value * math.sqrt(0.5)))
            active[:, cols] = (value * bell).astype(low)
            slope[:, cols] = bell + value * (
                jnp.exp(-0.5 * value * value) * (1.0 / math.sqrt(2.0 * math.pi)))

    ready("down")
    leave(active, w_down, lambda cols: scaled(n1, 0, cols), 1)
    norm_into(acc, n2, r2, w)
    h2[...] = scaled(n2, 1, slice(0, w)).astype(low)
    ready("ai")

    @pl.loop(0, groups)
    def _(z):
        cols = lane(z * inner, inner)
        q2[:, cols] = (dot(h2[...], w_attend_in[z, 0]) + attend_bias[0:1, cols]).astype(low)
        k2[:, cols] = dot(h2[...], w_attend_in[z, 1]).astype(low)
        v2[:, cols] = (dot(h2[...], w_attend_in[z, 2]) + attend_bias[1:2, cols]).astype(low)

    self_forward(s, groups, length, rows, q2, k2, v2, self_allowed, self_prob, context2)
    ready("ao")
    leave(context2, w_attend_out, lambda cols: scaled(n2, 1, cols), 2)
    norm_into(acc, n3, r3, w)
    layer_out[:, :w] = scaled(n3, 2, slice(0, w)).astype(low)
    if w < layer_out.shape[1]:
        layer_out[:, w:] = jnp.zeros((layer_out.shape[0], layer_out.shape[1] - w), low)
        entry[:, w:] = jnp.zeros((entry.shape[0], entry.shape[1] - w), wide)
    vectors[...] = jnp.zeros_like(vectors)
    up_sums[...] = jnp.zeros_like(up_sums)

    stores = []

    def weight_grads(left, right, row, size):
        for z in range(groups):
            for j in range(size // TILE):
                slot = len(stores)
                start = z * size + j * TILE
                staged[slot] = dot_tn(left[:, start : start + TILE], right[...]).astype(low)
                item = pltpu.make_async_copy(
                    staged.at[slot], grads.at[z, pl.ds(row + j * TILE, TILE), pl.ds(0, w)],
                    store_sem.at[slot])
                item.start()
                stores.append(item)

    def back_norm(incoming, normal, inverse, line):
        vectors[3 + line : 4 + line, :w] = down_sum(incoming * normal[...])
        vectors[6 + line : 7 + line, :w] = down_sum(incoming)
        out = norm_back(normal[...], inverse[...], gains[line : line + 1, :w], incoming, w)
        acc[...] = out
        low_grad[...] = out.astype(low)
        vectors[line : line + 1, :w] = down_sum(low_grad[...].astype(wide))

    back_norm(grad_out[:, :w].astype(wide), n3, r3, 2)

    @pl.loop(0, groups)
    def _(z):
        at = pl.ds(pl.multiple_of(z * inner, inner), inner)
        grad_context[:, lane(z * inner, inner)] = dot_nt(
            low_grad[...], w_attend_out[at, :]).astype(low)

    weight_grads(context2, low_grad, layout.attend_out, inner)
    self_backward(s, groups, length, rows, q2, k2, v2, self_prob, grad_context, dq2, dk2, dv2)
    for which, d in enumerate((dq2, dk2, dv2)):
        weight_grads(d, h2, layout.attend_in + which * inner, inner)
    attend_sums[0:1, :] = down_sum(dq2[...].astype(wide))
    attend_sums[1:2, :] = down_sum(dv2[...].astype(wide))

    @pl.loop(0, groups)
    def _(z):
        cols = lane(z * inner, inner)
        for which, d in enumerate((dq2, dk2, dv2)):
            acc[...] += dot_nt(d[:, cols], w_attend_in[z, which])

    back_norm(acc[...], n2, r2, 1)

    @pl.loop(0, groups)
    def _(z):
        for j in range(u // TILE):
            cols = lane(z * u + j * TILE)
            at = pl.ds(pl.multiple_of(z * u + j * TILE, TILE), TILE)
            value = (dot_nt(low_grad[...], w_down[at, :]) * slope[:, cols]).astype(low)
            dz[:, cols] = value
            up_sums[0:1, cols] = down_sum(value.astype(wide))

    weight_grads(active, low_grad, layout.down, u)
    weight_grads(dz, h1, layout.up, u)

    @pl.loop(0, groups)
    def _(z):
        acc[...] += dot_nt(dz[:, lane(z * u, u)], w_up[z])

    back_norm(acc[...], n1, r1, 0)
    entry[:, :w] = acc[...]

    @pl.loop(0, groups)
    def _(z):
        at = pl.ds(pl.multiple_of(z * inner, inner), inner)
        grad_context[:, lane(z * inner, inner)] = dot_nt(
            low_grad[...], w_cross_out[at, :]).astype(low)

    cross_backward(length, rows, q, k, v, cross_prob, grad_context, dq, dk, dv)
    weight_grads(context, low_grad, layout.cross_out, inner)
    for item in stores:
        item.wait()


def finish_kernel(s, groups, x, entry, dq, dk, dv, full, hidden_grad, grads, sums,
                  held, staged, sems, store_sem):
    w = s.width
    inner = full.shape[3]
    loads = [
        pltpu.make_async_copy(full.at[z, :, pl.ds(0, w), :], held.at[z, :, pl.ds(0, w), :],
                              sems.at[z]) for z in range(groups)]
    for load in loads:
        load.start()
    stores = []
    for which, d in enumerate((dq, dk, dv)):
        for z in range(groups):
            slot = len(stores)
            left = d[:, z * inner : (z + 1) * inner]
            staged[slot] = dot_tn(left, x[:, :w]).astype(low)
            item = pltpu.make_async_copy(
                staged.at[slot], grads.at[z, pl.ds(which * inner, inner), pl.ds(0, w)],
                store_sem.at[slot])
            item.start()
            stores.append(item)
    sums[0:1, :] = down_sum(dq[...].astype(wide))
    sums[1:2, :] = down_sum(dv[...].astype(wide))
    total = entry[:, :w]
    for z in range(groups):
        loads[z].wait()
        cols = slice(z * inner, (z + 1) * inner)
        for which, d in enumerate((dq, dk, dv)):
            total = total + dot_nt(d[:, cols], held[z, which, :w])
    hidden_grad[:, :w] = total.astype(low)
    if w < hidden_grad.shape[1]:
        hidden_grad[:, w:] = jnp.zeros((hidden_grad.shape[0], hidden_grad.shape[1] - w), low)
    for item in stores:
        item.wait()


def reduce_kernel(settings, totals, groups, stride, chunk, lags,
                  grads, layer_rows, hidden_rows, reduced, layer_full, hidden_full,
                  from_core, from_y, from_z, far, own, staged,
                  send_c, recv_c, send_y, recv_y, send_z, recv_z, send_f, recv_f,
                  own_sem, store_sem, send_a, recv_a, local):
    z = lax.axis_index("mp")
    copy = lax.axis_index("dp")
    side = lax.axis_index("stream")
    quarter = lax.rem(copy // stride, 4)
    base = lax.rem(copy, stride)
    y = quarter // 2
    core = lax.rem(quarter, 2)
    to_y = {"dp": (quarter ^ 2) * stride + base}
    to_c = {"dp": (quarter ^ 1) * stride + base}
    greet(groups, z, [to_y, to_c])
    lag_b, lag_c, lag_z = lags
    last = groups - 1

    cuts = 8
    piece_rows = layer_rows.shape[0] // cuts

    def piece(ref, k):
        return ref.at[pl.ds(pl.multiple_of(k * piece_rows, piece_rows), piece_rows)]

    def spread(ref_in, ref_out, which, k, way, hop, arrival=False):
        step = 1 - 2 * way
        origin = z - (hop + 1 if arrival else hop) * step
        dst = piece(ref_out.at[origin], k)
        src = piece(ref_in, k) if hop == 0 and not arrival else dst
        return pltpu.make_async_remote_copy(
            src, dst, send_a.at[which, k, way, hop], recv_a.at[which, k, way, hop],
            device_id={"mp": z + step}, device_id_type=MESH)

    def spread_sends(way, hop):
        if way == 0:
            return jnp.logical_and(z >= hop, z < last)
        return jnp.logical_and(z <= last - hop, z > 0)

    def spread_arrives(way, hop):
        return z >= hop + 1 if way == 0 else z <= last - 1 - hop

    def spreading(ref_in, ref_out, which, k):
        for hop in range(groups):
            now = k - hop

            @pl.when(jnp.logical_and(now >= 0, now < cuts))
            def _():
                for way in range(2):
                    if hop:
                        @pl.when(spread_arrives(way, hop - 1))
                        def _():
                            spread(ref_in, ref_out, which, now, way, hop - 1, True).wait_recv()
                    if hop < last:
                        @pl.when(spread_sends(way, hop))
                        def _():
                            spread(ref_in, ref_out, which, now, way, hop).start()

    mine = [pltpu.make_async_copy(a, b.at[z], local.at[k])
            for k, (a, b) in enumerate(((layer_rows, layer_full), (hidden_rows, hidden_full)))]
    for item in mine:
        item.start()

    def run(count, width, lanes_of, far_from):
        size = width[0]
        other = width[1]

        def rows(i):
            return pl.ds(pl.multiple_of(i * chunk, chunk), chunk)

        def core_copy(i, k):
            return pltpu.make_async_remote_copy(
                grads.at[:, rows(i), pl.ds(pl.multiple_of(lanes_of(1 - core, k), 128), other)],
                from_core.at[i, k, :, :, pl.ds(0, other)],
                send_c.at[i, k], recv_c.at[i, k], device_id=to_c, device_id_type=MESH)

        def core_arrival(i, k):
            block = from_core.at[i, k, :, :, pl.ds(0, size)]
            return pltpu.make_async_remote_copy(
                block, block, send_c.at[i, k], recv_c.at[i, k],
                device_id=to_c, device_id_type=MESH)

        def own_load(i, k):
            return pltpu.make_async_copy(
                grads.at[:, rows(i), pl.ds(pl.multiple_of(lanes_of(core, k), 128), size)],
                own.at[lax.rem(i, 2), k, :, :, pl.ds(0, size)], own_sem.at[lax.rem(i, 2), k])

        def y_copy(i):
            return pltpu.make_async_remote_copy(
                from_core.at[i, 1 - y, :, :, pl.ds(0, size)],
                from_y.at[i, :, :, pl.ds(0, size)],
                send_y.at[i], recv_y.at[i], device_id=to_y, device_id_type=MESH)

        def z_copy(i, way, t):
            step = 1 - 2 * way
            first = z == (0 if way == 0 else last)
            dst = from_z.at[i, way, t, :, pl.ds(0, size)]

            def make(src):
                return pltpu.make_async_remote_copy(
                    src, dst, send_z.at[i, way, t], recv_z.at[i, way, t],
                    device_id={"mp": z + step}, device_id_type=MESH)

            return first, make(from_core.at[i, y, t, :, pl.ds(0, size)]), make(dst)

        def z_wait(i, way, t):
            z_copy(i, way, t)[2].wait_recv()

        def stage_a(i):
            for k in range(2):
                core_copy(i, k).start()
                own_load(i, k).start()

        def stage_b(i):
            for k in range(2):
                core_arrival(i, k).wait_recv()
                own_load(i, k).wait()
                from_core[i, k, :, :, :size] += own[lax.rem(i, 2), k, :, :, :size]
            y_copy(i).start()

        def z_step(i, hop):
            for way in range(2):
                step = 1 - 2 * way
                t = z + step * (groups - hop)
                inside = t <= last if way == 0 else t >= 0

                @pl.when(inside)
                def _():
                    first, fresh, passed = z_copy(i, way, t)
                    pl.when(first)(fresh.start)

                    @pl.when(jnp.logical_not(first))
                    def _():
                        passed.wait_recv()
                        from_z[i, way, t, :, :size] += from_core[i, y, t, :, :size]
                        passed.start()

        def stage_c(i):
            y_copy(i).wait_recv()
            from_core[i, y, :, :, :size] += from_y[i, :, :, :size]
            z_step(i, 1)

        def out_store(i):
            slot = lax.rem(i, 2)
            return pltpu.make_async_copy(
                staged.at[slot, :, pl.ds(0, size)], reduced.at[rows(i), pl.ds(0, size)],
                store_sem.at[slot])

        def far_copy(i):
            return pltpu.make_async_remote_copy(
                far.at[0, i], far.at[1, i], send_f.at[i], recv_f.at[i],
                device_id=to_y, device_id_type=MESH)

        def far_store(i):
            slot = lax.rem(i, 2)
            return pltpu.make_async_copy(
                staged.at[slot, :, pl.ds(size, size)],
                reduced.at[rows(i), pl.ds(size, size)], store_sem.at[2 + slot])

        def final(i):
            for way in range(2):
                @pl.when(z != (0 if way == 0 else last))
                def _():
                    z_wait(i, way, z)

            @pl.when(z == 0)
            def _():
                from_z[i, 0, z, :, :size] = jnp.zeros((chunk, size), low)

            @pl.when(z == last)
            def _():
                from_z[i, 1, z, :, :size] = jnp.zeros((chunk, size), low)

            total = (from_core[i, y, z, :, :size].astype(wide)
                     + from_z[i, 0, z, :, :size].astype(wide)
                     + from_z[i, 1, z, :, :size].astype(wide))

            def keep():
                pl.when(i >= 2)(lambda: out_store(i - 2).wait())
                staged[lax.rem(i, 2), :, :size] = total
                out_store(i).start()

            if far_from is None:
                keep()
            else:
                pl.when(y == 0)(keep)

                @pl.when(y == 1)
                def _():
                    far[0, i] = total.astype(low)
                    far_copy(i).start()

        def land(i):
            @pl.when(y == 0)
            def _():
                far_copy(i).wait_recv()
                pl.when(i >= 2)(lambda: far_store(i - 2).wait())
                staged[lax.rem(i, 2), :, size:] = far[1, i].astype(wide)
                far_store(i).start()

        def at(i, stage):
            pl.when(jnp.logical_and(i >= 0, i < count))(lambda: stage(i))

        end_lag = lag_c + lag_z * groups + (2 if far_from is not None else 0)

        @pl.loop(0, count + end_lag)
        def _(j):
            at(j, stage_a)
            at(j - lag_b, stage_b)
            at(j - lag_c, stage_c)
            for hop in range(2, groups):
                at(j - lag_c - lag_z * (hop - 1), partial(lambda h, i: z_step(i, h), hop))
            at(j - lag_c - lag_z * (groups - 1), final)
            if far_from is not None:
                at(j - end_lag + 1, land)
            spreading(layer_rows, layer_full, 0, j)
            spreading(hidden_rows, hidden_full, 1, j - cuts)

        @pl.loop(0, count)
        def _(i):
            for k in range(2):
                core_copy(i, k).wait_send()
            y_copy(i).wait_send()
            for way in range(2):
                for hop in range(1, groups):
                    t = z + (1 - 2 * way) * (groups - hop)

                    @pl.when(t <= last if way == 0 else t >= 0)
                    def _():
                        z_copy(i, way, t)[1].wait_send()
            if far_from is not None:
                pl.when(y == 1)(lambda: far_copy(i).wait_send())

        def drain(store):
            for i in (count - 2, count - 1):
                store(i).wait()

        if far_from is None:
            drain(out_store)
        else:
            @pl.when(y == 0)
            def _():
                drain(out_store)
                drain(far_store)

    text, image = settings
    pl.when(side == 1)(lambda: run(
        totals[1] // chunk, (TILE, TILE), lambda c, k: (2 * k + c) * TILE, None))

    def text_lanes(c, k):
        return jnp.where(c == 0, k * 2 * TILE, TILE + k * 128)

    is_text = side == 0
    pl.when(jnp.logical_and(is_text, core == 0))(lambda: run(
        totals[0] // chunk, (TILE, 128), text_lanes, None))
    pl.when(jnp.logical_and(is_text, core == 1))(lambda: run(
        totals[0] // chunk, (128, TILE), text_lanes, True))

    for which, (ref_in, ref_out) in enumerate(((layer_rows, layer_full), (hidden_rows, hidden_full))):
        @pl.loop(0, cuts)
        def _(k):
            for way in range(2):
                for hop in range(last):
                    @pl.when(spread_sends(way, hop))
                    def _():
                        spread(ref_in, ref_out, which, k, way, hop).wait_send()
    for item in mine:
        item.wait()


def shards(
    hidden,
    cotangent,
    segments,
    cross_in,
    cross_bias,
    cross_out,
    up_weight,
    up_bias,
    down_weight,
    attend_in,
    attend_bias,
    attend_out,
    out_bias,
    norm_gains,
    norm_shifts,
):
    groups = lax.axis_size("mp")
    copies = lax.axis_size("dp")
    stride = copies // 4
    side = lax.axis_index("stream")
    member = lax.axis_index("mp")
    copy = lax.axis_index("dp")
    is_image = side == 1
    inner = cross_in.shape[3]
    padded = hidden.shape[2]
    units = up_weight.shape[2]
    length = segments.shape[2]
    text = Setting(TEXT_WIDTH, TEXT_HEADS, TEXT_FF, groups)
    image = Setting(IMAGE_WIDTH, IMAGE_HEADS, IMAGE_FF, groups)
    settings = (text, image)
    layouts = [Layout(s, inner) for s in settings]
    totals = [layout.total + 3 * inner for layout in layouts]
    rows_max = max(totals)
    rows_dev = segments.shape[1] // groups
    tokens = hidden.shape[1] // groups

    def shape(dims, kind=low):
        return jax.ShapeDtypeStruct(dims, kind)

    def by_stream(piece, *operands):
        return lax.cond(
            is_image,
            lambda *a: piece(image, layouts[1], *a),
            lambda *a: piece(text, layouts[0], *a),
            *operands,
        )

    dma = pltpu.SemaphoreType.DMA
    weights = (
        jnp.swapaxes(cross_in[0], 0, 1),
        cross_out[0],
        up_weight[0],
        down_weight[0],
        jnp.swapaxes(attend_in[0], 0, 1),
        attend_out[0],
    )
    count = len(weights)
    full = pl.pallas_call(
        partial(gather_kernel, settings, groups, stride),
        out_shape=tuple(shape((groups,) + w.shape) for w in weights),
        in_specs=[ANY] * count,
        out_specs=(ANY,) * count,
        scratch_shapes=[dma((count, 2, groups - 1))] * 4
        + [dma((count, 2, groups - 1, 2))] * 2
        + [dma((count,))],
        compiler_params=pltpu.CompilerParams(collective_id=0, has_side_effects=True),
        name="gather",
    )(*weights)
    f_cross_in, f_cross_out, f_up, f_down, f_attend_in, f_attend_out = full

    cross_line = lax.all_gather(cross_bias[0], "mp")
    cross_line = cross_line.transpose(1, 0, 2).reshape(2, groups * inner).astype(wide)
    attend_line = lax.all_gather(attend_bias[0], "mp")
    attend_line = attend_line.transpose(1, 0, 2).reshape(2, groups * inner).astype(wide)
    up_line = lax.all_gather(up_bias[0], "mp").astype(wide)

    own = lax.dynamic_slice_in_dim(hidden[0], member * tokens, tokens, 0)
    grad_out = lax.dynamic_slice_in_dim(cotangent[0], member * tokens, tokens, 0)
    seg = lax.dynamic_slice_in_dim(segments, member * rows_dev, rows_dev, 1)
    seg_own = lax.dynamic_index_in_dim(seg, side, 0, keepdims=False)
    seg_other = lax.dynamic_index_in_dim(seg, 1 - side, 0, keepdims=False)
    cross_allowed = (seg_own[:, :, None] == seg_other[:, None, :]).astype(wide)
    self_allowed = (seg_own[:, :, None] == seg_own[:, None, :]).astype(wide)
    cross_allowed = cross_allowed.reshape(tokens, length)
    self_allowed = self_allowed.reshape(tokens, length)

    co = groups * inner
    square = shape((tokens, co))

    def project(s, layout, own, bias, f_cross_in):
        return pl.pallas_call(
            partial(project_kernel, s, groups),
            out_shape=(square,) * 3,
            in_specs=[VMEM, VMEM, ANY],
            out_specs=(VMEM,) * 3,
            scratch_shapes=[pltpu.VMEM((groups, 3, padded, inner), low), dma((groups,))],
            compiler_params=pltpu.CompilerParams(vmem_limit_bytes=VMEM_LIMIT),
            name="project",
        )(own, bias, f_cross_in)

    queries, keys, values = by_stream(project, own, cross_line, f_cross_in)

    def swap(block):
        return lax.ppermute(block, "stream", [(0, 1), (1, 0)])

    pair_keys, pair_values = swap(keys), swap(values)

    def middle(s, layout, *operands):
        w, u = s.width, s.units
        all_units = groups * u
        heads = groups * s.per_group
        tiles = groups * layout.total // TILE
        operands = operands[:7] + (operands[7][:, :u].reshape(1, all_units),) + operands[8:]

        def real(*dims):
            return pltpu.VMEM(dims, wide)

        def half_size(*dims):
            return pltpu.VMEM(dims, low)

        out = pl.pallas_call(
            partial(middle_kernel, s, layout, groups, length),
            out_shape=(
                shape((tokens, padded)), shape((tokens, padded), wide), square, square, square,
                shape((groups, rows_max, padded)), shape((16, padded), wide),
                shape((1, all_units), wide), shape((2, co), wide),
            ),
            in_specs=[VMEM] * 12 + [ANY] * 5,
            out_specs=(VMEM,) * 5 + (ANY,) + (VMEM,) * 3,
            scratch_shapes=[
                half_size(co, w), half_size(groups, w, u), half_size(all_units, w),
                half_size(groups, 3, w, inner), half_size(co, w), half_size(tiles, TILE, w),
                half_size(tokens, co), real(CO_HEADS * rows_dev, length, length),
                real(tokens, w), real(tokens, w), real(tokens, w), real(tokens, w),
                real(tokens, 1), real(tokens, 1), real(tokens, 1),
                half_size(tokens, w), half_size(tokens, w),
                real(tokens, all_units), half_size(tokens, all_units),
                half_size(tokens, co), half_size(tokens, co), half_size(tokens, co),
                real(heads * rows_dev, length, length), half_size(tokens, co),
                half_size(tokens, w), half_size(tokens, co),
                half_size(tokens, co), half_size(tokens, co), half_size(tokens, co),
                half_size(tokens, all_units),
                dma((5 * groups,)), dma((tiles,)),
            ],
            compiler_params=pltpu.CompilerParams(vmem_limit_bytes=VMEM_LIMIT),
            name="middle",
        )(*operands)
        up_sums = out[7].reshape(groups, u)
        return out[:7] + (jnp.pad(up_sums, ((0, 0), (0, units - u))), out[8])

    layer_rows, entry, dq, pair_dk, pair_dv, grads, vectors, up_sums, attend_sums = by_stream(
        middle, own, grad_out, queries, pair_keys, pair_values, cross_allowed, self_allowed,
        up_line, attend_line, out_bias[0].astype(wide), norm_gains[0].astype(wide),
        norm_shifts[0].astype(wide), f_cross_out, f_up, f_down, f_attend_in, f_attend_out)
    dk, dv = swap(pair_dk), swap(pair_dv)

    def finish(s, layout, own, entry, dq, dk, dv, f_cross_in, grads):
        def kernel(x, e, a, b, c, f, g_in, hidden_grad, g, sums, *scratch):
            finish_kernel(s, groups, x, e, a, b, c, f, hidden_grad,
                          g.at[:, pl.ds(layout.total, 3 * inner)], sums, *scratch)

        return pl.pallas_call(
            kernel,
            out_shape=(shape((tokens, padded)), shape(grads.shape), shape((2, co), wide)),
            in_specs=[VMEM] * 5 + [ANY] * 2,
            out_specs=(VMEM, ANY, VMEM),
            scratch_shapes=[
                pltpu.VMEM((groups, 3, padded, inner), low),
                pltpu.VMEM((3 * groups, inner, s.width), low),
                dma((groups,)), dma((3 * groups,)),
            ],
            input_output_aliases={6: 1},
            compiler_params=pltpu.CompilerParams(vmem_limit_bytes=VMEM_LIMIT),
            name="finish",
        )(own, entry, dq, dk, dv, f_cross_in, grads)

    hidden_rows, grads, cross_sums = by_stream(
        finish, own, entry, dq, dk, dv, f_cross_in, grads)

    chunk = 128
    most = rows_max // chunk
    cuts = 8
    line = (groups, tokens, padded)
    reduced, layer_out, hidden_grad = pl.pallas_call(
        partial(reduce_kernel, settings, totals, groups, stride, chunk, (1, 3, 1)),
        out_shape=(shape((rows_max, TILE), wide), shape(line), shape(line)),
        in_specs=[ANY] * 3,
        out_specs=(ANY,) * 3,
        scratch_shapes=[
            pltpu.VMEM((most, 2, groups, chunk, TILE), low),
            pltpu.VMEM((most, groups, chunk, TILE), low),
            pltpu.VMEM((most, 2, groups, chunk, TILE), low),
            pltpu.VMEM((2, most, chunk, 128), low),
            pltpu.VMEM((2, 2, groups, chunk, TILE), low),
            pltpu.VMEM((2, chunk, TILE), wide),
            dma((most, 2)), dma((most, 2)), dma((most,)), dma((most,)),
            dma((most, 2, groups)), dma((most, 2, groups)), dma((most,)), dma((most,)),
            dma((2, 2)), dma((4,)),
            dma((2, cuts, 2, groups - 1)), dma((2, cuts, 2, groups - 1)), dma((2,)),
        ],
        compiler_params=pltpu.CompilerParams(
            collective_id=1, has_side_effects=True, vmem_limit_bytes=VMEM_LIMIT),
        name="reduce",
    )(grads, layer_rows, hidden_rows)

    if stride > 1:
        teams = [[q * stride + b for b in range(stride)] for q in range(4)]
        reduced = lax.psum_scatter(
            reduced.astype(low), "dp", scatter_dimension=1, axis_index_groups=teams, tiled=True
        ).astype(wide)
    columns = padded // copies
    real_block = copy * columns < jnp.where(is_image, IMAGE_WIDTH, TEXT_WIDTH)
    reduced = jnp.where(real_block, reduced, 0.0)

    def spread_rows(total, parts, width):
        return total.reshape(total.shape[:-1] + (groups, copies, width // copies))

    flat = jnp.concatenate([
        jnp.moveaxis(cross_sums.reshape(2, groups, copies, inner // copies), 0, 2).reshape(
            groups, copies, -1),
        jnp.moveaxis(attend_sums.reshape(2, groups, copies, inner // copies), 0, 2).reshape(
            groups, copies, -1),
        up_sums.reshape(groups, copies, units // copies),
        jnp.broadcast_to(
            jnp.moveaxis(vectors[:9].reshape(9, copies, columns), 0, 1).reshape(
                1, copies, 9 * columns), (groups, copies, 9 * columns)),
    ], axis=2)
    small = lax.psum_scatter(
        flat.reshape(groups * copies, -1), ("mp", "dp"), scatter_dimension=0, tiled=True)[0]
    part = inner // copies
    cross_bias_grad = small[: 2 * part].reshape(2, part)
    attend_bias_grad = small[2 * part : 4 * part].reshape(2, part)
    up_bias_grad = small[4 * part : 4 * part + units // copies]
    vector_grads = small[4 * part + units // copies :].reshape(9, columns)

    def unpack(s, layout, reduced):
        u = s.units

        def turned(start):
            block = reduced[start : start + 3 * inner].reshape(3, inner, columns)
            return block.transpose(2, 0, 1)

        return (
            turned(layout.total),
            reduced[layout.cross_out : layout.cross_out + inner],
            jnp.pad(reduced[layout.up : layout.up + u].T, ((0, 0), (0, units - u))),
            jnp.pad(reduced[layout.down : layout.down + u], ((0, units - u), (0, 0))),
            turned(layout.attend_in),
            reduced[layout.attend_out : layout.attend_out + inner],
        )

    g_cross_in, g_cross_out, g_up, g_down, g_attend_in, g_attend_out = by_stream(unpack, reduced)
    return (
        layer_out.reshape(1, groups * tokens, padded),
        hidden_grad.reshape(1, groups * tokens, padded),
        g_cross_in[None],
        cross_bias_grad[None],
        g_cross_out[None],
        g_up[None],
        up_bias_grad[None],
        g_down[None],
        g_attend_in[None],
        attend_bias_grad[None],
        g_attend_out[None],
        vector_grads[None, 0:3],
        vector_grads[None, 3:6],
        vector_grads[None, 6:9],
    )


def solution(mesh):
    placed = (
        P("stream", "dp", None),
        P("stream", "dp", None),
        P(None, "dp", None),
        P("stream", None, None, "mp"),
        P("stream", None, "mp"),
        P("stream", "mp", None),
        P("stream", None, "mp"),
        P("stream", "mp"),
        P("stream", "mp", None),
        P("stream", None, None, "mp"),
        P("stream", None, "mp"),
        P("stream", "mp", None),
        P("stream", None, None),
        P("stream", None, None),
        P("stream", None, None),
    )
    return jax.shard_map(
        shards,
        mesh=mesh,
        in_specs=placed,
        out_specs=(
            P("stream", "dp", None),
            P("stream", "dp", None),
            P("stream", "dp", None, "mp"),
            P("stream", None, ("mp", "dp")),
            P("stream", "mp", "dp"),
            P("stream", "dp", "mp"),
            P("stream", ("mp", "dp")),
            P("stream", "mp", "dp"),
            P("stream", "dp", None, "mp"),
            P("stream", None, ("mp", "dp")),
            P("stream", "mp", "dp"),
            P("stream", None, "dp"),
            P("stream", None, "dp"),
            P("stream", None, "dp"),
        ),
        check_vma=False,
    )
```

```python
import math
from functools import partial
from typing import Any, NamedTuple

import jax
import jax.numpy as jnp
from jax import lax
from jax.experimental import pallas as pl
from jax.experimental.pallas import tpu as pltpu
from jax.sharding import PartitionSpec as P

TEXT_WIDTH = 768
TEXT_HEADS = 12
TEXT_FF = 3072
IMAGE_WIDTH = 1024
IMAGE_HEADS = 8
IMAGE_FF = 1024
CO_HEADS = 8

norm_eps = 1e-12
masked_score = -1000000000.0
low = jnp.bfloat16
wide = jnp.float32
ANY = pl.BlockSpec(memory_space=pl.ANY)
VMEM = pl.BlockSpec(memory_space=pltpu.VMEM)
MESH = pl.DeviceIdType.MESH
VMEM_LIMIT = 65400 * 1024
TILE = 256


def dot(left, right):
    return jnp.dot(left, right, preferred_element_type=wide)


def dot_nt(left, right):
    return lax.dot_general(left, right, (((1,), (1,)), ((), ())), preferred_element_type=wide)


def dot_tn(left, right):
    return lax.dot_general(left, right, (((0,), (0,)), ((), ())), preferred_element_type=wide)


class Setting:
    def __init__(self, width, count, units, groups):
        self.width = width
        self.head = width // count
        self.units = units // groups
        self.lanes = width // groups
        self.parts = width // TILE
        self.per_group = count // groups


class Layout:
    def __init__(self, s, inner):
        self.attend_out = 0
        self.attend_in = inner
        self.down = 4 * inner
        self.up = 4 * inner + s.units
        self.cross_out = 4 * inner + 2 * s.units
        self.total = 5 * inner + 2 * s.units


def lane(start, size=TILE):
    return pl.ds(pl.multiple_of(start, 128), size)


def norm_back(normal, inverse, gain, incoming, w):
    scaled = incoming * gain
    first = jnp.sum(scaled, axis=-1, keepdims=True) * (1.0 / w)
    second = jnp.sum(scaled * normal, axis=-1, keepdims=True) * (1.0 / w)
    return inverse * (scaled - first - normal * second)


def down_sum(value):
    return jnp.sum(value, axis=0, keepdims=True)


def softmax_t(scores, allowed, scale):
    scores = jnp.where(allowed, scores, masked_score / scale)
    top = jnp.max(scores, axis=0, keepdims=True)
    exponent = jnp.exp2((scores - top) * (scale * math.log2(math.e)))
    return exponent * (1.0 / jnp.sum(exponent, axis=0, keepdims=True))


def score_grad_t(p, grad):
    return (p * (grad - jnp.sum(grad * p, axis=0, keepdims=True))).astype(low)


def halves(value):
    index = lax.broadcasted_iota(jnp.int32, value.shape, 1)
    zero = jnp.zeros_like(value)
    return jnp.concatenate(
        [jnp.where(index < 64, value, zero), jnp.where(index >= 64, value, zero)], axis=0)


def lower(value):
    index = lax.broadcasted_iota(jnp.int32, value.shape, 1)
    return jnp.where(index < 64, value, jnp.zeros_like(value))


def side_by_side(parts, axis=1):
    return parts[0] if len(parts) == 1 else jnp.concatenate(parts, axis=axis)


def split(value, count):
    size = value.shape[1] // count
    return [value[:, n * size : (n + 1) * size] for n in range(count)]


def block_kinds(head, heads):
    if head == 128:
        return [0] * heads
    return [2] * (heads // 2) + [1] * (heads % 2)


def spread_heads(kind, value):
    return halves(value) if kind == 2 else lower(value) if kind == 1 else value


def attend_forward(group, kinds, scale, length, rows, q, k, v, allowed, prob, context):
    heads = sum(max(kind, 1) for kind in kinds)
    base = group * len(kinds) * 128
    ats = [slice(r * length, (r + 1) * length) for r in range(rows)]
    step = 0
    for b, kind in enumerate(kinds):
        cols = lane(base + b * 128, 128)
        count = max(kind, 1)
        groups = [ats]
        for members in groups:
            scores = side_by_side(
                [dot_nt(k[at, cols], spread_heads(kind, q[at, cols])) for at in members])
            masks = side_by_side([allowed[at, :] for at in members for _ in range(count)])
            p = softmax_t(scores, masks > 0, scale)
            low_p = p.astype(low)
            tiles = split(p, count * len(members))
            low_tiles = split(low_p, count * len(members))
            out = [
                dot_tn(side_by_side(low_tiles[n * count : (n + 1) * count], 0),
                       spread_heads(kind, v[at, cols]))
                for n, at in enumerate(members)]
            for n, at in enumerate(members):
                r = ats.index(at)
                context[at, cols] = out[n].astype(low)
                for c in range(count):
                    prob[group * heads * rows + r * heads + step + c] = tiles[n * count + c]
        step += count


def attend_backward(group, kinds, scale, length, rows, q, k, v, prob, grad, dq, dk, dv):
    heads = sum(max(kind, 1) for kind in kinds)
    base = group * len(kinds) * 128
    ats = [slice(r * length, (r + 1) * length) for r in range(rows)]
    step = 0
    for b, kind in enumerate(kinds):
        cols = lane(base + b * 128, 128)
        count = max(kind, 1)
        groups = [ats]
        for members in groups:
            dcs = [spread_heads(kind, grad[at, cols]) for at in members]
            qs = [spread_heads(kind, q[at, cols]) for at in members]
            gp = side_by_side([dot_nt(v[at, cols], dc) for at, dc in zip(members, dcs)])
            p = side_by_side([
                prob[group * heads * rows + ats.index(at) * heads + step + c]
                for at in members for c in range(count)])
            low_p = split(p.astype(low), len(members))
            ds = split(score_grad_t(p, gp), len(members))
            grad_v = [dot(a, dc) for a, dc in zip(low_p, dcs)]
            grad_k = [dot(a, two) * scale for a, two in zip(ds, qs)]
            grad_q = [dot_tn(a, k[at, cols]) * scale for a, at in zip(ds, members)]
            for n, at in enumerate(members):
                value = grad_q[n]
                if kind:
                    index = lax.broadcasted_iota(jnp.int32, (length, 128), 1)
                    other = value[length:] if kind == 2 else jnp.zeros((length, 128), wide)
                    value = jnp.where(index < 64, value[:length], other)
                dq[at, cols] = value.astype(low)
                dk[at, cols] = grad_k[n].astype(low)
                dv[at, cols] = grad_v[n].astype(low)
        step += count
class Refs:
    def __init__(self, *groups):
        for group in groups:
            self.__dict__.update(group._asdict())


class Inputs(NamedTuple):
    cross_in: Any
    cross_out: Any
    up: Any
    down: Any
    attend_in: Any
    attend_out: Any
    hidden: Any
    cotangent: Any
    cross_bias: Any
    attend_bias: Any
    up_bias: Any
    out_bias: Any
    gains: Any
    shifts: Any
    cross_allowed: Any
    self_allowed: Any


class Results(NamedTuple):
    layer_full: Any
    hidden_full: Any
    reduced: Any
    small_out: Any
    f_cross_in: Any
    f_cross_out: Any
    f_up: Any
    f_down: Any
    f_attend_in: Any
    f_attend_out: Any
    grads: Any


class Scratch(NamedTuple):
    w_in: Any
    w_cross_out: Any
    w_attend_out: Any
    w_up: Any
    w_down: Any
    x: Any
    grad_out: Any
    q: Any
    k: Any
    v: Any
    pair_k: Any
    pair_v: Any
    back_k: Any
    back_v: Any
    cross_prob: Any
    self_prob: Any
    context: Any
    context2: Any
    acc: Any
    n1: Any
    n2: Any
    n3: Any
    r1: Any
    r2: Any
    r3: Any
    h1: Any
    h2: Any
    slope: Any
    active: Any
    dz: Any
    q2: Any
    k2: Any
    v2: Any
    d1: Any
    d2: Any
    d3: Any
    low_grad: Any
    grad_context: Any
    layer_rows: Any
    hidden_rows: Any
    zero: Any
    staged: Any
    from_core: Any
    from_y: Any
    from_z: Any
    far: Any
    own: Any
    staged_out: Any
    small_in: Any
    small_got: Any
    small_sum: Any
    small_sem: Any
    a_cross_bias: Any
    a_attend_bias: Any
    a_up_bias: Any
    send_gz: Any
    recv_gz: Any
    send_gy: Any
    recv_gy: Any
    send_gc: Any
    recv_gc: Any
    weight_sem: Any
    enter_sem: Any
    send_b: Any
    recv_b: Any
    send_x: Any
    recv_x: Any
    store_sem: Any
    send_c: Any
    recv_c: Any
    send_y: Any
    recv_y: Any
    send_z: Any
    recv_z: Any
    send_f: Any
    recv_f: Any
    own_sem: Any
    out_sem: Any
    send_a: Any
    recv_a: Any
    local_sem: Any
    send_s: Any
    recv_s: Any
    free: Any


class Plan(NamedTuple):
    groups: Any
    copies: Any
    inner: Any
    length: Any
    rows: Any
    tokens: Any
    units: Any
    chunk: Any
    slots: Any
    cuts: Any
    ring: Any
    lags: Any
    when: Any


def layer_kernel(settings, layouts, plan, *refs):
    first, second = len(Inputs._fields), len(Inputs._fields) + len(Results._fields)
    r = Refs(Inputs(*refs[:first]), Results(*refs[first:second]), Scratch(*refs[second:]))
    side = lax.axis_index("stream")
    greet(plan, r)
    for which, s in enumerate(settings):
        pl.when(side == which)(partial(run_stream, which, s, layouts[which], plan, r))


def peer_of(plan, offset):
    groups, copies = plan.groups, plan.copies
    me = lax.axis_index("mp") * copies + lax.axis_index("dp")
    index = lax.rem(me + offset, groups * copies)
    return me, index, {"mp": index // copies, "dp": lax.rem(index, copies)}


def greet(plan, r):
    barrier = pltpu.get_barrier_semaphore()
    count = plan.groups * plan.copies

    @pl.loop(1, count)
    def _(offset):
        pl.semaphore_signal(barrier, inc=1, device_id=peer_of(plan, offset)[2], device_id_type=MESH)

    pl.semaphore_signal(barrier, inc=1, device_id={"stream": 1 - lax.axis_index("stream")},
                        device_id_type=MESH)
    pl.semaphore_wait(barrier, count)


class Gather:
    def __init__(self, s, plan, r):
        self.groups, self.r = plan.groups, r
        stride, copy = plan.copies // 4, lax.axis_index("dp")
        self.z = lax.axis_index("mp")
        self.quarter = lax.rem(copy // stride, 4)
        base = lax.rem(copy, stride)
        self.to_y = {"dp": (self.quarter ^ 2) * stride + base}
        self.to_c = {"dp": (self.quarter ^ 1) * stride + base}
        self.at_end = jnp.logical_or(self.z == 0, self.z == self.groups - 1)
        w, u, inner = s.width, s.units, plan.inner

        def projection(ref, part):
            return ref.at[:, pl.ds(part * (w // 4), w // 4), :]

        def leave(ref, part):
            return ref.at[pl.ds(part * (inner // 4), inner // 4), pl.ds(0, w)]

        def enter(ref, part):
            return ref.at[pl.ds(part * (w // 4), w // 4), pl.ds(0, u)]

        def fall(ref, part):
            return ref.at[pl.ds(part * (u // 4), u // 4), pl.ds(0, w)]

        self.pieces = [
            (r.cross_in, r.f_cross_in, projection),
            (r.cross_out, r.f_cross_out, leave),
            (r.up, r.f_up, enter),
            (r.down, r.f_down, fall),
            (r.attend_in, r.f_attend_in, projection),
            (r.attend_out, r.f_attend_out, leave),
        ]

    def z_copy(self, p, way, hop):
        step = 1 - 2 * way
        origin = self.z - hop * step
        source, full, cut = self.pieces[p]
        dst = cut(full.at[origin], self.quarter)
        src = cut(source, self.quarter) if hop == 0 else dst
        return pltpu.make_async_remote_copy(
            src, dst, self.r.send_gz.at[p, way, hop], self.r.recv_gz.at[p, way, hop],
            device_id={"mp": self.z + step}, device_id_type=MESH)

    def block(self, p, way, hop, whose):
        source, full, cut = self.pieces[p]
        return cut(full.at[self.z - (hop + 1) * (1 - 2 * way)], whose)

    def z_arrival(self, p, way, hop):
        block = self.block(p, way, hop, self.quarter)
        return pltpu.make_async_remote_copy(
            block, block, self.r.send_gz.at[p, way, hop], self.r.recv_gz.at[p, way, hop],
            device_id={"mp": self.z - (1 - 2 * way)}, device_id_type=MESH)

    def y_copy(self, p, way, hop, mine=True):
        block = self.block(p, way, hop, self.quarter if mine else self.quarter ^ 2)
        return pltpu.make_async_remote_copy(
            block, block, self.r.send_gy.at[p, way, hop], self.r.recv_gy.at[p, way, hop],
            device_id=self.to_y, device_id_type=MESH)

    def c_copy(self, p, way, hop, which, mine=True):
        whose = (self.quarter if mine else self.quarter ^ 1) ^ (2 * which)
        block = self.block(p, way, hop, whose)
        return pltpu.make_async_remote_copy(
            block, block, self.r.send_gc.at[p, way, hop, which],
            self.r.recv_gc.at[p, way, hop, which], device_id=self.to_c, device_id_type=MESH)

    def sends(self, way, hop):
        last = self.groups - 1
        if way == 0:
            return jnp.logical_and(self.z >= hop, self.z < last)
        return jnp.logical_and(self.z <= last - hop, self.z > 0)

    def arrives(self, way, hop):
        return self.z >= hop + 1 if way == 0 else self.z <= self.groups - 2 - hop

    def each(self, test, action, hops=None):
        for hop in range(self.groups - 1) if hops is None else hops:
            for way in range(2):
                pl.when(test(way, hop))(partial(action, way, hop))

    def own(self, p):
        for way in range(2):
            pl.when(self.sends(way, 0))(lambda: self.z_copy(p, way, 0).start())

    def begin(self, ahead):
        for p in range(ahead):
            self.own(p)
        for p in range(ahead, len(self.pieces)):
            pl.when(self.at_end)(partial(self.own, p))

    def later(self, p):
        if p < len(self.pieces):
            pl.when(jnp.logical_not(self.at_end))(partial(self.own, p))

    def received(self, p, *hops):
        def action(way, hop):
            self.z_arrival(p, way, hop).wait_recv()
            if hop + 1 < self.groups - 1:
                pl.when(self.sends(way, hop + 1))(lambda: self.z_copy(p, way, hop + 1).start())
            self.y_copy(p, way, hop).start()
            self.c_copy(p, way, hop, 0).start()

        self.each(self.arrives, action, hops or None)

    def shared(self, p, *hops):
        def action(way, hop):
            self.y_copy(p, way, hop, mine=False).wait_recv()
            self.c_copy(p, way, hop, 1).start()

        self.each(self.arrives, action, hops or None)

    def settled(self, p, weights, name, *hops):
        def action(way, hop):
            for which in range(2):
                self.c_copy(p, way, hop, which, mine=False).wait_recv()
            for item in weights.copies(name, self.z - (hop + 1) * (1 - 2 * way), False):
                item.start()

        self.each(self.arrives, action, hops or None)

    def drained(self, p):
        self.each(self.sends, lambda way, hop: self.z_copy(p, way, hop).wait_send())

        def action(way, hop):
            self.y_copy(p, way, hop).wait_send()
            for which in range(2):
                self.c_copy(p, way, hop, which).wait_send()

        self.each(self.arrives, action)


class Weights:
    def __init__(self, s, plan, r):
        self.s, self.r, self.plan = s, r, plan
        self.z = lax.axis_index("mp")
        w, u, inner, groups = s.width, s.units, plan.inner, plan.groups
        self.kinds = {
            "cross_in": (0, r.cross_in, r.f_cross_in, r.w_in, 3),
            "cross_out": (1, r.cross_out, r.f_cross_out, r.w_cross_out, s.parts),
            "up": (2, r.up, r.f_up, r.w_up, u // TILE),
            "down": (3, r.down, r.f_down, r.w_down, s.parts),
            "attend_in": (4, r.attend_in, r.f_attend_in, r.w_in, 3),
            "attend_out": (5, r.attend_out, r.f_attend_out, r.w_attend_out, s.parts),
        }

    def copies(self, name, z, own):
        number, arg, full, held, blocks = self.kinds[name]
        source = arg if own else full.at[z]
        s, groups, inner = self.s, self.plan.groups, self.plan.inner
        for b in range(blocks):
            if name in ("cross_in", "attend_in"):
                src = source.at[b, pl.ds(0, s.width), :]
                row, size = (z * 3 + b) * s.width, s.width
            elif name == "up":
                src = source.at[pl.ds(0, s.width), pl.ds(b * TILE, TILE)]
                row, size = (z * blocks + b) * s.width, s.width
            else:
                size = s.units if name == "down" else inner
                src = source.at[pl.ds(0, size), pl.ds(b * TILE, TILE)]
                row = (b * groups + z) * size
            yield pltpu.make_async_copy(
                src, held.at[pl.ds(pl.multiple_of(row, TILE), size)], self.r.weight_sem.at[number, z, b])

    def load(self, name, which="all"):
        for z in range(self.plan.groups):
            if which in ("all", "own"):
                @pl.when(self.z == z)
                def _():
                    for item in self.copies(name, z, True):
                        item.start()

            if which in ("all", "rest"):
                @pl.when(self.z != z)
                def _():
                    for item in self.copies(name, z, False):
                        item.start()

    def wait(self, name):
        for z in range(self.plan.groups):
            for item in self.copies(name, z, False):
                item.wait()


class Outputs:
    def __init__(self, s, plan, r):
        self.s, self.r, self.groups, self.cuts = s, r, plan.groups, plan.cuts
        self.z = lax.axis_index("mp")
        self.last = self.groups - 1
        self.rows = plan.tokens // self.cuts
        self.pairs = ((r.layer_rows, r.layer_full), (r.hidden_rows, r.hidden_full))

    def cut(self, ref, k):
        return ref.at[pl.ds(pl.multiple_of(k * self.rows, self.rows), self.rows),
                      pl.ds(0, self.s.width)]

    def copy(self, which, k, way, hop, arrival=False):
        step = 1 - 2 * way
        origin = self.z - (hop + 1 if arrival else hop) * step
        rows, full = self.pairs[which]
        dst = self.cut(full.at[origin], k)
        src = self.cut(rows, k) if hop == 0 and not arrival else dst
        return pltpu.make_async_remote_copy(
            src, dst, self.r.send_a.at[which, k, way, hop], self.r.recv_a.at[which, k, way, hop],
            device_id={"mp": self.z + step}, device_id_type=MESH)

    def sends(self, way, hop):
        if way == 0:
            return jnp.logical_and(self.z >= hop, self.z < self.last)
        return jnp.logical_and(self.z <= self.last - hop, self.z > 0)

    def arrives(self, way, hop):
        return self.z >= hop + 1 if way == 0 else self.z <= self.last - 1 - hop

    def step(self, which, k):
        for hop in range(self.groups):
            now = k - hop

            @pl.when(jnp.logical_and(now >= 0, now < self.cuts))
            def _():
                for way in range(2):
                    if hop:
                        pl.when(self.arrives(way, hop - 1))(
                            lambda: self.copy(which, now, way, hop - 1, True).wait_recv())
                    if hop < self.last:
                        pl.when(self.sends(way, hop))(
                            lambda: self.copy(which, now, way, hop).start())

    def local(self, which):
        rows, full = self.pairs[which]
        width = self.s.width
        items = [pltpu.make_async_copy(rows.at[:, pl.ds(0, width)],
                                       full.at[self.z, :, pl.ds(0, width)],
                                       self.r.local_sem.at[which, self.groups])]
        padded = full.shape[2]
        if width < padded:
            items += [pltpu.make_async_copy(
                self.r.zero, full.at[z, :, pl.ds(width, padded - width)],
                self.r.local_sem.at[which, z]) for z in range(self.groups)]
        return items

    def drained(self):
        for which in range(2):
            @pl.loop(0, self.cuts)
            def _(k):
                for way in range(2):
                    for hop in range(self.last):
                        pl.when(self.sends(way, hop))(
                            lambda: self.copy(which, k, way, hop).wait_send())
            for item in self.local(which):
                item.wait()


class Reduce:
    def __init__(self, which, s, layout, plan, r):
        self.text = which == 0
        self.r, self.groups, self.chunk = r, plan.groups, plan.chunk
        self.slots, self.lags = plan.slots, plan.lags
        self.count = (layout.total + 3 * plan.inner) // self.chunk
        stride, copy = plan.copies // 4, lax.axis_index("dp")
        quarter = lax.rem(copy // stride, 4)
        base = lax.rem(copy, stride)
        self.z = lax.axis_index("mp")
        self.y, self.core = quarter // 2, lax.rem(quarter, 2)
        self.to_y = {"dp": (quarter ^ 2) * stride + base}
        self.to_c = {"dp": (quarter ^ 1) * stride + base}
        self.last = self.groups - 1

    def widths(self, action):
        if not self.text:
            action(TILE, TILE, False)
        else:
            pl.when(self.core == 0)(partial(action, TILE, 128, False))
            pl.when(self.core == 1)(partial(action, 128, TILE, True))

    def first_lane(self, core, y):
        if self.text:
            return pl.multiple_of(jnp.where(core == 0, y * 2 * TILE, TILE + y * 128), 128)
        return pl.multiple_of((2 * y + core) * TILE, 128)

    def rows(self, i):
        return pl.ds(pl.multiple_of(i * self.chunk, self.chunk), self.chunk)

    def slot(self, i):
        return lax.rem(i, self.slots)

    def core_copy(self, i, k, other):
        n = self.slot(i)
        return pltpu.make_async_remote_copy(
            self.r.grads.at[:, self.rows(i), pl.ds(self.first_lane(1 - self.core, k), other)],
            self.r.from_core.at[n, k, :, :, pl.ds(0, other)],
            self.r.send_c.at[n, k], self.r.recv_c.at[n, k],
            device_id=self.to_c, device_id_type=MESH)

    def core_arrival(self, i, k, size):
        n = self.slot(i)
        block = self.r.from_core.at[n, k, :, :, pl.ds(0, size)]
        return pltpu.make_async_remote_copy(
            block, block, self.r.send_c.at[n, k], self.r.recv_c.at[n, k],
            device_id=self.to_c, device_id_type=MESH)

    def own_load(self, i, k, size):
        n = lax.rem(i, 4)
        return pltpu.make_async_copy(
            self.r.grads.at[:, self.rows(i), pl.ds(self.first_lane(self.core, k), size)],
            self.r.own.at[n, k, :, :, pl.ds(0, size)], self.r.own_sem.at[n, k])

    def y_copy(self, i, size):
        n = self.slot(i)
        return pltpu.make_async_remote_copy(
            self.r.from_core.at[n, 1 - self.y, :, :, pl.ds(0, size)],
            self.r.from_y.at[n, :, :, pl.ds(0, size)],
            self.r.send_y.at[n], self.r.recv_y.at[n], device_id=self.to_y, device_id_type=MESH)

    def z_copy(self, i, way, t, size, fresh):
        n = self.slot(i)
        dst = self.r.from_z.at[n, way, t, :, pl.ds(0, size)]
        src = self.r.from_core.at[n, self.y, t, :, pl.ds(0, size)] if fresh else dst
        return pltpu.make_async_remote_copy(
            src, dst, self.r.send_z.at[n, way, t], self.r.recv_z.at[n, way, t],
            device_id={"mp": self.z + 1 - 2 * way}, device_id_type=MESH)

    def far_copy(self, i):
        n = self.slot(i)
        return pltpu.make_async_remote_copy(
            self.r.far.at[0, n], self.r.far.at[1, n], self.r.send_f.at[n], self.r.recv_f.at[n],
            device_id=self.to_y, device_id_type=MESH)

    def out_store(self, i, start, size):
        n = lax.rem(i, 2)
        return pltpu.make_async_copy(
            self.r.staged_out.at[n, :, pl.ds(start, size)],
            self.r.reduced.at[self.rows(i), pl.ds(start, size)],
            self.r.out_sem.at[1 if start else 0, n])

    def credit(self, i, sem):
        pl.when(i >= self.slots)(lambda: pl.semaphore_wait(sem, 1))

    def stage_a(self, i):
        self.credit(i, self.r.free.at[0])

        def action(size, other, far):
            for k in range(2):
                self.core_copy(i, k, other).start()
                self.own_load(i, k, size).start()

        self.widths(action)

    def stage_b(self, i):
        n = self.slot(i)

        def action(size, other, far):
            for k in range(2):
                self.core_arrival(i, k, size).wait_recv()
                self.own_load(i, k, size).wait()
                self.r.from_core[n, k, :, :, :size] += self.r.own[lax.rem(i, 4), k, :, :, :size]
            self.credit(i, self.r.free.at[1])
            self.y_copy(i, size).start()

        self.widths(action)

    def z_step(self, hop, i):
        n = self.slot(i)

        def action(size, other, far):
            for way in range(2):
                t = self.z + (1 - 2 * way) * (self.groups - hop)

                @pl.when(t <= self.last if way == 0 else t >= 0)
                def _():
                    first = self.z == (0 if way == 0 else self.last)
                    pl.when(first)(lambda: self.z_copy(i, way, t, size, True).start())

                    @pl.when(jnp.logical_not(first))
                    def _():
                        self.z_copy(i, way, t, size, False).wait_recv()
                        self.r.from_z[n, way, t, :, :size] += (
                            self.r.from_core[n, self.y, t, :, :size])
                        self.z_copy(i, way, t, size, False).start()

        self.widths(action)

    def stage_c(self, i):
        n = self.slot(i)

        def action(size, other, far):
            self.y_copy(i, size).wait_recv()
            self.r.from_core[n, self.y, :, :, :size] += self.r.from_y[n, :, :, :size]

        self.widths(action)
        pl.when(self.z < self.last)(lambda: self.credit(i, self.r.free.at[2]))
        pl.when(self.z > 0)(lambda: self.credit(i, self.r.free.at[3]))
        self.z_step(1, i)

    def final(self, i):
        n = self.slot(i)

        def action(size, other, far):
            for way in range(2):
                edge = 0 if way == 0 else self.last

                @pl.when(self.z != edge)
                def _():
                    self.z_copy(i, way, self.z, size, False).wait_recv()

                @pl.when(self.z == edge)
                def _():
                    self.r.from_z[n, way, self.z, :, :size] = jnp.zeros((self.chunk, size), low)

            total = (self.r.from_core[n, self.y, self.z, :, :size].astype(wide)
                     + self.r.from_z[n, 0, self.z, :, :size].astype(wide)
                     + self.r.from_z[n, 1, self.z, :, :size].astype(wide))

            def keep():
                pl.when(i >= 2)(lambda: self.out_store(i - 2, 0, size).wait())
                self.r.staged_out[lax.rem(i, 2), :, :size] = total
                self.out_store(i, 0, size).start()

            if far:
                pl.when(self.y == 0)(keep)

                @pl.when(self.y == 1)
                def _():
                    pl.when(i >= self.slots)(lambda: self.far_copy(i - self.slots).wait_send())
                    self.credit(i, self.r.free.at[4])
                    self.r.far[0, n] = total.astype(low)
                    self.far_copy(i).start()
            else:
                keep()
            for k in range(2):
                self.core_copy(i, k, other).wait_send()
            self.y_copy(i, size).wait_send()
            for way in range(2):
                for hop in range(1, self.groups):
                    t = self.z + (1 - 2 * way) * (self.groups - hop)
                    pl.when(t <= self.last if way == 0 else t >= 0)(
                        lambda: self.z_copy(i, way, t, size, True).wait_send())

        self.widths(action)

        @pl.when(i < self.count - self.slots)
        def _():
            def tell(index, target):
                pl.semaphore_signal(self.r.free.at[index], inc=1, device_id=target,
                                    device_id_type=MESH)

            tell(0, self.to_c)
            tell(1, self.to_y)
            pl.when(self.z > 0)(lambda: tell(2, {"mp": self.z - 1}))
            pl.when(self.z < self.last)(lambda: tell(3, {"mp": self.z + 1}))

    def land(self, i):
        n = self.slot(i)

        def action(size, other, far):
            if not far:
                return

            @pl.when(self.y == 0)
            def _():
                self.far_copy(i).wait_recv()
                pl.when(i >= 2)(lambda: self.out_store(i - 2, size, size).wait())
                self.r.staged_out[lax.rem(i, 2), :, size : 2 * size] = self.r.far[1, n].astype(wide)
                self.out_store(i, size, size).start()

                @pl.when(i < self.count - self.slots)
                def _():
                    pl.semaphore_signal(self.r.free.at[4], inc=1, device_id=self.to_y,
                                        device_id_type=MESH)

        self.widths(action)

    def iteration(self, j):
        lag_b, lag_c, lag_z, lag_f = self.lags

        def at(i, stage):
            pl.when(jnp.logical_and(i >= 0, i < self.count))(lambda: stage(i))

        at(j, self.stage_a)
        at(j - lag_b, self.stage_b)
        at(j - lag_c, self.stage_c)
        for hop in range(2, self.groups):
            at(j - lag_c - lag_z * (hop - 1), partial(self.z_step, hop))
        done = lag_c + lag_z * (self.groups - 1)
        at(j - done, self.final)
        if self.text:
            at(j - done - lag_f, self.land)

    def iterations(self):
        lag_b, lag_c, lag_z, lag_f = self.lags
        return self.count + lag_c + lag_z * (self.groups - 1) + (lag_f if self.text else 0)

    def drained(self):
        def action(size, other, far):
            pair = (self.count - 2, self.count - 1)
            if not far:
                for i in pair:
                    self.out_store(jnp.int32(i), 0, size).wait()
                return

            @pl.when(self.y == 0)
            def _():
                for i in pair:
                    self.out_store(jnp.int32(i), 0, size).wait()
                    self.out_store(jnp.int32(i), size, size).wait()

            @pl.when(self.y == 1)
            def _():
                @pl.loop(self.count - self.slots, self.count)
                def _(i):
                    self.far_copy(i).wait_send()

        self.widths(action)


class Small:
    def __init__(self, plan, r):
        self.plan, self.r = plan, r
        self.count = plan.groups * plan.copies
        self.per_row = max(1, self.count // 16)
        self.width = r.small_in.shape[1] // self.per_row

    def piece(self, ref, index):
        row, part = index // self.per_row, lax.rem(index, self.per_row)
        return ref.at[pl.ds(row, 1), pl.ds(pl.multiple_of(part * self.width, 128), self.width)]

    def copy(self, offset, first):
        me, peer, target = peer_of(self.plan, offset)
        if first:
            src, dst = self.piece(self.r.small_in, peer), self.r.small_got.at[me]
        else:
            src, dst = self.r.small_sum, self.piece(self.r.small_out, me)
        n = 0 if first else 1
        return pltpu.make_async_remote_copy(
            src, dst, self.r.send_s.at[n, offset], self.r.recv_s.at[n, offset],
            device_id=target, device_id_type=MESH)

    def every(self, action):
        @pl.loop(1, self.count)
        def _(offset):
            action(offset)

    def start(self):
        self.every(lambda offset: self.copy(offset, True).start())

    def local(self, first):
        me = peer_of(self.plan, 0)[0]
        pair = ((self.piece(self.r.small_in, me), self.r.small_got.at[me]) if first
                else (self.r.small_sum, self.piece(self.r.small_out, me)))
        return pltpu.make_async_copy(*pair, self.r.small_sem.at[0 if first else 1])

    def middle(self):
        self.local(True).start()
        self.every(lambda offset: self.copy(offset, True).wait_recv())
        self.local(True).wait()
        self.r.small_sum[...] = jnp.sum(self.r.small_got[...], axis=0)
        self.local(False).start()
        self.every(lambda offset: self.copy(offset, False).start())

    def finish(self):
        self.local(False).wait()
        self.every(lambda offset: self.copy(offset, False).wait_recv())
        for first in (True, False):
            self.every(lambda offset: self.copy(offset, first).wait_send())


def run_stream(which, s, layout, plan, r):
    groups, inner, length = plan.groups, plan.inner, plan.length
    rows_dev = plan.rows
    tokens = plan.tokens
    w, u = s.width, s.units
    z = lax.axis_index("mp")
    side = lax.axis_index("stream")
    gather = Gather(s, plan, r)
    weights = Weights(s, plan, r)
    outputs = Outputs(s, plan, r)
    reduce = Reduce(which, s, layout, plan, r)
    small = Small(plan, r)

    gather.begin(2)
    own_rows = pl.ds(pl.multiple_of(z * tokens, tokens), tokens)
    enter = [pltpu.make_async_copy(r.hidden.at[own_rows], r.x, r.enter_sem.at[0]),
             pltpu.make_async_copy(r.cotangent.at[own_rows], r.grad_out, r.enter_sem.at[1])]
    for item in enter:
        item.start()
    weights.load("cross_in", "own")
    for name in ("cross_out", "up", "down", "attend_out"):
        weights.load(name, "own")

    def bias_copy(step, kind):
        ref, full = ((r.cross_bias, r.a_cross_bias), (r.attend_bias, r.a_attend_bias),
                     (r.up_bias, r.a_up_bias))[kind]
        return pltpu.make_async_remote_copy(
            ref, full.at[z], r.send_b.at[kind, step], r.recv_b.at[kind, step],
            device_id={"mp": lax.rem(z + step, groups)}, device_id_type=MESH)

    for kind, (ref, full) in enumerate(((r.cross_bias, r.a_cross_bias),
                                        (r.attend_bias, r.a_attend_bias),
                                        (r.up_bias, r.a_up_bias))):
        for step in range(1, groups):
            bias_copy(step, kind).start()
        full[z] = ref[...]

    r.zero[...] = jnp.zeros_like(r.zero)

    def swap(source, target, number):
        return pltpu.make_async_remote_copy(
            source, target, r.send_x.at[number], r.recv_x.at[number],
            device_id={"stream": 1 - side}, device_id_type=MESH)

    self_kinds = block_kinds(s.head, s.per_group)
    cross_kinds = block_kinds(128, CO_HEADS // groups)
    self_scale, cross_scale = 1.0 / math.sqrt(s.head), 1.0 / math.sqrt(128)

    def in_block(index):
        return pl.ds(pl.multiple_of(index * w, TILE), w)

    def project(part, source, target, bias_ref, line):
        @pl.loop(0, groups)
        def _(g):
            cols = lane(g * inner, inner)
            value = dot(source[:, :w], r.w_in[in_block(g * 3 + part), :])
            if line is not None:
                value = value + bias_ref[g, line : line + 1].astype(wide)
            target[:, cols] = value.astype(low)

    def vector(ref, line, cols=slice(0, w)):
        return ref[line : line + 1, cols].astype(wide)

    def scaled(normal, line, cols):
        return normal[:, cols] * vector(r.gains, line, cols) + vector(r.shifts, line, cols)

    def leave(source, size, weight, residual, line):
        @pl.loop(0, s.parts)
        def _(j):
            cols = lane(j * TILE)
            at = pl.ds(pl.multiple_of(j * size, TILE), size)
            r.acc[:, cols] = (dot(source[:, :size], weight[at, :]) + residual(cols)
                              + vector(r.out_bias, line, cols))

    def norm(normal, inverse):
        summed = r.acc[:, :w]
        mean = jnp.sum(summed, axis=-1, keepdims=True) * (1.0 / w)
        centred = summed - mean
        scale = lax.rsqrt(
            jnp.sum(centred * centred, axis=-1, keepdims=True) * (1.0 / w) + norm_eps)
        normal[:, :w] = centred * scale
        inverse[...] = scale

    def cross_part(begin, end):
        @pl.loop(begin, end)
        def _(g):
            attend_forward(g, cross_kinds, cross_scale, length, rows_dev, r.q, r.pair_k, r.pair_v,
                           r.cross_allowed, r.cross_prob, r.context)

    def feed_part(begin, end):
        @pl.loop(begin, end)
        def _(g):
            for j in range(u // TILE):
                cols = lane(g * u + j * TILE)
                value = (dot(r.h1[:, :w], r.w_up[in_block(g * (u // TILE) + j), :])
                         + r.a_up_bias[g, 0:1, j * TILE : (j + 1) * TILE].astype(wide))
                bell = 0.5 * (1.0 + lax.erf(value * math.sqrt(0.5)))
                r.active[:, cols] = (value * bell).astype(low)
                r.slope[:, cols] = bell + value * (
                    jnp.exp(-0.5 * value * value) * (1.0 / math.sqrt(2.0 * math.pi)))

    gather.received(0)
    gather.later(2)
    gather.received(1)
    gather.later(3)
    gather.shared(0)
    gather.received(2, 0, 1)
    for kind in range(3):
        for step in range(1, groups):
            bias_copy(step, kind).wait()
    for item in enter:
        item.wait()
    gather.settled(0, weights, "cross_in")
    gather.received(2, 2)
    gather.later(4)
    gather.shared(1)
    weights.wait("cross_in")
    project(1, r.x, r.k, None, None)
    swap(r.k, r.pair_k, 0).start()
    project(2, r.x, r.v, r.a_cross_bias, 1)
    swap(r.v, r.pair_v, 1).start()
    gather.received(3, 0, 1)
    project(0, r.x, r.q, r.a_cross_bias, 0)
    weights.load("attend_in", "own")
    gather.settled(1, weights, "cross_out")
    gather.received(3, 2)
    gather.later(5)
    gather.shared(2)
    gather.settled(2, weights, "up")
    gather.received(4, 0, 1)
    swap(r.k, r.pair_k, 0).wait()
    swap(r.v, r.pair_v, 1).wait()
    cross_part(0, groups // 2)
    gather.received(5, 0)
    cross_part(groups // 2, groups)
    gather.received(4, 2)
    gather.received(5, 1)
    gather.shared(3)
    gather.settled(3, weights, "down")
    weights.wait("cross_out")
    leave(r.context, groups * inner, r.w_cross_out, lambda cols: r.x[:, cols].astype(wide), 0)
    norm(r.n1, r.r1)
    r.h1[:, :w] = scaled(r.n1, 0, slice(0, w)).astype(low)
    gather.received(5, 2)
    gather.shared(4, 0, 1)
    weights.wait("up")
    feed_part(0, groups // 2)
    gather.shared(4, 2)
    gather.settled(4, weights, "attend_in", 0, 1)
    feed_part(groups // 2, groups)
    gather.shared(5)
    gather.settled(4, weights, "attend_in", 2)
    gather.settled(5, weights, "attend_out")
    weights.wait("down")
    leave(r.active, groups * u, r.w_down, lambda cols: scaled(r.n1, 0, cols), 1)
    norm(r.n2, r.r2)
    r.h2[:, :w] = scaled(r.n2, 1, slice(0, w)).astype(low)
    weights.wait("attend_in")
    project(0, r.h2, r.q2, r.a_attend_bias, 0)
    project(1, r.h2, r.k2, None, None)
    project(2, r.h2, r.v2, r.a_attend_bias, 1)

    @pl.loop(0, groups)
    def _(g):
        attend_forward(g, self_kinds, self_scale, length, rows_dev, r.q2, r.k2, r.v2,
                       r.self_allowed, r.self_prob, r.context2)

    weights.wait("attend_out")
    leave(r.context2, groups * inner, r.w_attend_out, lambda cols: scaled(r.n2, 1, cols), 2)
    norm(r.n3, r.r3)
    r.layer_rows[:, :w] = scaled(r.n3, 2, slice(0, w)).astype(low)
    for item in outputs.local(0):
        item.start()
    for p in range(len(gather.pieces)):
        gather.drained(p)

    def stores(row):
        return [
            pltpu.make_async_copy(
                r.staged.at[g, :, pl.ds(0, w)],
                r.grads.at[g, pl.ds(pl.multiple_of(row, TILE), TILE), pl.ds(0, w)],
                r.store_sem.at[g])
            for g in range(groups)]

    def weight_grads(left, right, row, size):
        def step(k):
            for g, item in enumerate(stores(row + k * TILE)):
                r.staged[g, :, :w] = dot_tn(
                    left[:, lane(g * size + k * TILE)], right[:, :w]).astype(low)
                item.start()

        return step

    def flush():
        for item in stores(0):
            item.wait()

    def back_norm(incoming, normal, inverse, line):
        r.small_in[3 + line : 4 + line, :w] = down_sum(incoming * normal[:, :w])
        r.small_in[6 + line : 7 + line, :w] = down_sum(incoming)
        out = norm_back(normal[:, :w], inverse[...], vector(r.gains, line), incoming, w)
        r.acc[:, :w] = out
        r.low_grad[:, :w] = out.astype(low)
        r.small_in[line : line + 1, :w] = down_sum(out.astype(low).astype(wide))

    def leave_back(weight, size, row, count):
        total = None
        for j in range(s.parts):
            at = pl.ds(pl.multiple_of(j * size + row, TILE), count)
            part = dot_nt(r.low_grad[:, j * TILE : (j + 1) * TILE], weight[at, :])
            total = part if total is None else total + part
        return total

    def enter_back(d, weight, blocks):
        def step(g):
            total = r.acc[:, :w]
            for b, (ref, start) in enumerate(d(g)):
                total = total + dot_nt(ref[:, lane(start)], weight[in_block(g * blocks + b), :])
            r.acc[:, :w] = total

        return step

    def context_back(weight):
        def step(g):
            r.grad_context[:, lane(g * inner, inner)] = leave_back(
                weight, groups * inner, g * inner, inner).astype(low)

        return step

    def self_step(g):
        attend_backward(g, self_kinds, self_scale, length, rows_dev, r.q2, r.k2, r.v2,
                        r.self_prob, r.grad_context, r.d1, r.d2, r.d3)

    def cross_step(g):
        attend_backward(g, cross_kinds, cross_scale, length, rows_dev, r.q, r.pair_k, r.pair_v,
                        r.cross_prob, r.grad_context, r.d1, r.d2, r.d3)

    def second_norm(_):
        r.small_in[12:13, :] = down_sum(r.d1[...].astype(wide))
        r.small_in[13:14, :] = down_sum(r.d3[...].astype(wide))
        weights.load("cross_in")
        back_norm(r.acc[:, :w], r.n2, r.r2, 1)

    def slope_step(g):
        for j in range(u // TILE):
            cols = lane(g * u + j * TILE)
            value = leave_back(r.w_down, groups * u, g * u + j * TILE, TILE)
            r.dz[:, cols] = (value * r.slope[:, cols]).astype(low)

    def first_norm(_):
        back_norm(r.acc[:, :w], r.n1, r.r1, 0)
        units, width = plan.units, r.small_in.shape[1]
        for g in range(groups):
            for j in range(u // TILE):
                start = g * units + j * TILE
                r.small_in[9 + start // width : 10 + start // width,
                           start % width : start % width + TILE] = down_sum(
                    r.dz[:, g * u + j * TILE : g * u + (j + 1) * TILE].astype(wide))

    def pair_send(_):
        r.small_in[14:15, :] = down_sum(r.d1[...].astype(wide))
        weights.wait("cross_in")
        swap(r.d2, r.back_k, 2).start()
        swap(r.d3, r.back_v, 3).start()

    def pair_take(_):
        swap(r.d2, r.back_k, 2).wait()
        swap(r.d3, r.back_v, 3).wait()
        r.small_in[15:16, :] = down_sum(r.back_v[...].astype(wide))
        small.start()

    def hidden_store(_):
        r.hidden_rows[:, :w] = r.acc[:, :w].astype(low)
        for item in outputs.local(1):
            item.start()

    def attend_grads(k):
        for which_one, d in enumerate((r.d1, r.d2, r.d3)):
            pl.when(k == which_one)(lambda: weight_grads(
                d, r.h2, layout.attend_in + which_one * inner, inner)(0))

    def cross_grads(k):
        for which_one, d in enumerate((r.back_k, r.back_v)):
            pl.when(k == which_one)(lambda: weight_grads(
                d, r.x, layout.total + (1 + which_one) * inner, inner)(0))

    r.small_in[...] = jnp.zeros_like(r.small_in)
    back_norm(r.grad_out[:, :w].astype(wide), r.n3, r.r3, 2)
    pl.loop(0, groups)(context_back(r.w_attend_out))
    weight_grads(r.context2, r.low_grad, layout.attend_out, inner)(0)
    nb = u // TILE
    take = plan.when[which]
    schedule = (
        (0, 4, 2, False, self_step),
        (2, 3, 1, True, attend_grads),
        (2, 4, 2, False, enter_back(lambda g: [(d, g * inner) for d in (r.d1, r.d2, r.d3)],
                                    r.w_in, 3)),
        (4, 1, 1, False, second_norm),
        (5, 4, 2, False, slope_step),
        (5, nb, 1, True, weight_grads(r.active, r.low_grad, layout.down, u)),
        (5 + nb, nb, 1, True, weight_grads(r.dz, r.h1, layout.up, u)),
        (7, 4, 2, False, enter_back(lambda g: [(r.dz, g * u + b * TILE) for b in range(nb)],
                                    r.w_up, nb)),
        (9, 1, 1, False, first_norm),
        (10, 4, 2, False, context_back(r.w_cross_out)),
        (12, 4, 2, False, cross_step),
        (14, 1, 1, False, pair_send),
        (11, 1, 1, True, weight_grads(r.context, r.low_grad, layout.cross_out, inner)),
        (15, 1, 1, True, weight_grads(r.d1, r.x, layout.total, inner)),
        (take, 1, 1, False, pair_take),
        (take, 2, 1, True, cross_grads),
        (take + 2, 4, 2, False, enter_back(
            lambda g: [(d, g * inner) for d in (r.d1, r.back_k, r.back_v)], r.w_in, 3)),
        (take + 4, 1, 1, False, hidden_store),
        (take + 5, 1, 1, False, lambda _: small.middle()),
    )
    storing = sorted({start + n for start, steps, per, keeps, _ in schedule if keeps
                      for n in range(steps)})
    assert len(storing) == sum(steps for _, steps, _, keeps, _ in schedule if keeps)
    hidden_at = take + 5

    @pl.loop(0, max(reduce.iterations(), hidden_at + plan.cuts + groups))
    def _(j):
        flushes = j == 0
        for n in storing:
            flushes = jnp.logical_or(flushes, j == n + 1)
        pl.when(flushes)(flush)
        for start, steps, per, _, step in schedule:
            @pl.when(jnp.logical_and(j >= start, j < start + steps // per))
            def _():
                if per == 1:
                    step(j - start)
                else:
                    pl.loop(0, per)(lambda n: step((j - start) * per + n))
        reduce.iteration(j)
        outputs.step(0, j - 1)
        outputs.step(1, j - hidden_at)

    reduce.drained()
    outputs.drained()
    small.finish()


def shards(
    hidden,
    cotangent,
    segments,
    cross_in,
    cross_bias,
    cross_out,
    up_weight,
    up_bias,
    down_weight,
    attend_in,
    attend_bias,
    attend_out,
    out_bias,
    norm_gains,
    norm_shifts,
):
    groups = lax.axis_size("mp")
    copies = lax.axis_size("dp")
    stride = copies // 4
    side = lax.axis_index("stream")
    member = lax.axis_index("mp")
    copy = lax.axis_index("dp")
    is_image = side == 1
    inner = cross_in.shape[3]
    padded = hidden.shape[2]
    units = up_weight.shape[2]
    length = segments.shape[2]
    text = Setting(TEXT_WIDTH, TEXT_HEADS, TEXT_FF, groups)
    image = Setting(IMAGE_WIDTH, IMAGE_HEADS, IMAGE_FF, groups)
    settings = (text, image)
    layouts = [Layout(s, inner) for s in settings]
    rows_max = max(layout.total for layout in layouts) + 3 * inner
    rows_dev = segments.shape[1] // groups
    tokens = hidden.shape[1] // groups
    co = groups * inner

    def shape(dims, kind=low):
        return jax.ShapeDtypeStruct(dims, kind)

    seg = lax.dynamic_slice_in_dim(segments, member * rows_dev, rows_dev, 1)
    seg_own = lax.dynamic_index_in_dim(seg, side, 0, keepdims=False)
    seg_other = lax.dynamic_index_in_dim(seg, 1 - side, 0, keepdims=False)
    cross_allowed = (seg_other[:, :, None] == seg_own[:, None, :]).astype(wide)
    self_allowed = (seg_own[:, :, None] == seg_own[:, None, :]).astype(wide)

    dma = pltpu.SemaphoreType.DMA

    def real(*dims):
        return pltpu.VMEM(dims, wide)

    def short(*dims):
        return pltpu.VMEM(dims, low)

    chunk, slots, cuts, ring = 64, 20, 8, 4
    widest = max(s.units for s in settings) * groups
    up_rows = max(groups * s.units * s.width for s in settings) // TILE
    heads = max(groups * s.per_group for s in settings)
    pieces, hops = 6, groups - 1
    peers = groups * copies
    small_width = padded // max(1, peers // 16)
    scratch = Scratch(
        w_in=short(groups * 3 * padded, inner),
        w_cross_out=short(padded // TILE * co, TILE),
        w_attend_out=short(padded // TILE * co, TILE),
        w_up=short(up_rows, TILE),
        w_down=short(up_rows, TILE),
        x=short(tokens, padded),
        grad_out=short(tokens, padded),
        q=short(tokens, co),
        k=short(tokens, co),
        v=short(tokens, co),
        pair_k=short(tokens, co),
        pair_v=short(tokens, co),
        back_k=short(tokens, co),
        back_v=short(tokens, co),
        cross_prob=real(CO_HEADS * rows_dev, length, length),
        self_prob=real(heads * rows_dev, length, length),
        context=short(tokens, co),
        context2=short(tokens, co),
        acc=real(tokens, padded),
        n1=real(tokens, padded),
        n2=real(tokens, padded),
        n3=real(tokens, padded),
        r1=real(tokens, 1),
        r2=real(tokens, 1),
        r3=real(tokens, 1),
        h1=short(tokens, padded),
        h2=short(tokens, padded),
        slope=real(tokens, widest),
        active=short(tokens, widest),
        dz=short(tokens, widest),
        q2=short(tokens, co),
        k2=short(tokens, co),
        v2=short(tokens, co),
        d1=short(tokens, co),
        d2=short(tokens, co),
        d3=short(tokens, co),
        low_grad=short(tokens, padded),
        grad_context=short(tokens, co),
        layer_rows=short(tokens, padded),
        hidden_rows=short(tokens, padded),
        zero=short(tokens, IMAGE_WIDTH - TEXT_WIDTH),
        staged=short(ring, TILE, padded),
        from_core=short(slots, 2, groups, chunk, TILE),
        from_y=short(slots, groups, chunk, TILE),
        from_z=short(slots, 2, groups, chunk, TILE),
        far=short(2, slots, chunk, 128),
        own=short(4, 2, groups, chunk, TILE),
        staged_out=real(2, chunk, TILE),
        small_in=real(16, padded),
        small_got=real(peers, 1, small_width),
        small_sum=real(1, small_width),
        small_sem=dma((2,)),
        a_cross_bias=short(groups, 2, inner),
        a_attend_bias=short(groups, 2, inner),
        a_up_bias=short(groups, 1, units),
        send_gz=dma((pieces, 2, hops)),
        recv_gz=dma((pieces, 2, hops)),
        send_gy=dma((pieces, 2, hops)),
        recv_gy=dma((pieces, 2, hops)),
        send_gc=dma((pieces, 2, hops, 2)),
        recv_gc=dma((pieces, 2, hops, 2)),
        weight_sem=dma((pieces, groups, 4)),
        enter_sem=dma((2,)),
        send_b=dma((3, groups)),
        recv_b=dma((3, groups)),
        send_x=dma((4,)),
        recv_x=dma((4,)),
        store_sem=dma((ring,)),
        send_c=dma((slots, 2)),
        recv_c=dma((slots, 2)),
        send_y=dma((slots,)),
        recv_y=dma((slots,)),
        send_z=dma((slots, 2, groups)),
        recv_z=dma((slots, 2, groups)),
        send_f=dma((slots,)),
        recv_f=dma((slots,)),
        own_sem=dma((4, 2)),
        out_sem=dma((2, 2)),
        send_a=dma((2, cuts, 2, hops)),
        recv_a=dma((2, cuts, 2, hops)),
        local_sem=dma((2, groups + 1)),
        send_s=dma((2, peers)),
        recv_s=dma((2, peers)),
        free=pltpu.SemaphoreType.REGULAR((5,)),
    )
    plan = Plan(
        groups=groups, copies=copies, inner=inner, length=length, rows=rows_dev,
        tokens=tokens, units=units, chunk=chunk, slots=slots, cuts=cuts,
        ring=ring, lags=(3, 8, 2, 2),
        when=(26, 24),
    )
    weights = (
        jnp.swapaxes(cross_in[0], 0, 1),
        cross_out[0],
        up_weight[0],
        down_weight[0],
        jnp.swapaxes(attend_in[0], 0, 1),
        attend_out[0],
    )
    line = shape((groups, tokens, padded))
    out = pl.pallas_call(
        partial(layer_kernel, settings, layouts, plan),
        out_shape=(
            line, line, shape((rows_max, TILE), wide), shape((16, padded), wide),
        ) + tuple(shape((groups,) + w.shape) for w in weights)
        + (shape((groups, rows_max, padded)),),
        in_specs=[ANY] * 8 + [VMEM] * 8,
        out_specs=(ANY,) * 3 + (VMEM,) + (ANY,) * 7,
        scratch_shapes=list(scratch),
        compiler_params=pltpu.CompilerParams(
            collective_id=0, has_side_effects=True, vmem_limit_bytes=VMEM_LIMIT),
        name="layer",
    )(*weights, hidden[0], cotangent[0], cross_bias[0], attend_bias[0], up_bias,
      out_bias[0], norm_gains[0], norm_shifts[0],
      cross_allowed.reshape(tokens, length), self_allowed.reshape(tokens, length))
    layer_out, hidden_grad, reduced, small = out[:4]

    if stride > 1:
        teams = [[q * stride + b for b in range(stride)] for q in range(4)]
        reduced = lax.psum_scatter(
            reduced.astype(low), "dp", scatter_dimension=1, axis_index_groups=teams, tiled=True
        ).astype(wide)
    columns = padded // copies
    real_block = copy * columns < jnp.where(is_image, IMAGE_WIDTH, TEXT_WIDTH)
    reduced = jnp.where(real_block, reduced, 0.0)

    part = inner // copies
    vector_grads = lax.dynamic_slice_in_dim(small[:9], copy * columns, columns, 1)
    up_bias_grad = lax.dynamic_slice_in_dim(
        small[9:12].reshape(groups * units), (member * copies + copy) * (units // copies),
        units // copies, 0)
    pair_grads = lax.dynamic_slice_in_dim(
        small[12:16], (member * copies + copy) * part, part, 1)

    def unpack(s, layout, reduced):
        u = s.units

        def turned(start):
            block = reduced[start : start + 3 * inner].reshape(3, inner, columns)
            return block.transpose(2, 0, 1)

        return (
            turned(layout.total),
            reduced[layout.cross_out : layout.cross_out + inner],
            jnp.pad(reduced[layout.up : layout.up + u].T, ((0, 0), (0, units - u))),
            jnp.pad(reduced[layout.down : layout.down + u], ((0, units - u), (0, 0))),
            turned(layout.attend_in),
            reduced[layout.attend_out : layout.attend_out + inner],
        )

    g_cross_in, g_cross_out, g_up, g_down, g_attend_in, g_attend_out = lax.cond(
        is_image, partial(unpack, image, layouts[1]), partial(unpack, text, layouts[0]), reduced)
    return (
        layer_out.reshape(1, groups * tokens, padded),
        hidden_grad.reshape(1, groups * tokens, padded),
        g_cross_in[None],
        pair_grads[None, 2:4],
        g_cross_out[None],
        g_up[None],
        up_bias_grad[None],
        g_down[None],
        g_attend_in[None],
        pair_grads[None, 0:2],
        g_attend_out[None],
        vector_grads[None, 0:3],
        vector_grads[None, 3:6],
        vector_grads[None, 6:9],
    )


def solution(mesh):
    placed = (
        P("stream", "dp", None),
        P("stream", "dp", None),
        P(None, "dp", None),
        P("stream", None, None, "mp"),
        P("stream", None, "mp"),
        P("stream", "mp", None),
        P("stream", None, "mp"),
        P("stream", "mp"),
        P("stream", "mp", None),
        P("stream", None, None, "mp"),
        P("stream", None, "mp"),
        P("stream", "mp", None),
        P("stream", None, None),
        P("stream", None, None),
        P("stream", None, None),
    )
    return jax.shard_map(
        shards,
        mesh=mesh,
        in_specs=placed,
        out_specs=(
            P("stream", "dp", None),
            P("stream", "dp", None),
            P("stream", "dp", None, "mp"),
            P("stream", None, ("mp", "dp")),
            P("stream", "mp", "dp"),
            P("stream", "dp", "mp"),
            P("stream", ("mp", "dp")),
            P("stream", "mp", "dp"),
            P("stream", "dp", None, "mp"),
            P("stream", None, ("mp", "dp")),
            P("stream", "mp", "dp"),
            P("stream", None, "dp"),
            P("stream", None, "dp"),
            P("stream", None, "dp"),
        ),
        check_vma=False,
    )
```

```python
import math
from functools import partial
from typing import Any, NamedTuple

import jax
import jax.numpy as jnp
from jax import lax
from jax.experimental import pallas as pl
from jax.experimental.pallas import tpu as pltpu
from jax.sharding import PartitionSpec as P

TEXT_WIDTH = 768
TEXT_HEADS = 12
TEXT_FF = 3072
IMAGE_WIDTH = 1024
IMAGE_HEADS = 8
IMAGE_FF = 1024
CO_HEADS = 8

norm_eps = 1e-12
masked_score = -1000000000.0
low = jnp.bfloat16
wide = jnp.float32
ANY = pl.BlockSpec(memory_space=pl.ANY)
VMEM = pl.BlockSpec(memory_space=pltpu.VMEM)
MESH = pl.DeviceIdType.MESH
VMEM_LIMIT = 65400 * 1024
TILE = 256


def dot(left, right):
    return jnp.dot(left, right, preferred_element_type=wide)


def dot_nt(left, right):
    return lax.dot_general(left, right, (((1,), (1,)), ((), ())), preferred_element_type=wide)


def dot_tn(left, right):
    return lax.dot_general(left, right, (((0,), (0,)), ((), ())), preferred_element_type=wide)


class Setting:
    def __init__(self, width, count, units, groups):
        self.width = width
        self.head = width // count
        self.units = units // groups
        self.lanes = width // groups
        self.parts = width // TILE
        self.per_group = count // groups


class Layout:
    def __init__(self, inner, units):
        self.units = units
        self.attend_out = 0
        self.attend_in = inner
        self.down = 4 * inner
        self.up = 4 * inner + units
        self.cross_out = 4 * inner + 2 * units
        self.cross_in = 5 * inner + 2 * units
        self.total = 8 * inner + 2 * units


def lane(start, size=TILE):
    return pl.ds(pl.multiple_of(start, 128), size)


def norm_back(normal, inverse, gain, incoming, w):
    scaled = incoming * gain
    first = jnp.sum(scaled, axis=-1, keepdims=True) * (1.0 / w)
    second = jnp.sum(scaled * normal, axis=-1, keepdims=True) * (1.0 / w)
    return inverse * (scaled - first - normal * second)


def down_sum(value):
    return jnp.sum(value, axis=0, keepdims=True)


def softmax_t(scores, allowed, scale):
    scores = jnp.where(allowed, scores, masked_score / scale)
    top = jnp.max(scores, axis=0, keepdims=True)
    exponent = jnp.exp2((scores - top) * (scale * math.log2(math.e)))
    return exponent * (1.0 / jnp.sum(exponent, axis=0, keepdims=True))


def score_grad_t(p, grad):
    return (p * (grad - jnp.sum(grad * p, axis=0, keepdims=True))).astype(low)


def halves(value):
    index = lax.broadcasted_iota(jnp.int32, value.shape, 1)
    zero = jnp.zeros_like(value)
    return jnp.concatenate(
        [jnp.where(index < 64, value, zero), jnp.where(index >= 64, value, zero)], axis=0)


def lower(value):
    index = lax.broadcasted_iota(jnp.int32, value.shape, 1)
    return jnp.where(index < 64, value, jnp.zeros_like(value))


def side_by_side(parts, axis=1):
    return parts[0] if len(parts) == 1 else jnp.concatenate(parts, axis=axis)


def split(value, count):
    size = value.shape[1] // count
    return [value[:, n * size : (n + 1) * size] for n in range(count)]


def block_kinds(head, heads):
    if head == 128:
        return [0] * heads
    return [2] * (heads // 2) + [1] * (heads % 2)


def spread_heads(kind, value):
    return halves(value) if kind == 2 else lower(value) if kind == 1 else value


def attend_forward(group, kinds, scale, length, rows, q, k, v, allowed, prob, context):
    heads = sum(max(kind, 1) for kind in kinds)
    base = group * len(kinds) * 128
    ats = [slice(r * length, (r + 1) * length) for r in range(rows)]
    step = 0
    for b, kind in enumerate(kinds):
        cols = lane(base + b * 128, 128)
        count = max(kind, 1)
        groups = [ats]
        for members in groups:
            scores = side_by_side(
                [dot_nt(k[at, cols], spread_heads(kind, q[at, cols])) for at in members])
            masks = side_by_side([allowed[at, :] for at in members for _ in range(count)])
            p = softmax_t(scores, masks > 0, scale)
            low_p = p.astype(low)
            tiles = split(p, count * len(members))
            low_tiles = split(low_p, count * len(members))
            out = [
                dot_tn(side_by_side(low_tiles[n * count : (n + 1) * count], 0),
                       spread_heads(kind, v[at, cols]))
                for n, at in enumerate(members)]
            for n, at in enumerate(members):
                r = ats.index(at)
                context[at, cols] = out[n].astype(low)
                for c in range(count):
                    prob[group * heads * rows + r * heads + step + c] = tiles[n * count + c]
        step += count


def attend_backward(group, kinds, scale, length, rows, q, k, v, prob, grad, dq, dk, dv):
    heads = sum(max(kind, 1) for kind in kinds)
    base = group * len(kinds) * 128
    ats = [slice(r * length, (r + 1) * length) for r in range(rows)]
    step = 0
    for b, kind in enumerate(kinds):
        cols = lane(base + b * 128, 128)
        count = max(kind, 1)
        groups = [ats]
        for members in groups:
            dcs = [spread_heads(kind, grad[at, cols]) for at in members]
            qs = [spread_heads(kind, q[at, cols]) for at in members]
            gp = side_by_side([dot_nt(v[at, cols], dc) for at, dc in zip(members, dcs)])
            p = side_by_side([
                prob[group * heads * rows + ats.index(at) * heads + step + c]
                for at in members for c in range(count)])
            low_p = split(p.astype(low), len(members))
            ds = split(score_grad_t(p, gp), len(members))
            grad_v = [dot(a, dc) for a, dc in zip(low_p, dcs)]
            grad_k = [dot(a, two) * scale for a, two in zip(ds, qs)]
            grad_q = [dot_tn(a, k[at, cols]) * scale for a, at in zip(ds, members)]
            for n, at in enumerate(members):
                value = grad_q[n]
                if kind:
                    index = lax.broadcasted_iota(jnp.int32, (length, 128), 1)
                    other = value[length:] if kind == 2 else jnp.zeros((length, 128), wide)
                    value = jnp.where(index < 64, value[:length], other)
                dq[at, cols] = value.astype(low)
                dk[at, cols] = grad_k[n].astype(low)
                dv[at, cols] = grad_v[n].astype(low)
        step += count
class Refs:
    def __init__(self, *groups):
        for group in groups:
            self.__dict__.update(group._asdict())


class Inputs(NamedTuple):
    cross_in: Any
    cross_out: Any
    up: Any
    down: Any
    attend_in: Any
    attend_out: Any
    hidden: Any
    cotangent: Any
    cross_bias: Any
    attend_bias: Any
    up_bias: Any
    out_bias: Any
    gains: Any
    shifts: Any
    cross_allowed: Any
    self_allowed: Any


class Results(NamedTuple):
    layer_full: Any
    hidden_full: Any
    reduced: Any
    small_out: Any
    f_cross_in: Any
    f_cross_out: Any
    f_up: Any
    f_down: Any
    f_attend_in: Any
    f_attend_out: Any
    grads: Any


class Scratch(NamedTuple):
    w_in: Any
    w_cross_out: Any
    w_attend_out: Any
    w_up: Any
    w_down: Any
    x: Any
    grad_out: Any
    q: Any
    k: Any
    v: Any
    pair_k: Any
    pair_v: Any
    back: Any
    cross_prob: Any
    self_prob: Any
    context: Any
    context2: Any
    acc: Any
    n1: Any
    n2: Any
    n3: Any
    r1: Any
    r2: Any
    r3: Any
    h1: Any
    h2: Any
    slope: Any
    active: Any
    dz: Any
    q2: Any
    k2: Any
    v2: Any
    d: Any
    low_grad: Any
    grad_context: Any
    layer_rows: Any
    hidden_rows: Any
    zero: Any
    staged: Any
    from_core: Any
    from_y: Any
    from_z: Any
    far: Any
    own: Any
    staged_out: Any
    small_in: Any
    small_got: Any
    small_sum: Any
    small_sem: Any
    a_cross_bias: Any
    a_attend_bias: Any
    a_up_bias: Any
    send_gz: Any
    recv_gz: Any
    send_gy: Any
    recv_gy: Any
    send_gc: Any
    recv_gc: Any
    weight_sem: Any
    enter_sem: Any
    send_b: Any
    recv_b: Any
    send_x: Any
    recv_x: Any
    store_sem: Any
    send_c: Any
    recv_c: Any
    send_y: Any
    recv_y: Any
    send_z: Any
    recv_z: Any
    send_f: Any
    recv_f: Any
    own_sem: Any
    out_sem: Any
    send_a: Any
    recv_a: Any
    local_sem: Any
    send_s: Any
    recv_s: Any
    free: Any
    zero_sem: Any


class Plan(NamedTuple):
    groups: Any
    copies: Any
    inner: Any
    length: Any
    rows: Any
    tokens: Any
    units: Any
    chunk: Any
    slots: Any
    cuts: Any
    ring: Any
    lags: Any
    when: Any
    forward: Any


def layer_kernel(settings, layout, plan, *refs):
    first, second = len(Inputs._fields), len(Inputs._fields) + len(Results._fields)
    r = Refs(Inputs(*refs[:first]), Results(*refs[first:second]), Scratch(*refs[second:]))
    side = lax.axis_index("stream")
    greet(plan, r)
    for which, s in enumerate(settings):
        pl.when(side == which)(partial(run_stream, which, s, layout, plan, r))


def peer_of(plan, offset):
    groups, copies = plan.groups, plan.copies
    me = lax.axis_index("mp") * copies + lax.axis_index("dp")
    index = lax.rem(me + offset, groups * copies)
    return me, index, {"mp": index // copies, "dp": lax.rem(index, copies)}


def greet(plan, r):
    barrier = pltpu.get_barrier_semaphore()
    count = plan.groups * plan.copies

    @pl.loop(1, count)
    def _(offset):
        pl.semaphore_signal(barrier, inc=1, device_id=peer_of(plan, offset)[2], device_id_type=MESH)

    pl.semaphore_signal(barrier, inc=1, device_id={"stream": 1 - lax.axis_index("stream")},
                        device_id_type=MESH)
    pl.semaphore_wait(barrier, count)


class Piece(NamedTuple):
    own: Any
    gathered: Any
    every: Any
    whole: Any
    ref: Any
    full: Any
    held: Any
    place: Any


def pieces_of(s, plan, r):
    w, u, inner, groups = s.width, s.units, plan.inner, plan.groups
    pieces, named = [], {}

    def add(name, ref, full, held, cut, whole, place):
        named.setdefault(name, []).append(len(pieces))
        pieces.append(Piece(
            lambda part: cut(ref, (), part), lambda z, part: cut(full, (z,), part),
            lambda part: cut(full, (slice(None),), part), whole, ref, full, held, place))

    def matrix(name, b, ref, full):
        add(name, ref, full, r.w_in,
            lambda a, at, part: a.at[at + (b, pl.ds(part * (w // 4), w // 4), slice(None))],
            lambda a: [a.at[b, pl.ds(0, w), :]],
            lambda z: [pl.ds(pl.multiple_of((z * 3 + b) * w, TILE), w)])

    def rows(name, j, size, ref, full, held):
        add(name, ref, full, held,
            lambda a, at, part: a.at[
                at + (pl.ds(j * TILE + part * (TILE // 4), TILE // 4), pl.ds(0, w))],
            lambda a: [a.at[pl.ds(j * TILE, TILE), pl.ds(b * TILE, TILE)] for b in range(s.parts)],
            lambda z: [pl.ds(pl.multiple_of((b * groups + z) * size + j * TILE, TILE), TILE)
                       for b in range(s.parts)])

    def columns(name, j, ref, full, held):
        add(name, ref, full, held,
            lambda a, at, part: a.at[at + (pl.ds(part * (w // 4), w // 4), pl.ds(j * TILE, TILE))],
            lambda a: [a.at[pl.ds(0, w), pl.ds(j * TILE, TILE)]],
            lambda z: [pl.ds(pl.multiple_of((z * (u // TILE) + j) * w, TILE), w)])

    matrix("k", 1, r.cross_in, r.f_cross_in)
    matrix("v", 2, r.cross_in, r.f_cross_in)
    matrix("q", 0, r.cross_in, r.f_cross_in)
    rows("cross_out", 0, inner, r.cross_out, r.f_cross_out, r.w_cross_out)
    for j in range(u // TILE):
        columns("up", j, r.up, r.f_up, r.w_up)
    for j in range(u // TILE):
        rows("down", j, u, r.down, r.f_down, r.w_down)
    for b in range(3):
        matrix("attend_in", b, r.attend_in, r.f_attend_in)
    rows("attend_out", 0, inner, r.attend_out, r.f_attend_out, r.w_attend_out)
    return pieces, named


class Gather:
    def __init__(self, s, plan, r):
        self.groups, self.r = plan.groups, r
        stride, copy = plan.copies // 4, lax.axis_index("dp")
        self.z = lax.axis_index("mp")
        self.quarter = lax.rem(copy // stride, 4)
        base = lax.rem(copy, stride)
        self.to_y = {"dp": (self.quarter ^ 2) * stride + base}
        self.to_c = {"dp": (self.quarter ^ 1) * stride + base}
        self.at_end = jnp.logical_or(self.z == 0, self.z == self.groups - 1)
        self.pieces, self.named = pieces_of(s, plan, r)

    def z_copy(self, p, way, hop):
        step = 1 - 2 * way
        origin = self.z - hop * step
        piece = self.pieces[p]
        dst = piece.gathered(origin, self.quarter)
        src = piece.own(self.quarter) if hop == 0 else dst
        return pltpu.make_async_remote_copy(
            src, dst, self.r.send_gz.at[p, way, hop], self.r.recv_gz.at[p, way, hop],
            device_id={"mp": self.z + step}, device_id_type=MESH)

    def block(self, p, way, hop, whose):
        return self.pieces[p].gathered(self.z - (hop + 1) * (1 - 2 * way), whose)

    def z_arrival(self, p, way, hop):
        block = self.block(p, way, hop, self.quarter)
        return pltpu.make_async_remote_copy(
            block, block, self.r.send_gz.at[p, way, hop], self.r.recv_gz.at[p, way, hop],
            device_id={"mp": self.z - (1 - 2 * way)}, device_id_type=MESH)

    def y_copy(self, p, way, hop, mine=True):
        block = self.block(p, way, hop, self.quarter if mine else self.quarter ^ 2)
        return pltpu.make_async_remote_copy(
            block, block, self.r.send_gy.at[p, way, hop], self.r.recv_gy.at[p, way, hop],
            device_id=self.to_y, device_id_type=MESH)

    def c_copy(self, p, which, mine=True):
        whose = (self.quarter if mine else self.quarter ^ 1) ^ (2 * which)
        block = self.pieces[p].every(whose)
        return pltpu.make_async_remote_copy(
            block, block, self.r.send_gc.at[p, which], self.r.recv_gc.at[p, which],
            device_id=self.to_c, device_id_type=MESH)

    def sends(self, way, hop):
        last = self.groups - 1
        if way == 0:
            return jnp.logical_and(self.z >= hop, self.z < last)
        return jnp.logical_and(self.z <= last - hop, self.z > 0)

    def arrives(self, way, hop):
        return self.z >= hop + 1 if way == 0 else self.z <= self.groups - 2 - hop

    def each(self, test, action, hops=None):
        for hop in range(self.groups - 1) if hops is None else hops:
            for way in range(2):
                pl.when(test(way, hop))(partial(action, way, hop))

    def own(self, p):
        for way in range(2):
            pl.when(self.sends(way, 0))(lambda: self.z_copy(p, way, 0).start())

    def begin(self, ahead):
        for p in range(ahead):
            self.own(p)
        for p in range(ahead, len(self.pieces)):
            pl.when(self.at_end)(partial(self.own, p))

    def wave(self, i, ahead):
        count, last = len(self.pieces), self.groups - 2
        for hop in range(self.groups - 1):
            if 0 <= i - hop < count:
                self.received(i - hop, hop)
        if 0 <= i - last < count:
            self.c_copy(i - last, 0).start()
        if i + ahead < count:
            pl.when(jnp.logical_not(self.at_end))(partial(self.own, i + ahead))
        for hop in range(self.groups - 1):
            if 0 <= i - hop - 1 < count:
                self.shared(i - hop - 1, hop)
        if 0 <= i - last - 1 < count:
            self.c_copy(i - last - 1, 1).start()

    def waves(self):
        return len(self.pieces) + self.groups - 1

    def received(self, p, *hops):
        def action(way, hop):
            self.z_arrival(p, way, hop).wait_recv()
            if hop + 1 < self.groups - 1:
                pl.when(self.sends(way, hop + 1))(lambda: self.z_copy(p, way, hop + 1).start())
            self.y_copy(p, way, hop).start()

        self.each(self.arrives, action, hops or None)

    def shared(self, p, *hops):
        def action(way, hop):
            self.y_copy(p, way, hop, mine=False).wait_recv()

        self.each(self.arrives, action, hops or None)

    def settled(self, weights, *names):
        for name in names:
            for p in self.named[name]:
                for which in range(2):
                    self.c_copy(p, which, mine=False).wait_recv()

                def action(way, hop):
                    for item in weights.copies(p, self.z - (hop + 1) * (1 - 2 * way), False):
                        item.start()

                self.each(self.arrives, action)

    def drained(self, p):
        self.each(self.sends, lambda way, hop: self.z_copy(p, way, hop).wait_send())

        self.each(self.arrives, lambda way, hop: self.y_copy(p, way, hop).wait_send())
        for which in range(2):
            self.c_copy(p, which).wait_send()


class Weights:
    def __init__(self, s, plan, r):
        self.r, self.groups = r, plan.groups
        self.z = lax.axis_index("mp")
        self.pieces, self.named = pieces_of(s, plan, r)

    def copies(self, p, z, own):
        piece = self.pieces[p]
        blocks = piece.whole(piece.ref if own else piece.full.at[z])
        for b, (src, rows) in enumerate(zip(blocks, piece.place(z))):
            yield pltpu.make_async_copy(src, piece.held.at[rows], self.r.weight_sem.at[p, z, b])

    def load_own(self, *names):
        for name in names:
            for p in self.named[name]:
                for item in self.copies(p, self.z, True):
                    item.start()

    def load_rest(self, *names):
        for name in names:
            for p in self.named[name]:
                @pl.loop(0, self.groups)
                def _(z):
                    @pl.when(self.z != z)
                    def _():
                        for item in self.copies(p, z, False):
                            item.start()

    def wait(self, *names):
        for name in names:
            for p in self.named[name]:
                @pl.loop(0, self.groups)
                def _(z):
                    for item in self.copies(p, z, False):
                        item.wait()


class Outputs:
    def __init__(self, s, plan, r):
        self.s, self.r, self.groups, self.cuts = s, r, plan.groups, plan.cuts
        self.z = lax.axis_index("mp")
        self.last = self.groups - 1
        self.rows = plan.tokens // self.cuts
        self.pairs = ((r.layer_rows, r.layer_full), (r.hidden_rows, r.hidden_full))

    def cut(self, ref, k):
        return ref.at[pl.ds(pl.multiple_of(k * self.rows, self.rows), self.rows),
                      pl.ds(0, self.s.width)]

    def copy(self, which, k, way, hop, arrival=False):
        step = 1 - 2 * way
        origin = self.z - (hop + 1 if arrival else hop) * step
        rows, full = self.pairs[which]
        dst = self.cut(full.at[origin], k)
        src = self.cut(rows, k) if hop == 0 and not arrival else dst
        return pltpu.make_async_remote_copy(
            src, dst, self.r.send_a.at[which, k, way, hop], self.r.recv_a.at[which, k, way, hop],
            device_id={"mp": self.z + step}, device_id_type=MESH)

    def sends(self, way, hop):
        if way == 0:
            return jnp.logical_and(self.z >= hop, self.z < self.last)
        return jnp.logical_and(self.z <= self.last - hop, self.z > 0)

    def arrives(self, way, hop):
        return self.z >= hop + 1 if way == 0 else self.z <= self.last - 1 - hop

    def begin(self, which):
        @pl.loop(0, self.cuts)
        def _(k):
            for way in range(2):
                pl.when(self.sends(way, 0))(lambda: self.copy(which, k, way, 0).start())

    def step(self, which, k, begun=False):
        for hop in range(1 if begun else 0, self.groups):
            now = k - hop

            @pl.when(jnp.logical_and(now >= 0, now < self.cuts))
            def _():
                for way in range(2):
                    if hop:
                        pl.when(self.arrives(way, hop - 1))(
                            lambda: self.copy(which, now, way, hop - 1, True).wait_recv())
                    if hop < self.last:
                        pl.when(self.sends(way, hop))(
                            lambda: self.copy(which, now, way, hop).start())

    def local(self, which):
        rows, full = self.pairs[which]
        width = self.s.width
        items = [pltpu.make_async_copy(rows.at[:, pl.ds(0, width)],
                                       full.at[self.z, :, pl.ds(0, width)],
                                       self.r.local_sem.at[which, self.groups])]
        padded = full.shape[2]
        if width < padded:
            items += [pltpu.make_async_copy(
                self.r.zero, full.at[z, :, pl.ds(width, padded - width)],
                self.r.local_sem.at[which, z]) for z in range(self.groups)]
        return items

    def drained(self):
        for which in range(2):
            @pl.loop(0, self.cuts)
            def _(k):
                for way in range(2):
                    for hop in range(self.last):
                        pl.when(self.sends(way, hop))(
                            lambda: self.copy(which, k, way, hop).wait_send())
            for item in self.local(which):
                item.wait()


class Reduce:
    def __init__(self, which, s, layout, plan, r):
        self.text = which == 0
        self.r, self.groups, self.chunk = r, plan.groups, plan.chunk
        self.slots, self.lags = plan.slots, plan.lags
        self.inner, self.used = plan.inner, s.lanes // self.chunk
        self.narrow = 4 * self.used
        self.feed = s.units // self.chunk
        self.layout = layout
        self.count = self.narrow + 2 * self.feed + plan.inner // self.chunk * 4
        stride, copy = plan.copies // 4, lax.axis_index("dp")
        quarter = lax.rem(copy // stride, 4)
        base = lax.rem(copy, stride)
        self.z = lax.axis_index("mp")
        self.y, self.core = quarter // 2, lax.rem(quarter, 2)
        self.to_y = {"dp": (quarter ^ 2) * stride + base}
        self.to_c = {"dp": (quarter ^ 1) * stride + base}
        self.last = self.groups - 1

    def widths(self, action):
        if not self.text:
            action(TILE, TILE, False)
        else:
            pl.when(self.core == 0)(partial(action, TILE, 128, False))
            pl.when(self.core == 1)(partial(action, 128, TILE, True))

    def first_lane(self, core, y):
        if self.text:
            return pl.multiple_of(jnp.where(core == 0, y * 2 * TILE, TILE + y * 128), 128)
        return pl.multiple_of((2 * y + core) * TILE, 128)

    def rows(self, i):
        early = (i // self.used) * self.inner + lax.rem(i, self.used) * self.chunk
        n = i - self.narrow
        late = jnp.where(
            n < self.feed, self.layout.down + n * self.chunk,
            jnp.where(n < 2 * self.feed, self.layout.up + (n - self.feed) * self.chunk,
                      self.layout.cross_out + (n - 2 * self.feed) * self.chunk))
        start = jnp.where(i < self.narrow, early, late)
        return pl.ds(pl.multiple_of(start, self.chunk), self.chunk)

    def slot(self, i):
        return lax.rem(i, self.slots)

    def core_copy(self, i, k, other):
        n = self.slot(i)
        return pltpu.make_async_remote_copy(
            self.r.grads.at[:, self.rows(i), pl.ds(self.first_lane(1 - self.core, k), other)],
            self.r.from_core.at[n, k, :, :, pl.ds(0, other)],
            self.r.send_c.at[n, k], self.r.recv_c.at[n, k],
            device_id=self.to_c, device_id_type=MESH)

    def core_arrival(self, i, k, size):
        n = self.slot(i)
        block = self.r.from_core.at[n, k, :, :, pl.ds(0, size)]
        return pltpu.make_async_remote_copy(
            block, block, self.r.send_c.at[n, k], self.r.recv_c.at[n, k],
            device_id=self.to_c, device_id_type=MESH)

    def own_load(self, i, k, size):
        n = lax.rem(i, 4)
        return pltpu.make_async_copy(
            self.r.grads.at[:, self.rows(i), pl.ds(self.first_lane(self.core, k), size)],
            self.r.own.at[n, k, :, :, pl.ds(0, size)], self.r.own_sem.at[n, k])

    def y_copy(self, i, size):
        n = self.slot(i)
        return pltpu.make_async_remote_copy(
            self.r.from_core.at[n, 1 - self.y, :, :, pl.ds(0, size)],
            self.r.from_y.at[n, :, :, pl.ds(0, size)],
            self.r.send_y.at[n], self.r.recv_y.at[n], device_id=self.to_y, device_id_type=MESH)

    def z_copy(self, i, way, t, size, fresh):
        n = self.slot(i)
        dst = self.r.from_z.at[n, way, t, :, pl.ds(0, size)]
        src = self.r.from_core.at[n, self.y, t, :, pl.ds(0, size)] if fresh else dst
        return pltpu.make_async_remote_copy(
            src, dst, self.r.send_z.at[n, way, t], self.r.recv_z.at[n, way, t],
            device_id={"mp": self.z + 1 - 2 * way}, device_id_type=MESH)

    def far_copy(self, i):
        n = self.slot(i)
        return pltpu.make_async_remote_copy(
            self.r.far.at[0, n], self.r.far.at[1, n], self.r.send_f.at[n], self.r.recv_f.at[n],
            device_id=self.to_y, device_id_type=MESH)

    def out_store(self, i, start, size):
        n = lax.rem(i, 2)
        return pltpu.make_async_copy(
            self.r.staged_out.at[n, :, pl.ds(start, size)],
            self.r.reduced.at[self.rows(i), pl.ds(start, size)],
            self.r.out_sem.at[1 if start else 0, n])

    def credit(self, i, sem):
        pl.when(i >= self.slots)(lambda: pl.semaphore_wait(sem, 1))

    def stage_a(self, i):
        self.credit(i, self.r.free.at[0])

        def action(size, other, far):
            for k in range(2):
                self.core_copy(i, k, other).start()
                self.own_load(i, k, size).start()

        self.widths(action)

    def stage_b(self, i):
        n = self.slot(i)

        def action(size, other, far):
            for k in range(2):
                self.core_arrival(i, k, size).wait_recv()
                self.own_load(i, k, size).wait()
                self.r.from_core[n, k, :, :, :size] += self.r.own[lax.rem(i, 4), k, :, :, :size]
            self.credit(i, self.r.free.at[1])
            self.y_copy(i, size).start()

        self.widths(action)

    def z_step(self, hop, i):
        n = self.slot(i)

        def action(size, other, far):
            for way in range(2):
                t = self.z + (1 - 2 * way) * (self.groups - hop)

                @pl.when(t <= self.last if way == 0 else t >= 0)
                def _():
                    first = self.z == (0 if way == 0 else self.last)
                    pl.when(first)(lambda: self.z_copy(i, way, t, size, True).start())

                    @pl.when(jnp.logical_not(first))
                    def _():
                        self.z_copy(i, way, t, size, False).wait_recv()
                        self.r.from_z[n, way, t, :, :size] += (
                            self.r.from_core[n, self.y, t, :, :size])
                        self.z_copy(i, way, t, size, False).start()

        self.widths(action)

    def stage_c(self, i):
        n = self.slot(i)

        def action(size, other, far):
            self.y_copy(i, size).wait_recv()
            self.r.from_core[n, self.y, :, :, :size] += self.r.from_y[n, :, :, :size]

        self.widths(action)
        pl.when(self.z < self.last)(lambda: self.credit(i, self.r.free.at[2]))
        pl.when(self.z > 0)(lambda: self.credit(i, self.r.free.at[3]))
        self.z_step(1, i)

    def final(self, i):
        n = self.slot(i)

        def action(size, other, far):
            for way in range(2):
                edge = 0 if way == 0 else self.last

                @pl.when(self.z != edge)
                def _():
                    self.z_copy(i, way, self.z, size, False).wait_recv()

                @pl.when(self.z == edge)
                def _():
                    self.r.from_z[n, way, self.z, :, :size] = jnp.zeros((self.chunk, size), low)

            total = (self.r.from_core[n, self.y, self.z, :, :size].astype(wide)
                     + self.r.from_z[n, 0, self.z, :, :size].astype(wide)
                     + self.r.from_z[n, 1, self.z, :, :size].astype(wide))

            def keep():
                pl.when(i >= 2)(lambda: self.out_store(i - 2, 0, size).wait())
                self.r.staged_out[lax.rem(i, 2), :, :size] = total
                self.out_store(i, 0, size).start()

            if far:
                pl.when(self.y == 0)(keep)

                @pl.when(self.y == 1)
                def _():
                    pl.when(i >= self.slots)(lambda: self.far_copy(i - self.slots).wait_send())
                    self.credit(i, self.r.free.at[4])
                    self.r.far[0, n] = total.astype(low)
                    self.far_copy(i).start()
            else:
                keep()
            for k in range(2):
                self.core_copy(i, k, other).wait_send()
            self.y_copy(i, size).wait_send()
            for way in range(2):
                for hop in range(1, self.groups):
                    t = self.z + (1 - 2 * way) * (self.groups - hop)
                    pl.when(t <= self.last if way == 0 else t >= 0)(
                        lambda: self.z_copy(i, way, t, size, True).wait_send())

        self.widths(action)

        @pl.when(i < self.count - self.slots)
        def _():
            def tell(index, target):
                pl.semaphore_signal(self.r.free.at[index], inc=1, device_id=target,
                                    device_id_type=MESH)

            tell(0, self.to_c)
            tell(1, self.to_y)
            pl.when(self.z > 0)(lambda: tell(2, {"mp": self.z - 1}))
            pl.when(self.z < self.last)(lambda: tell(3, {"mp": self.z + 1}))

    def land(self, i):
        n = self.slot(i)

        def action(size, other, far):
            if not far:
                return

            @pl.when(self.y == 0)
            def _():
                self.far_copy(i).wait_recv()
                pl.when(i >= 2)(lambda: self.out_store(i - 2, size, size).wait())
                self.r.staged_out[lax.rem(i, 2), :, size : 2 * size] = self.r.far[1, n].astype(wide)
                self.out_store(i, size, size).start()

                @pl.when(i < self.count - self.slots)
                def _():
                    pl.semaphore_signal(self.r.free.at[4], inc=1, device_id=self.to_y,
                                        device_id_type=MESH)

        self.widths(action)

    def zeros(self, s, zero):
        blocks = [(4 * self.chunk * n + self.used * self.chunk, self.inner - self.used * self.chunk)
                  for n in range(4)] if self.used * self.chunk < self.inner else []
        for start in (self.layout.down, self.layout.up):
            blocks += [(row, TILE) for row in range(start + s.units, start + self.layout.units, TILE)]
        number = 0
        for always, group in ((True, blocks), (False, [(row, TILE) for row in range(
                0, self.layout.total, TILE)] if self.text else [])):
            test = self.y + self.core == 2
            for row, size in group:
                yield (jnp.logical_not(test) if always and self.text else test if self.text
                       else self.y >= 0, pltpu.make_async_copy(
                    zero.at[pl.ds(0, size), pl.ds(0, TILE)],
                    self.r.reduced.at[pl.ds(row, size)], self.r.zero_sem.at[number]))
                number += 1

    def iteration(self, j):
        lag_b, lag_c, lag_z, lag_f = self.lags

        def at(i, stage):
            pl.when(jnp.logical_and(i >= 0, i < self.count))(lambda: stage(i))

        at(j, self.stage_a)
        at(j - lag_b, self.stage_b)
        at(j - lag_c, self.stage_c)
        for hop in range(2, self.groups):
            at(j - lag_c - lag_z * (hop - 1), partial(self.z_step, hop))
        done = lag_c + lag_z * (self.groups - 1)
        at(j - done, self.final)
        if self.text:
            at(j - done - lag_f, self.land)

    def iterations(self):
        lag_b, lag_c, lag_z, lag_f = self.lags
        return self.count + lag_c + lag_z * (self.groups - 1) + (lag_f if self.text else 0)

    def drained(self):
        def action(size, other, far):
            pair = (self.count - 2, self.count - 1)
            if not far:
                for i in pair:
                    self.out_store(jnp.int32(i), 0, size).wait()
                return

            @pl.when(self.y == 0)
            def _():
                for i in pair:
                    self.out_store(jnp.int32(i), 0, size).wait()
                    self.out_store(jnp.int32(i), size, size).wait()

            @pl.when(self.y == 1)
            def _():
                @pl.loop(self.count - self.slots, self.count)
                def _(i):
                    self.far_copy(i).wait_send()

        self.widths(action)


class Small:
    def __init__(self, plan, r):
        self.plan, self.r = plan, r
        self.count = plan.groups * plan.copies
        self.per_row = max(1, self.count // 16)
        self.width = r.small_in.shape[1] // self.per_row

    def piece(self, ref, index):
        row, part = index // self.per_row, lax.rem(index, self.per_row)
        return ref.at[pl.ds(row, 1), pl.ds(pl.multiple_of(part * self.width, 128), self.width)]

    def copy(self, offset, first):
        me, peer, target = peer_of(self.plan, offset)
        if first:
            src, dst = self.piece(self.r.small_in, peer), self.r.small_got.at[me]
        else:
            src, dst = self.r.small_sum, self.piece(self.r.small_out, me)
        n = 0 if first else 1
        return pltpu.make_async_remote_copy(
            src, dst, self.r.send_s.at[n, offset], self.r.recv_s.at[n, offset],
            device_id=target, device_id_type=MESH)

    def every(self, action):
        @pl.loop(1, self.count)
        def _(offset):
            action(offset)

    def start(self):
        self.every(lambda offset: self.copy(offset, True).start())

    def local(self, first):
        me = peer_of(self.plan, 0)[0]
        pair = ((self.piece(self.r.small_in, me), self.r.small_got.at[me]) if first
                else (self.r.small_sum, self.piece(self.r.small_out, me)))
        return pltpu.make_async_copy(*pair, self.r.small_sem.at[0 if first else 1])

    def middle(self):
        self.local(True).start()
        self.every(lambda offset: self.copy(offset, True).wait_recv())
        self.local(True).wait()
        self.r.small_sum[...] = jnp.sum(self.r.small_got[...], axis=0)
        self.local(False).start()
        self.every(lambda offset: self.copy(offset, False).start())

    def finish(self):
        self.local(False).wait()
        self.every(lambda offset: self.copy(offset, False).wait_recv())
        for first in (True, False):
            self.every(lambda offset: self.copy(offset, first).wait_send())


def run_stream(which, s, layout, plan, r):
    groups, inner, length = plan.groups, plan.inner, plan.length
    rows_dev = plan.rows
    tokens = plan.tokens
    w, u = s.width, s.units
    z = lax.axis_index("mp")
    side = lax.axis_index("stream")
    gather = Gather(s, plan, r)
    weights = Weights(s, plan, r)
    outputs = Outputs(s, plan, r)
    reduce = Reduce(which, s, layout, plan, r)
    small = Small(plan, r)

    gather.begin(2)
    own_rows = pl.ds(pl.multiple_of(z * tokens, tokens), tokens)
    enter = [pltpu.make_async_copy(r.hidden.at[own_rows], r.x, r.enter_sem.at[0]),
             pltpu.make_async_copy(r.cotangent.at[own_rows], r.grad_out, r.enter_sem.at[1])]
    for item in enter:
        item.start()
    weights.load_own("k", "v", "q", "cross_out", "up", "down", "attend_out")

    def bias_copy(step, kind):
        ref, full = ((r.cross_bias, r.a_cross_bias), (r.attend_bias, r.a_attend_bias),
                     (r.up_bias, r.a_up_bias))[kind]
        return pltpu.make_async_remote_copy(
            ref, full.at[z], r.send_b.at[kind, step], r.recv_b.at[kind, step],
            device_id={"mp": lax.rem(z + step, groups)}, device_id_type=MESH)

    for kind, (ref, full) in enumerate(((r.cross_bias, r.a_cross_bias),
                                        (r.attend_bias, r.a_attend_bias),
                                        (r.up_bias, r.a_up_bias))):
        for step in range(1, groups):
            bias_copy(step, kind).start()
        full[z] = ref[...]

    r.zero[...] = jnp.zeros_like(r.zero)
    r.acc[:, :TILE] = jnp.zeros((tokens, TILE), wide)
    for test, item in reduce.zeros(s, r.acc):
        pl.when(test)(item.start)

    def swap(source, target, number):
        return pltpu.make_async_remote_copy(
            source, target, r.send_x.at[number], r.recv_x.at[number],
            device_id={"stream": 1 - side}, device_id_type=MESH)

    self_kinds = block_kinds(s.head, s.per_group)
    cross_kinds = block_kinds(128, CO_HEADS // groups)
    self_scale, cross_scale = 1.0 / math.sqrt(s.head), 1.0 / math.sqrt(128)

    def in_block(index):
        return pl.ds(pl.multiple_of(index * w, TILE), w)

    def project(part, source, target, bias_ref, line):
        @pl.loop(0, groups)
        def _(g):
            cols = lane(g * inner, inner)
            value = dot(source[:, :w], r.w_in[in_block(g * 3 + part), :])
            if line is not None:
                value = value + bias_ref[g, line : line + 1].astype(wide)
            target[:, cols] = value.astype(low)

    def vector(ref, line, cols=slice(0, w)):
        return ref[line : line + 1, cols].astype(wide)

    def scaled(normal, line, cols):
        return normal[:, cols] * vector(r.gains, line, cols) + vector(r.shifts, line, cols)

    def leave(source, size, weight, residual, line):
        @pl.loop(0, s.parts)
        def _(j):
            cols = lane(j * TILE)
            at = pl.ds(pl.multiple_of(j * size, TILE), size)
            r.acc[:, cols] = (dot(source[:, :size], weight[at, :]) + residual(cols)
                              + vector(r.out_bias, line, cols))

    strip = 64

    def strips(action):
        @pl.loop(0, tokens // strip)
        def _(k):
            action(pl.ds(pl.multiple_of(k * strip, strip), strip))

    def norm(normal, inverse, line, low_out):
        def action(at):
            summed = r.acc[at, :w]
            mean = jnp.sum(summed, axis=-1, keepdims=True) * (1.0 / w)
            centred = summed - mean
            scale = lax.rsqrt(
                jnp.sum(centred * centred, axis=-1, keepdims=True) * (1.0 / w) + norm_eps)
            normal[at, :w] = centred * scale
            inverse[at, :] = scale
            low_out[at, :w] = (
                centred * scale * vector(r.gains, line) + vector(r.shifts, line)).astype(low)

        strips(action)

    def cross_part(begin, end):
        @pl.loop(begin, end)
        def _(g):
            attend_forward(g, cross_kinds, cross_scale, length, rows_dev, r.q, r.pair_k, r.pair_v,
                           r.cross_allowed, r.cross_prob, r.context)

    def feed_part(begin, end):
        @pl.loop(begin, end)
        def _(g):
            for j in range(u // TILE):
                cols = lane(g * u + j * TILE)
                value = (dot(r.h1[:, :w], r.w_up[in_block(g * (u // TILE) + j), :])
                         + r.a_up_bias[g, 0:1, j * TILE : (j + 1) * TILE].astype(wide))
                bell = 0.5 * (1.0 + lax.erf(value * math.sqrt(0.5)))
                r.active[:, cols] = (value * bell).astype(low)
                r.slope[:, cols] = bell + value * (
                    jnp.exp(-0.5 * value * value) * (1.0 / math.sqrt(2.0 * math.pi)))

    def do_key():
        gather.settled(weights, "k")
        for item in enter:
            item.wait()
        weights.wait("k")
        project(1, r.x, r.k, None, None)
        swap(r.k, r.pair_k, 0).start()

    def do_value():
        gather.settled(weights, "v")
        for kind in range(3):
            for step in range(1, groups):
                bias_copy(step, kind).wait()
        weights.wait("v")
        project(2, r.x, r.v, r.a_cross_bias, 1)
        swap(r.v, r.pair_v, 1).start()

    def do_query():
        gather.settled(weights, "q")
        weights.wait("q")
        project(0, r.x, r.q, r.a_cross_bias, 0)
        weights.load_own("attend_in")

    def do_cross_first():
        gather.settled(weights, "cross_out")
        swap(r.k, r.pair_k, 0).wait()
        swap(r.v, r.pair_v, 1).wait()
        cross_part(0, groups // 2)

    def do_cross_second():
        cross_part(groups // 2, groups)
        gather.settled(weights, "up")

    def do_first_norm():
        for test, item in reduce.zeros(s, r.acc):
            pl.when(test)(item.wait)
        weights.wait("cross_out")
        leave(r.context, groups * inner, r.w_cross_out, lambda cols: r.x[:, cols].astype(wide), 0)
        norm(r.n1, r.r1, 0, r.h1)

    def do_feed_first():
        weights.wait("up")
        feed_part(0, groups // 2)
        gather.settled(weights, "down")

    def do_feed_second():
        feed_part(groups // 2, groups)

    work = dict(zip(plan.forward[which], (
        do_key, do_value, do_query, do_cross_first, do_cross_second, do_first_norm,
        do_feed_first, do_feed_second)))
    for i in range(gather.waves() + 1):
        gather.wave(i, 2)
        if i in work:
            work[i]()
    weights.wait("down")
    leave(r.active, groups * u, r.w_down, lambda cols: scaled(r.n1, 0, cols), 1)
    norm(r.n2, r.r2, 1, r.h2)
    gather.settled(weights, "attend_in", "attend_out")
    weights.wait("attend_in")
    project(0, r.h2, r.q2, r.a_attend_bias, 0)
    project(1, r.h2, r.k2, None, None)
    project(2, r.h2, r.v2, r.a_attend_bias, 1)

    @pl.loop(0, groups)
    def _(g):
        attend_forward(g, self_kinds, self_scale, length, rows_dev, r.q2, r.k2, r.v2,
                       r.self_allowed, r.self_prob, r.context2)

    weights.wait("attend_out")
    leave(r.context2, groups * inner, r.w_attend_out, lambda cols: scaled(r.n2, 1, cols), 2)
    norm(r.n3, r.r3, 2, r.layer_rows)
    outputs.begin(0)
    for item in outputs.local(0):
        item.start()
    for p in range(len(gather.pieces)):
        gather.drained(p)

    def store(row, g):
        return pltpu.make_async_copy(
            r.staged.at[g, :, pl.ds(0, w)],
            r.grads.at[g, pl.ds(pl.multiple_of(row, TILE), TILE), pl.ds(0, w)],
            r.store_sem.at[g])

    def weight_grads(left, right, row, size):
        def step(k):
            @pl.loop(0, groups)
            def _(g):
                r.staged[g, :, :w] = dot_tn(left(lane(g * size + k * TILE)), right[:, :w]).astype(low)
                store(row + k * TILE, g).start()

        return step

    def flush():
        pl.loop(0, groups)(lambda g: store(0, g).wait())

    def back_norm(source, normal, inverse, line):
        def action(at):
            incoming = source[at, :w].astype(wide)
            r.small_in[3 + line : 4 + line, :w] += down_sum(incoming * normal[at, :w])
            r.small_in[6 + line : 7 + line, :w] += down_sum(incoming)
            out = norm_back(normal[at, :w], inverse[at, :], vector(r.gains, line), incoming, w)
            r.acc[at, :w] = out
            r.low_grad[at, :w] = out.astype(low)
            r.small_in[line : line + 1, :w] += down_sum(out.astype(low).astype(wide))

        strips(action)

    def leave_back(weight, size, row, count):
        total = None
        for j in range(s.parts):
            at = pl.ds(pl.multiple_of(j * size + row, TILE), count)
            part = dot_nt(r.low_grad[:, j * TILE : (j + 1) * TILE], weight[at, :])
            total = part if total is None else total + part
        return total

    def enter_back(d, weight, blocks):
        def step(g):
            total = r.acc[:, :w]
            for b, (ref, start) in enumerate(d(g)):
                total = total + dot_nt(ref[:, lane(start)], weight[in_block(g * blocks + b), :])
            r.acc[:, :w] = total

        return step

    def context_back(weight):
        def step(g):
            r.grad_context[:, lane(g * inner, inner)] = leave_back(
                weight, groups * inner, g * inner, inner).astype(low)

        return step

    def self_step(g):
        attend_backward(g, self_kinds, self_scale, length, rows_dev, r.q2, r.k2, r.v2,
                        r.self_prob, r.grad_context, r.d.at[0], r.d.at[1], r.d.at[2])

    def cross_step(g):
        attend_backward(g, cross_kinds, cross_scale, length, rows_dev, r.q, r.pair_k, r.pair_v,
                        r.cross_prob, r.grad_context, r.d.at[0], r.d.at[1], r.d.at[2])

    def second_norm(_):
        r.small_in[12:13, :] = down_sum(r.d[0].astype(wide))
        r.small_in[13:14, :] = down_sum(r.d[2].astype(wide))
        weights.load_own("q", "k", "v")
        weights.load_rest("q", "k", "v")
        back_norm(r.acc, r.n2, r.r2, 1)

    def slope_step(g):
        for j in range(u // TILE):
            cols = lane(g * u + j * TILE)
            value = leave_back(r.w_down, groups * u, g * u + j * TILE, TILE)
            r.dz[:, cols] = (value * r.slope[:, cols]).astype(low)

    def first_norm(_):
        back_norm(r.acc, r.n1, r.r1, 0)
        units, width = plan.units, r.small_in.shape[1]
        for g in range(groups):
            for j in range(u // TILE):
                start = g * units + j * TILE
                r.small_in[9 + start // width : 10 + start // width,
                           start % width : start % width + TILE] = down_sum(
                    r.dz[:, g * u + j * TILE : g * u + (j + 1) * TILE].astype(wide))

    def pair_send(_):
        r.small_in[14:15, :] = down_sum(r.d[0].astype(wide))
        weights.wait("q", "k", "v")
        swap(r.d.at[1], r.back.at[0], 2).start()
        swap(r.d.at[2], r.back.at[1], 3).start()

    def pair_take(_):
        swap(r.d.at[1], r.back.at[0], 2).wait()
        swap(r.d.at[2], r.back.at[1], 3).wait()
        r.small_in[15:16, :] = down_sum(r.back[1].astype(wide))
        small.start()

    def hidden_store(_):
        r.hidden_rows[:, :w] = r.acc[:, :w].astype(low)
        for item in outputs.local(1):
            item.start()

    def attend_grads(k):
        weight_grads(lambda cols: r.d[k, :, cols], r.h2, layout.attend_in + k * inner, inner)(0)

    def cross_grads(k):
        weight_grads(lambda cols: r.back[k, :, cols], r.x,
                     layout.cross_in + (1 + k) * inner, inner)(0)

    def of(ref):
        return lambda cols: ref[:, cols]

    r.small_in[...] = jnp.zeros_like(r.small_in)
    back_norm(r.grad_out, r.n3, r.r3, 2)
    pl.loop(0, groups)(context_back(r.w_attend_out))
    weight_grads(of(r.context2), r.low_grad, layout.attend_out, inner)(0)
    nb = u // TILE
    take = plan.when[which]
    schedule = (
        (0, 4, 2, False, self_step),
        (2, 3, 1, True, attend_grads),
        (2, 4, 2, False, enter_back(lambda g: [(d, g * inner) for d in (r.d.at[0], r.d.at[1], r.d.at[2])],
                                    r.w_in, 3)),
        (4, 1, 1, False, second_norm),
        (5, 4, 2, False, slope_step),
        (5, nb, 1, True, weight_grads(of(r.active), r.low_grad, layout.down, u)),
        (5 + nb, nb, 1, True, weight_grads(of(r.dz), r.h1, layout.up, u)),
        (7, 4, 2, False, enter_back(lambda g: [(r.dz, g * u + b * TILE) for b in range(nb)],
                                    r.w_up, nb)),
        (9, 1, 1, False, first_norm),
        (10, 4, 2, False, context_back(r.w_cross_out)),
        (12, 4, 2, False, cross_step),
        (14, 1, 1, False, pair_send),
        (11, 1, 1, True, weight_grads(of(r.context), r.low_grad, layout.cross_out, inner)),
        (15, 1, 1, True, weight_grads(of(r.d.at[0]), r.x, layout.cross_in, inner)),
        (take, 1, 1, False, pair_take),
        (take, 2, 1, True, cross_grads),
        (take + 2, 4, 2, False, enter_back(
            lambda g: [(d, g * inner) for d in (r.d.at[0], r.back.at[0], r.back.at[1])], r.w_in, 3)),
        (take + 4, 1, 1, False, hidden_store),
        (take + 5, 1, 1, False, lambda _: small.middle()),
    )
    storing = sorted({start + n for start, steps, per, keeps, _ in schedule if keeps
                      for n in range(steps)})
    assert len(storing) == sum(steps for _, steps, _, keeps, _ in schedule if keeps)
    hidden_at = take + 5

    @pl.loop(0, max(reduce.iterations(), hidden_at + plan.cuts + groups))
    def _(j):
        flushes = j == 0
        for n in storing:
            flushes = jnp.logical_or(flushes, j == n + 1)
        pl.when(flushes)(flush)
        for start, steps, per, _, step in schedule:
            @pl.when(jnp.logical_and(j >= start, j < start + steps // per))
            def _():
                if per == 1:
                    step(j - start)
                else:
                    pl.loop(0, per)(lambda n: step((j - start) * per + n))
        reduce.iteration(j)
        outputs.step(0, j, True)
        outputs.step(1, j - hidden_at)

    reduce.drained()
    outputs.drained()
    small.finish()


def shards(
    hidden,
    cotangent,
    segments,
    cross_in,
    cross_bias,
    cross_out,
    up_weight,
    up_bias,
    down_weight,
    attend_in,
    attend_bias,
    attend_out,
    out_bias,
    norm_gains,
    norm_shifts,
):
    groups = lax.axis_size("mp")
    copies = lax.axis_size("dp")
    stride = copies // 4
    side = lax.axis_index("stream")
    member = lax.axis_index("mp")
    copy = lax.axis_index("dp")
    inner = cross_in.shape[3]
    padded = hidden.shape[2]
    units = up_weight.shape[2]
    length = segments.shape[2]
    text = Setting(TEXT_WIDTH, TEXT_HEADS, TEXT_FF, groups)
    image = Setting(IMAGE_WIDTH, IMAGE_HEADS, IMAGE_FF, groups)
    settings = (text, image)
    layout = Layout(inner, units)
    rows_max = layout.total
    rows_dev = segments.shape[1] // groups
    tokens = hidden.shape[1] // groups
    co = groups * inner

    def shape(dims, kind=low):
        return jax.ShapeDtypeStruct(dims, kind)

    seg = lax.dynamic_slice_in_dim(segments, member * rows_dev, rows_dev, 1)
    seg_own = lax.dynamic_index_in_dim(seg, side, 0, keepdims=False)
    seg_other = lax.dynamic_index_in_dim(seg, 1 - side, 0, keepdims=False)
    cross_allowed = (seg_other[:, :, None] == seg_own[:, None, :]).astype(wide)
    self_allowed = (seg_own[:, :, None] == seg_own[:, None, :]).astype(wide)

    dma = pltpu.SemaphoreType.DMA

    def real(*dims):
        return pltpu.VMEM(dims, wide)

    def short(*dims):
        return pltpu.VMEM(dims, low)

    chunk, slots, cuts, ring = 64, 20, 8, 4
    widest = max(s.units for s in settings) * groups
    up_rows = max(groups * s.units * s.width for s in settings) // TILE
    heads = max(groups * s.per_group for s in settings)
    pieces, hops = 8 + 2 * max(s.units for s in settings) // TILE, groups - 1
    peers = groups * copies
    small_width = padded // max(1, peers // 16)
    scratch = Scratch(
        w_in=short(groups * 3 * padded, inner),
        w_cross_out=short(padded // TILE * co, TILE),
        w_attend_out=short(padded // TILE * co, TILE),
        w_up=short(up_rows, TILE),
        w_down=short(up_rows, TILE),
        x=short(tokens, padded),
        grad_out=short(tokens, padded),
        q=short(tokens, co),
        k=short(tokens, co),
        v=short(tokens, co),
        pair_k=short(tokens, co),
        pair_v=short(tokens, co),
        back=short(2, tokens, co),
        cross_prob=real(CO_HEADS * rows_dev, length, length),
        self_prob=real(heads * rows_dev, length, length),
        context=short(tokens, co),
        context2=short(tokens, co),
        acc=real(tokens, padded),
        n1=real(tokens, padded),
        n2=real(tokens, padded),
        n3=real(tokens, padded),
        r1=real(tokens, 1),
        r2=real(tokens, 1),
        r3=real(tokens, 1),
        h1=short(tokens, padded),
        h2=short(tokens, padded),
        slope=real(tokens, widest),
        active=short(tokens, widest),
        dz=short(tokens, widest),
        q2=short(tokens, co),
        k2=short(tokens, co),
        v2=short(tokens, co),
        d=short(3, tokens, co),
        low_grad=short(tokens, padded),
        grad_context=short(tokens, co),
        layer_rows=short(tokens, padded),
        hidden_rows=short(tokens, padded),
        zero=short(tokens, IMAGE_WIDTH - TEXT_WIDTH),
        staged=short(ring, TILE, padded),
        from_core=short(slots, 2, groups, chunk, TILE),
        from_y=short(slots, groups, chunk, TILE),
        from_z=short(slots, 2, groups, chunk, TILE),
        far=short(2, slots, chunk, 128),
        own=short(4, 2, groups, chunk, TILE),
        staged_out=real(2, chunk, TILE),
        small_in=real(16, padded),
        small_got=real(peers, 1, small_width),
        small_sum=real(1, small_width),
        small_sem=dma((2,)),
        a_cross_bias=short(groups, 2, inner),
        a_attend_bias=short(groups, 2, inner),
        a_up_bias=short(groups, 1, units),
        send_gz=dma((pieces, 2, hops)),
        recv_gz=dma((pieces, 2, hops)),
        send_gy=dma((pieces, 2, hops)),
        recv_gy=dma((pieces, 2, hops)),
        send_gc=dma((pieces, 2)),
        recv_gc=dma((pieces, 2)),
        weight_sem=dma((pieces, groups, 4)),
        enter_sem=dma((2,)),
        send_b=dma((3, groups)),
        recv_b=dma((3, groups)),
        send_x=dma((4,)),
        recv_x=dma((4,)),
        store_sem=dma((ring,)),
        send_c=dma((slots, 2)),
        recv_c=dma((slots, 2)),
        send_y=dma((slots,)),
        recv_y=dma((slots,)),
        send_z=dma((slots, 2, groups)),
        recv_z=dma((slots, 2, groups)),
        send_f=dma((slots,)),
        recv_f=dma((slots,)),
        own_sem=dma((4, 2)),
        out_sem=dma((2, 2)),
        send_a=dma((2, cuts, 2, hops)),
        recv_a=dma((2, cuts, 2, hops)),
        local_sem=dma((2, groups + 1)),
        send_s=dma((2, peers)),
        recv_s=dma((2, peers)),
        free=pltpu.SemaphoreType.REGULAR((5,)),
        zero_sem=dma((4 + rows_max // TILE,)),
    )
    plan = Plan(
        groups=groups, copies=copies, inner=inner, length=length, rows=rows_dev,
        tokens=tokens, units=units, chunk=chunk, slots=slots, cuts=cuts,
        ring=ring, lags=(3, 8, 2, 2),
        when=(26, 24),
        forward=((4, 5, 6, 10, 11, 12, 13, 14), (4, 5, 6, 8, 9, 10, 11, 12)),
    )
    weights = (
        jnp.swapaxes(cross_in[0], 0, 1),
        cross_out[0],
        up_weight[0],
        down_weight[0],
        jnp.swapaxes(attend_in[0], 0, 1),
        attend_out[0],
    )
    line = shape((groups, tokens, padded))
    out = pl.pallas_call(
        partial(layer_kernel, settings, layout, plan),
        out_shape=(
            line, line, shape((rows_max, TILE), wide), shape((16, padded), wide),
        ) + tuple(shape((groups,) + w.shape) for w in weights)
        + (shape((groups, rows_max, padded)),),
        in_specs=[ANY] * 8 + [VMEM] * 8,
        out_specs=(ANY,) * 3 + (VMEM,) + (ANY,) * 7,
        scratch_shapes=list(scratch),
        compiler_params=pltpu.CompilerParams(
            collective_id=0, has_side_effects=True, vmem_limit_bytes=VMEM_LIMIT),
        name="layer",
    )(*weights, hidden[0], cotangent[0], cross_bias[0], attend_bias[0], up_bias,
      out_bias[0], norm_gains[0], norm_shifts[0],
      cross_allowed.reshape(tokens, length), self_allowed.reshape(tokens, length))
    layer_out, hidden_grad, reduced, small = out[:4]

    if stride > 1:
        teams = [[q * stride + b for b in range(stride)] for q in range(4)]
        reduced = lax.psum_scatter(
            reduced.astype(low), "dp", scatter_dimension=1, axis_index_groups=teams, tiled=True
        ).astype(wide)
    columns = padded // copies
    part = inner // copies
    vector_grads = lax.dynamic_slice_in_dim(small[:9], copy * columns, columns, 1)
    up_bias_grad = lax.dynamic_slice_in_dim(
        small[9:12].reshape(groups * units), (member * copies + copy) * (units // copies),
        units // copies, 0)
    pair_grads = lax.dynamic_slice_in_dim(
        small[12:16], (member * copies + copy) * part, part, 1)

    def turned(start):
        return reduced[start : start + 3 * inner].reshape(3, inner, columns).transpose(2, 0, 1)

    g_cross_in, g_attend_in = turned(layout.cross_in), turned(layout.attend_in)
    g_cross_out = reduced[layout.cross_out : layout.cross_out + inner]
    g_attend_out = reduced[layout.attend_out : layout.attend_out + inner]
    g_up = reduced[layout.up : layout.up + units].T
    g_down = reduced[layout.down : layout.down + units]
    return (
        layer_out.reshape(1, groups * tokens, padded),
        hidden_grad.reshape(1, groups * tokens, padded),
        g_cross_in[None],
        pair_grads[None, 2:4],
        g_cross_out[None],
        g_up[None],
        up_bias_grad[None],
        g_down[None],
        g_attend_in[None],
        pair_grads[None, 0:2],
        g_attend_out[None],
        vector_grads[None, 0:3],
        vector_grads[None, 3:6],
        vector_grads[None, 6:9],
    )


def solution(mesh):
    placed = (
        P("stream", "dp", None),
        P("stream", "dp", None),
        P(None, "dp", None),
        P("stream", None, None, "mp"),
        P("stream", None, "mp"),
        P("stream", "mp", None),
        P("stream", None, "mp"),
        P("stream", "mp"),
        P("stream", "mp", None),
        P("stream", None, None, "mp"),
        P("stream", None, "mp"),
        P("stream", "mp", None),
        P("stream", None, None),
        P("stream", None, None),
        P("stream", None, None),
    )
    return jax.shard_map(
        shards,
        mesh=mesh,
        in_specs=placed,
        out_specs=(
            P("stream", "dp", None),
            P("stream", "dp", None),
            P("stream", "dp", None, "mp"),
            P("stream", None, ("mp", "dp")),
            P("stream", "mp", "dp"),
            P("stream", "dp", "mp"),
            P("stream", ("mp", "dp")),
            P("stream", "mp", "dp"),
            P("stream", "dp", None, "mp"),
            P("stream", None, ("mp", "dp")),
            P("stream", "mp", "dp"),
            P("stream", None, "dp"),
            P("stream", None, "dp"),
            P("stream", None, "dp"),
        ),
        check_vma=False,
    )
```

```python
import math
from functools import partial
from typing import Any, NamedTuple

import jax
import jax.numpy as jnp
from jax import lax
from jax.experimental import pallas as pl
from jax.experimental.pallas import tpu as pltpu
from jax.sharding import PartitionSpec as P

TEXT_WIDTH = 768
TEXT_HEADS = 12
TEXT_FF = 3072
IMAGE_WIDTH = 1024
IMAGE_HEADS = 8
IMAGE_FF = 1024
CO_HEADS = 8

norm_eps = 1e-12
masked_score = -1000000000.0
low = jnp.bfloat16
wide = jnp.float32
ANY = pl.BlockSpec(memory_space=pl.ANY)
VMEM = pl.BlockSpec(memory_space=pltpu.VMEM)
HBM = pl.BlockSpec(memory_space=pltpu.HBM)
MESH = pl.DeviceIdType.MESH
VMEM_LIMIT = 65400 * 1024
TILE = 256
PACE = 3


def dot(left, right):
    return jnp.dot(left, right, preferred_element_type=wide)


def dot_nt(left, right):
    return lax.dot_general(left, right, (((1,), (1,)), ((), ())), preferred_element_type=wide)


def dot_tn(left, right):
    return lax.dot_general(left, right, (((0,), (0,)), ((), ())), preferred_element_type=wide)


class Setting:
    def __init__(self, width, count, units, groups):
        self.width = width
        self.head = width // count
        self.units = units // groups
        self.lanes = width // groups
        self.parts = width // TILE
        self.per_group = count // groups


class Layout:
    def __init__(self, inner, units):
        self.units = units
        self.attend_out = 0
        self.attend_in = inner
        self.down = 4 * inner
        self.up = 4 * inner + units
        self.cross_out = 4 * inner + 2 * units
        self.cross_in = 5 * inner + 2 * units
        self.total = 8 * inner + 2 * units


def lane(start, size=TILE):
    return pl.ds(pl.multiple_of(start, 128), size)


def norm_back(normal, inverse, gain, incoming, w):
    scaled = incoming * gain
    first = jnp.sum(scaled, axis=-1, keepdims=True) * (1.0 / w)
    second = jnp.sum(scaled * normal, axis=-1, keepdims=True) * (1.0 / w)
    return inverse * (scaled - first - normal * second)


def down_sum(value):
    return jnp.sum(value, axis=0, keepdims=True)


def softmax_t(scores, allowed, scale):
    scores = jnp.where(allowed, scores, masked_score / scale)
    top = jnp.max(scores, axis=0, keepdims=True)
    exponent = jnp.exp2((scores - top) * (scale * math.log2(math.e)))
    return exponent * (1.0 / jnp.sum(exponent, axis=0, keepdims=True))


def score_grad_t(p, grad):
    return (p * (grad - jnp.sum(grad * p, axis=0, keepdims=True))).astype(low)


def halves(value):
    index = lax.broadcasted_iota(jnp.int32, value.shape, 1)
    zero = jnp.zeros_like(value)
    return jnp.concatenate(
        [jnp.where(index < 64, value, zero), jnp.where(index >= 64, value, zero)], axis=0)


def lower(value):
    index = lax.broadcasted_iota(jnp.int32, value.shape, 1)
    return jnp.where(index < 64, value, jnp.zeros_like(value))


def side_by_side(parts, axis=1):
    return parts[0] if len(parts) == 1 else jnp.concatenate(parts, axis=axis)


def split(value, count):
    size = value.shape[1] // count
    return [value[:, n * size : (n + 1) * size] for n in range(count)]


def block_kinds(head, heads):
    if head == 128:
        return [0] * heads
    return [2] * (heads // 2) + [1] * (heads % 2)


def spread_heads(kind, value):
    return halves(value) if kind == 2 else lower(value) if kind == 1 else value


def attend_forward(group, kinds, scale, length, rows, q, k, v, allowed, prob, context):
    heads = sum(max(kind, 1) for kind in kinds)
    base = group * len(kinds) * 128
    ats = [slice(r * length, (r + 1) * length) for r in range(rows)]
    step = 0
    for b, kind in enumerate(kinds):
        cols = lane(base + b * 128, 128)
        count = max(kind, 1)
        groups = [ats]
        for members in groups:
            scores = side_by_side(
                [dot_nt(k[at, cols], spread_heads(kind, q[at, cols])) for at in members])
            masks = side_by_side([allowed[at, :] for at in members for _ in range(count)])
            p = softmax_t(scores, masks > 0, scale)
            low_p = p.astype(low)
            tiles = split(p, count * len(members))
            low_tiles = split(low_p, count * len(members))
            out = [
                dot_tn(side_by_side(low_tiles[n * count : (n + 1) * count], 0),
                       spread_heads(kind, v[at, cols]))
                for n, at in enumerate(members)]
            for n, at in enumerate(members):
                r = ats.index(at)
                context[at, cols] = out[n].astype(low)
                for c in range(count):
                    prob[group * heads * rows + r * heads + step + c] = tiles[n * count + c]
        step += count


def attend_backward(group, kinds, scale, length, rows, q, k, v, prob, grad, dq, dk, dv):
    heads = sum(max(kind, 1) for kind in kinds)
    base = group * len(kinds) * 128
    ats = [slice(r * length, (r + 1) * length) for r in range(rows)]
    step = 0
    for b, kind in enumerate(kinds):
        cols = lane(base + b * 128, 128)
        count = max(kind, 1)
        groups = [ats]
        for members in groups:
            dcs = [spread_heads(kind, grad[at, cols]) for at in members]
            qs = [spread_heads(kind, q[at, cols]) for at in members]
            gp = side_by_side([dot_nt(v[at, cols], dc) for at, dc in zip(members, dcs)])
            p = side_by_side([
                prob[group * heads * rows + ats.index(at) * heads + step + c]
                for at in members for c in range(count)])
            low_p = split(p.astype(low), len(members))
            ds = split(score_grad_t(p, gp), len(members))
            grad_v = [dot(a, dc) for a, dc in zip(low_p, dcs)]
            grad_k = [dot(a, two) * scale for a, two in zip(ds, qs)]
            grad_q = [dot_tn(a, k[at, cols]) * scale for a, at in zip(ds, members)]
            for n, at in enumerate(members):
                value = grad_q[n]
                if kind:
                    index = lax.broadcasted_iota(jnp.int32, (length, 128), 1)
                    other = value[length:] if kind == 2 else jnp.zeros((length, 128), wide)
                    value = jnp.where(index < 64, value[:length], other)
                dq[at, cols] = value.astype(low)
                dk[at, cols] = grad_k[n].astype(low)
                dv[at, cols] = grad_v[n].astype(low)
        step += count
class Refs:
    def __init__(self, *groups):
        for group in groups:
            self.__dict__.update(group._asdict())


class Inputs(NamedTuple):
    cross_in: Any
    cross_out: Any
    up: Any
    down: Any
    attend_in: Any
    attend_out: Any
    hidden: Any
    cotangent: Any
    cross_bias: Any
    attend_bias: Any
    up_bias: Any
    out_bias: Any
    gains: Any
    shifts: Any
    cross_allowed: Any
    self_allowed: Any


class Results(NamedTuple):
    layer_full: Any
    hidden_full: Any
    reduced: Any
    small_out: Any
    f_cross_in: Any
    f_cross_out: Any
    f_up: Any
    f_down: Any
    f_attend_in: Any
    f_attend_out: Any
    grads: Any


class Scratch(NamedTuple):
    w_in: Any
    w_cross_out: Any
    w_attend_out: Any
    w_up: Any
    w_down: Any
    x: Any
    grad_out: Any
    q: Any
    k: Any
    v: Any
    pair_k: Any
    pair_v: Any
    back: Any
    cross_prob: Any
    self_prob: Any
    context: Any
    context2: Any
    acc: Any
    n1: Any
    n2: Any
    n3: Any
    r1: Any
    r2: Any
    r3: Any
    h1: Any
    h2: Any
    slope: Any
    active: Any
    dz: Any
    q2: Any
    k2: Any
    v2: Any
    d: Any
    low_grad: Any
    grad_context: Any
    layer_rows: Any
    hidden_rows: Any
    zero: Any
    staged: Any
    from_core: Any
    from_y: Any
    from_z: Any
    far: Any
    own: Any
    staged_out: Any
    small_in: Any
    small_got: Any
    small_sum: Any
    small_sem: Any
    a_cross_bias: Any
    a_attend_bias: Any
    a_up_bias: Any
    send_gz: Any
    recv_gz: Any
    send_gy: Any
    recv_gy: Any
    send_gc: Any
    recv_gc: Any
    weight_sem: Any
    enter_sem: Any
    send_b: Any
    recv_b: Any
    send_x: Any
    recv_x: Any
    store_sem: Any
    send_c: Any
    recv_c: Any
    send_y: Any
    recv_y: Any
    send_z: Any
    recv_z: Any
    send_f: Any
    recv_f: Any
    own_sem: Any
    out_sem: Any
    send_a: Any
    recv_a: Any
    local_sem: Any
    send_s: Any
    recv_s: Any
    free: Any
    zero_sem: Any


class Plan(NamedTuple):
    groups: Any
    copies: Any
    inner: Any
    length: Any
    rows: Any
    tokens: Any
    units: Any
    chunk: Any
    slots: Any
    cuts: Any
    ring: Any
    lags: Any
    when: Any
    forward: Any


def layer_kernel(settings, layout, plan, *refs):
    first, second = len(Inputs._fields), len(Inputs._fields) + len(Results._fields)
    r = Refs(Inputs(*refs[:first]), Results(*refs[first:second]), Scratch(*refs[second:]))
    side = lax.axis_index("stream")
    greet(plan, r)
    for which, s in enumerate(settings):
        pl.when(side == which)(partial(run_stream, which, s, layout, plan, r))


def peer_of(plan, offset):
    groups, copies = plan.groups, plan.copies
    me = lax.axis_index("mp") * copies + lax.axis_index("dp")
    index = lax.rem(me + offset, groups * copies)
    return me, index, {"mp": index // copies, "dp": lax.rem(index, copies)}


def greet(plan, r):
    barrier = pltpu.get_barrier_semaphore()
    count = plan.groups * plan.copies

    @pl.loop(1, count)
    def _(offset):
        pl.semaphore_signal(barrier, inc=1, device_id=peer_of(plan, offset)[2], device_id_type=MESH)

    pl.semaphore_signal(barrier, inc=1, device_id={"stream": 1 - lax.axis_index("stream")},
                        device_id_type=MESH)
    pl.semaphore_wait(barrier, count)


class Piece(NamedTuple):
    own: Any
    gathered: Any
    every: Any
    sized: Any
    whole: Any
    ref: Any
    full: Any
    held: Any
    place: Any


def pieces_of(s, plan, r):
    w, u, inner, groups = s.width, s.units, plan.inner, plan.groups
    pieces, named = [], {}

    def add(name, size, ref, full, held, cut, whole, place):
        named.setdefault(name, []).append(len(pieces))
        pieces.append(Piece(
            lambda part: cut(ref, (), part * size, size),
            lambda z, part: cut(full, (z,), part * size, size),
            lambda part: cut(full, (slice(None),), part * size, size),
            lambda n: cut(full, (pl.ds(0, min(n, 2)),), 0, n * size // min(n, 2)), whole, ref, full, held, place))

    def matrix(name, b, ref, full):
        add(name, w // 4, ref, full, r.w_in,
            lambda a, at, start, size: a.at[at + (b, pl.ds(start, size), slice(None))],
            lambda a: [a.at[b, pl.ds(0, w), :]],
            lambda z: [pl.ds(pl.multiple_of((z * 3 + b) * w, TILE), w)])

    def rows(name, j, count, ref, full, held):
        add(name, TILE // 4, ref, full, held,
            lambda a, at, start, size: a.at[at + (pl.ds(j * TILE + start, size), pl.ds(0, w))],
            lambda a: [a.at[pl.ds(j * TILE, TILE), pl.ds(b * TILE, TILE)] for b in range(s.parts)],
            lambda z: [pl.ds(pl.multiple_of((b * groups + z) * count + j * TILE, TILE), TILE)
                       for b in range(s.parts)])

    def columns(name, j, ref, full, held):
        add(name, w // 4, ref, full, held,
            lambda a, at, start, size: a.at[at + (pl.ds(start, size), pl.ds(j * TILE, TILE))],
            lambda a: [a.at[pl.ds(0, w), pl.ds(j * TILE, TILE)]],
            lambda z: [pl.ds(pl.multiple_of((z * (u // TILE) + j) * w, TILE), w)])

    matrix("k", 1, r.cross_in, r.f_cross_in)
    matrix("v", 2, r.cross_in, r.f_cross_in)
    matrix("q", 0, r.cross_in, r.f_cross_in)
    rows("cross_out", 0, inner, r.cross_out, r.f_cross_out, r.w_cross_out)
    for j in range(u // TILE):
        columns("up", j, r.up, r.f_up, r.w_up)
    for j in range(u // TILE):
        rows("down", j, u, r.down, r.f_down, r.w_down)
    for b in range(3):
        matrix("attend_in", b, r.attend_in, r.f_attend_in)
    rows("attend_out", 0, inner, r.attend_out, r.f_attend_out, r.w_attend_out)
    return pieces, named


class Gather:
    def __init__(self, s, plan, r):
        self.groups, self.r = plan.groups, r
        stride, copy = plan.copies // 4, lax.axis_index("dp")
        self.z = lax.axis_index("mp")
        self.quarter = lax.rem(copy // stride, 4)
        base = lax.rem(copy, stride)
        self.to_y = {"dp": (self.quarter ^ 2) * stride + base}
        self.to_c = {"dp": (self.quarter ^ 1) * stride + base}
        self.at_end = jnp.logical_or(self.z == 0, self.z == self.groups - 1)
        self.pieces, self.named = pieces_of(s, plan, r)

    def z_copy(self, p, way, hop):
        step = 1 - 2 * way
        origin = self.z - hop * step
        piece = self.pieces[p]
        dst = piece.gathered(origin, self.quarter)
        src = piece.own(self.quarter) if hop == 0 else dst
        return pltpu.make_async_remote_copy(
            src, dst, self.r.send_gz.at[p], self.r.recv_gz.at[p, origin],
            device_id={"mp": self.z + step}, device_id_type=MESH)

    def block(self, p, way, hop, whose):
        return self.pieces[p].gathered(self.z - (hop + 1) * (1 - 2 * way), whose)

    def z_arrival(self, p, way, hop):
        block = self.block(p, way, hop, self.quarter)
        origin = self.z - (hop + 1) * (1 - 2 * way)
        return pltpu.make_async_remote_copy(
            block, block, self.r.send_gz.at[p], self.r.recv_gz.at[p, origin],
            device_id={"mp": self.z - (1 - 2 * way)}, device_id_type=MESH)

    def y_copy(self, p, way, hop):
        block = self.block(p, way, hop, self.quarter)
        return pltpu.make_async_remote_copy(
            block, block, self.r.send_gy.at[p], self.r.recv_gy.at[p],
            device_id=self.to_y, device_id_type=MESH)

    def c_copy(self, p, which):
        block = self.pieces[p].every(self.quarter ^ (2 * which))
        return pltpu.make_async_remote_copy(
            block, block, self.r.send_gc.at[p], self.r.recv_gc.at[p],
            device_id=self.to_c, device_id_type=MESH)

    def total(self, p, n, send, recv, target):
        block = self.pieces[p].sized(n)
        return pltpu.make_async_remote_copy(
            block, block, send.at[p], recv.at[p], device_id=target, device_id_type=MESH)

    def y_all(self, p):
        return self.total(p, self.groups - 1, self.r.send_gy, self.r.recv_gy, self.to_y)

    def c_all(self, p):
        return self.total(p, 2 * self.groups, self.r.send_gc, self.r.recv_gc, self.to_c)

    def sends(self, way, hop):
        last = self.groups - 1
        if way == 0:
            return jnp.logical_and(self.z >= hop, self.z < last)
        return jnp.logical_and(self.z <= last - hop, self.z > 0)

    def arrives(self, way, hop):
        return self.z >= hop + 1 if way == 0 else self.z <= self.groups - 2 - hop

    def each(self, test, action, hops=None):
        for hop in range(self.groups - 1) if hops is None else hops:
            for way in range(2):
                pl.when(test(way, hop))(partial(action, way, hop))

    def own(self, p):
        for way in range(2):
            pl.when(self.sends(way, 0))(lambda: self.z_copy(p, way, 0).start())

    def begin(self, ahead):
        for p in range(ahead):
            self.own(p)
        for p in range(ahead, len(self.pieces)):
            pl.when(self.at_end)(partial(self.own, p))

    def wave(self, i, ahead):
        count, last = len(self.pieces), self.groups - 2
        for hop in range(self.groups - 1):
            if 0 <= i - hop < count:
                self.received(i - hop, hop)
        if 0 <= i - last < count:
            self.c_copy(i - last, 0).start()
        if i + ahead < count:
            pl.when(jnp.logical_not(self.at_end))(partial(self.own, i + ahead))
        if 0 <= i - last - 1 < count:
            self.y_all(i - last - 1).wait_recv()
            self.c_copy(i - last - 1, 1).start()

    def waves(self):
        return len(self.pieces) + self.groups - 1

    def received(self, p, *hops):
        def action(way, hop):
            self.z_arrival(p, way, hop).wait_recv()
            if hop + 1 < self.groups - 1:
                pl.when(self.sends(way, hop + 1))(lambda: self.z_copy(p, way, hop + 1).start())
            self.y_copy(p, way, hop).start()

        self.each(self.arrives, action, hops or None)

    def settled(self, weights, *names):
        for name in names:
            for p in self.named[name]:
                self.c_all(p).wait_recv()

                def action(way, hop):
                    for item in weights.copies(p, self.z - (hop + 1) * (1 - 2 * way), False):
                        item.start()

                self.each(self.arrives, action)

    def drained(self, p):
        for test, n in ((self.at_end, 1), (jnp.logical_not(self.at_end), self.groups + 1)):
            pl.when(test)(lambda: self.total(
                p, n, self.r.send_gz, self.r.recv_gy, self.to_y).wait_send())
        self.y_all(p).wait_send()
        self.c_all(p).wait_send()


class Weights:
    def __init__(self, s, plan, r):
        self.r, self.groups = r, plan.groups
        self.z = lax.axis_index("mp")
        self.pieces, self.named = pieces_of(s, plan, r)

    def copies(self, p, z, own):
        piece = self.pieces[p]
        blocks = piece.whole(piece.ref if own else piece.full.at[z])
        for src, rows in zip(blocks, piece.place(z)):
            yield pltpu.make_async_copy(src, piece.held.at[rows], self.r.weight_sem.at[p])

    def load_own(self, *names):
        for name in names:
            for p in self.named[name]:
                for item in self.copies(p, self.z, True):
                    item.start()

    def load_rest(self, *names):
        for name in names:
            for p in self.named[name]:
                @pl.loop(0, self.groups)
                def _(z):
                    @pl.when(self.z != z)
                    def _():
                        for item in self.copies(p, z, False):
                            item.start()

    def wait(self, *names):
        for name in names:
            for p in self.named[name]:
                piece = self.pieces[p]
                blocks = piece.whole(piece.ref)
                rows = self.groups * len(blocks) * blocks[0].shape[0]
                held = piece.held.at[pl.ds(0, rows)]
                pltpu.make_async_copy(held, held, self.r.weight_sem.at[p]).wait()


class Outputs:
    def __init__(self, s, plan, r):
        self.s, self.r, self.groups, self.cuts = s, r, plan.groups, plan.cuts
        self.z = lax.axis_index("mp")
        self.last = self.groups - 1
        self.rows = plan.tokens // self.cuts
        self.pairs = ((r.layer_rows, r.layer_full), (r.hidden_rows, r.hidden_full))

    def cut(self, ref, k):
        return ref.at[pl.ds(pl.multiple_of(k * self.rows, self.rows), self.rows),
                      pl.ds(0, self.s.width)]

    def copy(self, which, k, way, hop, arrival=False):
        step = 1 - 2 * way
        origin = self.z - (hop + 1 if arrival else hop) * step
        rows, full = self.pairs[which]
        dst = self.cut(full.at[origin], k)
        src = self.cut(rows, k) if hop == 0 and not arrival else dst
        return pltpu.make_async_remote_copy(
            src, dst, self.r.send_a.at[which, way], self.r.recv_a.at[which, k, origin],
            device_id={"mp": self.z + step}, device_id_type=MESH)

    def sends(self, way, hop):
        if way == 0:
            return jnp.logical_and(self.z >= hop, self.z < self.last)
        return jnp.logical_and(self.z <= self.last - hop, self.z > 0)

    def arrives(self, way, hop):
        return self.z >= hop + 1 if way == 0 else self.z <= self.last - 1 - hop

    def begin(self, which):
        @pl.loop(0, self.cuts)
        def _(k):
            for way in range(2):
                pl.when(self.sends(way, 0))(lambda: self.copy(which, k, way, 0).start())

    def step(self, which, k, begun=False):
        for hop in range(1 if begun else 0, self.groups):
            now = k - PACE * hop

            @pl.when(jnp.logical_and(now >= 0, now < self.cuts))
            def _():
                for way in range(2):
                    if hop:
                        pl.when(self.arrives(way, hop - 1))(
                            lambda: self.copy(which, now, way, hop - 1, True).wait_recv())
                    if hop < self.last:
                        pl.when(self.sends(way, hop))(
                            lambda: self.copy(which, now, way, hop).start())

    def local(self, which):
        rows, full = self.pairs[which]
        width = self.s.width
        items = [pltpu.make_async_copy(rows.at[:, pl.ds(0, width)],
                                       full.at[self.z, :, pl.ds(0, width)],
                                       self.r.local_sem.at[which, self.groups])]
        padded = full.shape[2]
        if width < padded:
            items += [pltpu.make_async_copy(
                self.r.zero, full.at[z, :, pl.ds(width, padded - width)],
                self.r.local_sem.at[which, z]) for z in range(self.groups)]
        return items

    def drained(self, which):
        full = self.pairs[which][1]
        for way in range(2):
            count = self.z + 1 if way == 0 else self.groups - self.z
            for n in range(1, self.groups):
                block = full.at[pl.ds(0, n), :, pl.ds(0, self.s.width)]
                pl.when(jnp.logical_and(self.sends(way, 0), count == n))(
                    lambda: pltpu.make_async_remote_copy(
                        block, block, self.r.send_a.at[which, way], self.r.recv_a.at[which, 0, 0],
                        device_id={"mp": self.z + 1 - 2 * way}, device_id_type=MESH).wait_send())
        for item in self.local(which):
            item.wait()


class Reduce:
    def __init__(self, which, s, layout, plan, r):
        self.text = which == 0
        self.r, self.groups, self.chunk = r, plan.groups, plan.chunk
        self.slots, self.lags = plan.slots, plan.lags
        self.inner, self.used = plan.inner, s.lanes // self.chunk
        self.narrow = 4 * self.used
        self.feed = s.units // self.chunk
        self.layout = layout
        self.count = self.narrow + 2 * self.feed + plan.inner // self.chunk * 4
        stride, copy = plan.copies // 4, lax.axis_index("dp")
        quarter = lax.rem(copy // stride, 4)
        base = lax.rem(copy, stride)
        self.z = lax.axis_index("mp")
        self.y, self.core = quarter // 2, lax.rem(quarter, 2)
        self.to_y = {"dp": (quarter ^ 2) * stride + base}
        self.to_c = {"dp": (quarter ^ 1) * stride + base}
        self.last = self.groups - 1

    def widths(self, action):
        if not self.text:
            action(TILE, TILE, False)
        else:
            pl.when(self.core == 0)(partial(action, TILE, 128, False))
            pl.when(self.core == 1)(partial(action, 128, TILE, True))

    def first_lane(self, core, y):
        if self.text:
            return pl.multiple_of(jnp.where(core == 0, y * 2 * TILE, TILE + y * 128), 128)
        return pl.multiple_of((2 * y + core) * TILE, 128)

    def rows(self, i):
        early = (i // self.used) * self.inner + lax.rem(i, self.used) * self.chunk
        n = i - self.narrow
        late = jnp.where(
            n < self.feed, self.layout.down + n * self.chunk,
            jnp.where(n < 2 * self.feed, self.layout.up + (n - self.feed) * self.chunk,
                      self.layout.cross_out + (n - 2 * self.feed) * self.chunk))
        start = jnp.where(i < self.narrow, early, late)
        return pl.ds(pl.multiple_of(start, self.chunk), self.chunk)

    def slot(self, i):
        return lax.rem(i, self.slots)

    def core_copy(self, i, k, other):
        n = self.slot(i)
        return pltpu.make_async_remote_copy(
            self.r.grads.at[:, self.rows(i), pl.ds(self.first_lane(1 - self.core, k), other)],
            self.r.from_core.at[n, k, :, :, pl.ds(0, other)],
            self.r.send_c.at[n], self.r.recv_c.at[n],
            device_id=self.to_c, device_id_type=MESH)

    def core_both(self, i, size):
        n = self.slot(i)
        block = self.r.from_core.at[n, :, :, :, pl.ds(0, size)]
        return pltpu.make_async_remote_copy(
            block, block, self.r.send_c.at[n], self.r.recv_c.at[n],
            device_id=self.to_c, device_id_type=MESH)

    def own_load(self, i, k, size):
        n = lax.rem(i, 4)
        return pltpu.make_async_copy(
            self.r.grads.at[:, self.rows(i), pl.ds(self.first_lane(self.core, k), size)],
            self.r.own.at[n, k, :, :, pl.ds(0, size)], self.r.own_sem.at[n])

    def own_both(self, i, size):
        n = lax.rem(i, 4)
        block = self.r.own.at[n, :, :, :, pl.ds(0, size)]
        return pltpu.make_async_copy(block, block, self.r.own_sem.at[n])

    def y_copy(self, i, size):
        n = self.slot(i)
        return pltpu.make_async_remote_copy(
            self.r.from_core.at[n, 1 - self.y, :, :, pl.ds(0, size)],
            self.r.from_y.at[n, :, :, pl.ds(0, size)],
            self.r.send_y.at[n], self.r.recv_y.at[n], device_id=self.to_y, device_id_type=MESH)

    def z_copy(self, i, way, t, size, fresh):
        n = self.slot(i)
        place = t + 1 - way
        dst = self.r.from_z.at[n, place, :, pl.ds(0, size)]
        src = self.r.from_core.at[n, self.y, t, :, pl.ds(0, size)] if fresh else dst
        return pltpu.make_async_remote_copy(
            src, dst, self.r.send_z.at[n], self.r.recv_z.at[n, place],
            device_id={"mp": self.z + 1 - 2 * way}, device_id_type=MESH)

    def far_copy(self, i):
        n = self.slot(i)
        return pltpu.make_async_remote_copy(
            self.r.far.at[0, n], self.r.far.at[1, n], self.r.send_f.at[n], self.r.recv_f.at[n],
            device_id=self.to_y, device_id_type=MESH)

    def out_store(self, i, start, size):
        n = lax.rem(i, 2)
        return pltpu.make_async_copy(
            self.r.staged_out.at[n, :, pl.ds(start, size)],
            self.r.reduced.at[self.rows(i), pl.ds(start, size)],
            self.r.out_sem.at[1 if start else 0, n])

    def credit(self, i, sem):
        pl.when(i >= self.slots)(lambda: pl.semaphore_wait(sem, 1))

    def stage_a(self, i):
        self.credit(i, self.r.free.at[0])

        def action(size, other, far):
            for k in range(2):
                self.core_copy(i, k, other).start()
                self.own_load(i, k, size).start()

        self.widths(action)

    def stage_b(self, i):
        n = self.slot(i)

        def action(size, other, far):
            self.core_both(i, size).wait_recv()
            self.own_both(i, size).wait()
            for k in range(2):
                self.r.from_core[n, k, :, :, :size] += self.r.own[lax.rem(i, 4), k, :, :, :size]
            self.credit(i, self.r.free.at[1])
            self.y_copy(i, size).start()

        self.widths(action)

    def z_step(self, hop, i):
        n = self.slot(i)

        def action(size, other, far):
            for way in range(2):
                t = self.z + (1 - 2 * way) * (self.groups - hop)

                @pl.when(t <= self.last if way == 0 else t >= 0)
                def _():
                    first = self.z == (0 if way == 0 else self.last)
                    pl.when(first)(lambda: self.z_copy(i, way, t, size, True).start())

                    @pl.when(jnp.logical_not(first))
                    def _():
                        self.z_copy(i, way, t, size, False).wait_recv()
                        self.r.from_z[n, t + 1 - way, :, :size] += (
                            self.r.from_core[n, self.y, t, :, :size])
                        self.z_copy(i, way, t, size, False).start()

        self.widths(action)

    def stage_c(self, i):
        n = self.slot(i)

        def action(size, other, far):
            self.y_copy(i, size).wait_recv()
            self.r.from_core[n, self.y, :, :, :size] += self.r.from_y[n, :, :, :size]

        self.widths(action)
        pl.when(self.z < self.last)(lambda: self.credit(i, self.r.free.at[2]))
        pl.when(self.z > 0)(lambda: self.credit(i, self.r.free.at[3]))
        self.z_step(1, i)

    def final(self, i):
        n = self.slot(i)

        def action(size, other, far):
            for way in range(2):
                edge = 0 if way == 0 else self.last

                @pl.when(self.z != edge)
                def _():
                    self.z_copy(i, way, self.z, size, False).wait_recv()

                @pl.when(self.z == edge)
                def _():
                    self.r.from_z[n, self.z + 1 - way, :, :size] = jnp.zeros((self.chunk, size), low)

            total = (self.r.from_core[n, self.y, self.z, :, :size].astype(wide)
                     + self.r.from_z[n, self.z + 1, :, :size].astype(wide)
                     + self.r.from_z[n, self.z, :, :size].astype(wide))

            def keep():
                pl.when(i >= 2)(lambda: self.out_store(i - 2, 0, size).wait())
                self.r.staged_out[lax.rem(i, 2), :, :size] = total.astype(low)
                self.out_store(i, 0, size).start()

            if far:
                pl.when(self.y == 0)(keep)

                @pl.when(self.y == 1)
                def _():
                    pl.when(i >= self.slots)(lambda: self.far_copy(i - self.slots).wait_send())
                    self.credit(i, self.r.free.at[4])
                    self.r.far[0, n] = total.astype(low)
                    self.far_copy(i).start()
            else:
                keep()
            self.core_both(i, other).wait_send()
            self.y_copy(i, size).wait_send()
            block = self.r.from_z.at[n, pl.ds(0, self.last), :, pl.ds(0, size)]
            pltpu.make_async_remote_copy(
                block, block, self.r.send_z.at[n], self.r.recv_z.at[n, 0],
                device_id=self.to_y, device_id_type=MESH).wait_send()

        self.widths(action)

        @pl.when(i < self.count - self.slots)
        def _():
            def tell(index, target):
                pl.semaphore_signal(self.r.free.at[index], inc=1, device_id=target,
                                    device_id_type=MESH)

            tell(0, self.to_c)
            tell(1, self.to_y)
            pl.when(self.z > 0)(lambda: tell(2, {"mp": self.z - 1}))
            pl.when(self.z < self.last)(lambda: tell(3, {"mp": self.z + 1}))

    def land(self, i):
        n = self.slot(i)

        def action(size, other, far):
            if not far:
                return

            @pl.when(self.y == 0)
            def _():
                self.far_copy(i).wait_recv()
                pl.when(i >= 2)(lambda: self.out_store(i - 2, size, size).wait())
                self.r.staged_out[lax.rem(i, 2), :, size : 2 * size] = self.r.far[1, n]
                self.out_store(i, size, size).start()

                @pl.when(i < self.count - self.slots)
                def _():
                    pl.semaphore_signal(self.r.free.at[4], inc=1, device_id=self.to_y,
                                        device_id_type=MESH)

        self.widths(action)

    def zeros(self, s, zero):
        blocks = [(4 * self.chunk * n + self.used * self.chunk, self.inner - self.used * self.chunk)
                  for n in range(4)] if self.used * self.chunk < self.inner else []
        for start in (self.layout.down, self.layout.up):
            blocks += [(row, TILE) for row in range(start + s.units, start + self.layout.units, TILE)]
        number = 0
        for always, group in ((True, blocks), (False, [(row, TILE) for row in range(
                0, self.layout.total, TILE)] if self.text else [])):
            test = self.y + self.core == 2
            for row, size in group:
                yield (jnp.logical_not(test) if always and self.text else test if self.text
                       else self.y >= 0, pltpu.make_async_copy(
                    zero.at[pl.ds(0, size), pl.ds(0, TILE)],
                    self.r.reduced.at[pl.ds(row, size)], self.r.zero_sem.at[number]))
                number += 1

    def iteration(self, j):
        lag_b, lag_c, lag_z, lag_f = self.lags

        def at(i, stage):
            pl.when(jnp.logical_and(i >= 0, i < self.count))(lambda: stage(i))

        at(j, self.stage_a)
        at(j - lag_b, self.stage_b)
        at(j - lag_c, self.stage_c)
        for hop in range(2, self.groups):
            at(j - lag_c - lag_z * (hop - 1), partial(self.z_step, hop))
        done = lag_c + lag_z * (self.groups - 1)
        at(j - done, self.final)
        if self.text:
            at(j - done - lag_f, self.land)

    def iterations(self):
        lag_b, lag_c, lag_z, lag_f = self.lags
        return self.count + lag_c + lag_z * (self.groups - 1) + (lag_f if self.text else 0)

    def drained(self):
        def action(size, other, far):
            pair = (self.count - 2, self.count - 1)
            if not far:
                for i in pair:
                    self.out_store(jnp.int32(i), 0, size).wait()
                return

            @pl.when(self.y == 0)
            def _():
                for i in pair:
                    self.out_store(jnp.int32(i), 0, size).wait()
                    self.out_store(jnp.int32(i), size, size).wait()

            @pl.when(self.y == 1)
            def _():
                @pl.loop(self.count - self.slots, self.count)
                def _(i):
                    self.far_copy(i).wait_send()

        self.widths(action)


class Small:
    def __init__(self, plan, r):
        self.plan, self.r = plan, r
        self.count = plan.groups * plan.copies
        self.per_row = max(1, self.count // 16)
        self.width = r.small_in.shape[1] // self.per_row

    def piece(self, ref, index):
        row, part = index // self.per_row, lax.rem(index, self.per_row)
        return ref.at[pl.ds(row, 1), pl.ds(pl.multiple_of(part * self.width, 128), self.width)]

    def copy(self, offset, first):
        me, peer, target = peer_of(self.plan, offset)
        if first:
            src, dst = self.piece(self.r.small_in, peer), self.r.small_got.at[me]
        else:
            src, dst = self.r.small_sum, self.piece(self.r.small_out, me)
        n = 0 if first else 1
        return pltpu.make_async_remote_copy(
            src, dst, self.r.send_s.at[n], self.r.recv_s.at[n],
            device_id=target, device_id_type=MESH)

    def all(self, first):
        n = 0 if first else 1
        block = self.r.small_got.at[pl.ds(0, self.count - 1)]
        return pltpu.make_async_remote_copy(
            block, block, self.r.send_s.at[n], self.r.recv_s.at[n],
            device_id=peer_of(self.plan, 1)[2], device_id_type=MESH)

    def every(self, action):
        @pl.loop(1, self.count)
        def _(offset):
            action(offset)

    def start(self):
        self.every(lambda offset: self.copy(offset, True).start())

    def local(self, first):
        me = peer_of(self.plan, 0)[0]
        pair = ((self.piece(self.r.small_in, me), self.r.small_got.at[me]) if first
                else (self.r.small_sum, self.piece(self.r.small_out, me)))
        return pltpu.make_async_copy(*pair, self.r.small_sem.at[0 if first else 1])

    def middle(self):
        self.local(True).start()
        self.all(True).wait_recv()
        self.local(True).wait()
        self.r.small_sum[...] = jnp.sum(self.r.small_got[...], axis=0)
        self.local(False).start()
        self.every(lambda offset: self.copy(offset, False).start())

    def finish(self):
        self.local(False).wait()
        self.all(False).wait_recv()
        for first in (True, False):
            self.all(first).wait_send()


def run_stream(which, s, layout, plan, r):
    groups, inner, length = plan.groups, plan.inner, plan.length
    rows_dev = plan.rows
    tokens = plan.tokens
    w, u = s.width, s.units
    z = lax.axis_index("mp")
    side = lax.axis_index("stream")
    gather = Gather(s, plan, r)
    weights = Weights(s, plan, r)
    outputs = Outputs(s, plan, r)
    reduce = Reduce(which, s, layout, plan, r)
    small = Small(plan, r)

    gather.begin(2)
    own_rows = pl.ds(pl.multiple_of(z * tokens, tokens), tokens)
    enter = [pltpu.make_async_copy(r.hidden.at[own_rows], r.x, r.enter_sem.at[0]),
             pltpu.make_async_copy(r.cotangent.at[own_rows], r.grad_out, r.enter_sem.at[1])]
    for item in enter:
        item.start()
    weights.load_own("k", "v", "q", "cross_out", "up", "down", "attend_out")

    def bias_copy(step, kind):
        ref, full = ((r.cross_bias, r.a_cross_bias), (r.attend_bias, r.a_attend_bias),
                     (r.up_bias, r.a_up_bias))[kind]
        return pltpu.make_async_remote_copy(
            ref, full.at[z], r.send_b.at[kind], r.recv_b.at[kind],
            device_id={"mp": lax.rem(z + step, groups)}, device_id_type=MESH)

    for kind, (ref, full) in enumerate(((r.cross_bias, r.a_cross_bias),
                                        (r.attend_bias, r.a_attend_bias),
                                        (r.up_bias, r.a_up_bias))):
        for step in range(1, groups):
            bias_copy(step, kind).start()
        full[z] = ref[...]

    r.zero[...] = jnp.zeros_like(r.zero)
    r.low_grad[:, :TILE] = jnp.zeros((tokens, TILE), low)
    for test, item in reduce.zeros(s, r.low_grad):
        pl.when(test)(item.start)

    def swap(source, target, number):
        return pltpu.make_async_remote_copy(
            source, target, r.send_x.at[number], r.recv_x.at[number],
            device_id={"stream": 1 - side}, device_id_type=MESH)

    self_kinds = block_kinds(s.head, s.per_group)
    cross_kinds = block_kinds(128, CO_HEADS // groups)
    self_scale, cross_scale = 1.0 / math.sqrt(s.head), 1.0 / math.sqrt(128)

    def in_block(index):
        return pl.ds(pl.multiple_of(index * w, TILE), w)

    def project(part, source, target, bias_ref, line):
        @pl.loop(0, groups)
        def _(g):
            cols = lane(g * inner, inner)
            value = dot(source[:, :w], r.w_in[in_block(g * 3 + part), :])
            if line is not None:
                value = value + bias_ref[g, line : line + 1].astype(wide)
            target[:, cols] = value.astype(low)

    def vector(ref, line, cols=slice(0, w)):
        return ref[line : line + 1, cols].astype(wide)

    def scaled(normal, line, cols):
        return normal[:, cols] * vector(r.gains, line, cols) + vector(r.shifts, line, cols)

    def leave(source, size, weight, residual, line):
        @pl.loop(0, s.parts)
        def _(j):
            cols = lane(j * TILE)
            at = pl.ds(pl.multiple_of(j * size, TILE), size)
            r.acc[:, cols] = (dot(source[:, :size], weight[at, :]) + residual(cols)
                              + vector(r.out_bias, line, cols))

    strip = 64

    def strips(action):
        @pl.loop(0, tokens // strip)
        def _(k):
            action(pl.ds(pl.multiple_of(k * strip, strip), strip))

    def norm(normal, inverse, line, low_out):
        def action(at):
            summed = r.acc[at, :w]
            mean = jnp.sum(summed, axis=-1, keepdims=True) * (1.0 / w)
            centred = summed - mean
            scale = lax.rsqrt(
                jnp.sum(centred * centred, axis=-1, keepdims=True) * (1.0 / w) + norm_eps)
            normal[at, :w] = centred * scale
            inverse[at, :] = scale
            low_out[at, :w] = (
                centred * scale * vector(r.gains, line) + vector(r.shifts, line)).astype(low)

        strips(action)

    def cross_part(begin, end):
        @pl.loop(begin, end)
        def _(g):
            attend_forward(g, cross_kinds, cross_scale, length, rows_dev, r.q, r.pair_k, r.pair_v,
                           r.cross_allowed, r.cross_prob, r.context)

    def feed_part(begin, end):
        @pl.loop(begin, end)
        def _(g):
            for j in range(u // TILE):
                cols = lane(g * u + j * TILE)
                value = (dot(r.h1[:, :w], r.w_up[in_block(g * (u // TILE) + j), :])
                         + r.a_up_bias[g, 0:1, j * TILE : (j + 1) * TILE].astype(wide))
                bell = 0.5 * (1.0 + lax.erf(value * math.sqrt(0.5)))
                r.active[:, cols] = (value * bell).astype(low)
                r.slope[:, cols] = bell + value * (
                    jnp.exp(-0.5 * value * value) * (1.0 / math.sqrt(2.0 * math.pi)))

    def do_key():
        gather.settled(weights, "k")
        for item in enter:
            item.wait()
        weights.wait("k")
        project(1, r.x, r.k, None, None)
        swap(r.k, r.pair_k, 0).start()

    def do_value():
        gather.settled(weights, "v")
        for kind, full in enumerate((r.a_cross_bias, r.a_attend_bias, r.a_up_bias)):
            block = full.at[pl.ds(0, groups - 1)]
            pltpu.make_async_remote_copy(
                block, block, r.send_b.at[kind], r.recv_b.at[kind],
                device_id={"mp": lax.rem(z + 1, groups)}, device_id_type=MESH).wait()
        weights.wait("v")
        project(2, r.x, r.v, r.a_cross_bias, 1)
        swap(r.v, r.pair_v, 1).start()

    def do_query():
        gather.settled(weights, "q")
        weights.wait("q")
        project(0, r.x, r.q, r.a_cross_bias, 0)
        weights.load_own("attend_in")

    def do_cross_first():
        gather.settled(weights, "cross_out")
        swap(r.k, r.pair_k, 0).wait()
        swap(r.v, r.pair_v, 1).wait()
        cross_part(0, groups // 2)

    def do_cross_second():
        cross_part(groups // 2, groups)
        gather.settled(weights, "up")

    def do_first_norm():
        for test, item in reduce.zeros(s, r.low_grad):
            pl.when(test)(item.wait)
        weights.wait("cross_out")
        leave(r.context, groups * inner, r.w_cross_out, lambda cols: r.x[:, cols].astype(wide), 0)
        norm(r.n1, r.r1, 0, r.h1)

    def do_feed_first():
        weights.wait("up")
        feed_part(0, groups // 2)
        gather.settled(weights, "down")

    def do_feed_second():
        feed_part(groups // 2, groups)

    work = dict(zip(plan.forward[which], (
        do_key, do_value, do_query, do_cross_first, do_cross_second, do_first_norm,
        do_feed_first, do_feed_second)))
    for i in range(gather.waves() + 1):
        gather.wave(i, 2)
        if i in work:
            work[i]()
    weights.wait("down")
    leave(r.active, groups * u, r.w_down, lambda cols: scaled(r.n1, 0, cols), 1)
    norm(r.n2, r.r2, 1, r.h2)
    gather.settled(weights, "attend_in", "attend_out")
    weights.wait("attend_in")
    project(0, r.h2, r.q2, r.a_attend_bias, 0)
    project(1, r.h2, r.k2, None, None)
    project(2, r.h2, r.v2, r.a_attend_bias, 1)

    @pl.loop(0, groups)
    def _(g):
        attend_forward(g, self_kinds, self_scale, length, rows_dev, r.q2, r.k2, r.v2,
                       r.self_allowed, r.self_prob, r.context2)

    weights.wait("attend_out")
    leave(r.context2, groups * inner, r.w_attend_out, lambda cols: scaled(r.n2, 1, cols), 2)
    norm(r.n3, r.r3, 2, r.layer_rows)
    outputs.begin(0)
    for item in outputs.local(0):
        item.start()

    def store(row, g):
        return pltpu.make_async_copy(
            r.staged.at[g, :, pl.ds(0, w)],
            r.grads.at[g, pl.ds(pl.multiple_of(row, TILE), TILE), pl.ds(0, w)],
            r.store_sem.at[g])

    def weight_grads(left, right, row, size):
        def step(k):
            @pl.loop(0, groups)
            def _(g):
                r.staged[g, :, :w] = dot_tn(left(lane(g * size + k * TILE)), right[:, :w]).astype(low)
                store(row + k * TILE, g).start()

        return step

    def flush():
        pl.loop(0, groups)(lambda g: store(0, g).wait())

    def back_norm(source, normal, inverse, line):
        def action(at):
            incoming = source[at, :w].astype(wide)
            r.small_in[3 + line : 4 + line, :w] += down_sum(incoming * normal[at, :w])
            r.small_in[6 + line : 7 + line, :w] += down_sum(incoming)
            out = norm_back(normal[at, :w], inverse[at, :], vector(r.gains, line), incoming, w)
            r.acc[at, :w] = out
            r.low_grad[at, :w] = out.astype(low)
            r.small_in[line : line + 1, :w] += down_sum(out.astype(low).astype(wide))

        strips(action)

    def leave_back(weight, size, row, count):
        total = None
        for j in range(s.parts):
            at = pl.ds(pl.multiple_of(j * size + row, TILE), count)
            part = dot_nt(r.low_grad[:, j * TILE : (j + 1) * TILE], weight[at, :])
            total = part if total is None else total + part
        return total

    def enter_back(d, weight, blocks):
        def step(g):
            total = r.acc[:, :w]
            for b, (ref, start) in enumerate(d(g)):
                total = total + dot_nt(ref[:, lane(start)], weight[in_block(g * blocks + b), :])
            r.acc[:, :w] = total

        return step

    def context_back(weight):
        def step(g):
            r.grad_context[:, lane(g * inner, inner)] = leave_back(
                weight, groups * inner, g * inner, inner).astype(low)

        return step

    def self_step(g):
        attend_backward(g, self_kinds, self_scale, length, rows_dev, r.q2, r.k2, r.v2,
                        r.self_prob, r.grad_context, r.d.at[0], r.d.at[1], r.d.at[2])

    def cross_step(g):
        attend_backward(g, cross_kinds, cross_scale, length, rows_dev, r.q, r.pair_k, r.pair_v,
                        r.cross_prob, r.grad_context, r.d.at[0], r.d.at[1], r.d.at[2])

    def second_norm(_):
        r.small_in[12:13, :] = down_sum(r.d[0].astype(wide))
        r.small_in[13:14, :] = down_sum(r.d[2].astype(wide))
        weights.load_own("q", "k", "v")
        weights.load_rest("q", "k", "v")
        back_norm(r.acc, r.n2, r.r2, 1)

    def slope_step(g):
        for j in range(u // TILE):
            cols = lane(g * u + j * TILE)
            value = leave_back(r.w_down, groups * u, g * u + j * TILE, TILE)
            r.dz[:, cols] = (value * r.slope[:, cols]).astype(low)

    def first_norm(_):
        back_norm(r.acc, r.n1, r.r1, 0)
        units, width = plan.units, r.small_in.shape[1]
        for g in range(groups):
            for j in range(u // TILE):
                start = g * units + j * TILE
                r.small_in[9 + start // width : 10 + start // width,
                           start % width : start % width + TILE] = down_sum(
                    r.dz[:, g * u + j * TILE : g * u + (j + 1) * TILE].astype(wide))

    def pair_send(_):
        r.small_in[14:15, :] = down_sum(r.d[0].astype(wide))
        weights.wait("q", "k", "v")
        swap(r.d.at[1], r.back.at[0], 2).start()
        swap(r.d.at[2], r.back.at[1], 3).start()

    def pair_take(_):
        swap(r.d.at[1], r.back.at[0], 2).wait()
        swap(r.d.at[2], r.back.at[1], 3).wait()
        r.small_in[15:16, :] = down_sum(r.back[1].astype(wide))
        small.start()

    def hidden_store(_):
        r.hidden_rows[:, :w] = r.acc[:, :w].astype(low)
        for item in outputs.local(1):
            item.start()

    def drain_gather(_):
        for p in range(len(gather.pieces)):
            gather.drained(p)

    def attend_grads(k):
        weight_grads(lambda cols: r.d[k, :, cols], r.h2, layout.attend_in + k * inner, inner)(0)

    def cross_grads(k):
        weight_grads(lambda cols: r.back[k, :, cols], r.x,
                     layout.cross_in + (1 + k) * inner, inner)(0)

    def of(ref):
        return lambda cols: ref[:, cols]

    r.small_in[...] = jnp.zeros_like(r.small_in)
    back_norm(r.grad_out, r.n3, r.r3, 2)
    pl.loop(0, groups)(context_back(r.w_attend_out))
    weight_grads(of(r.context2), r.low_grad, layout.attend_out, inner)(0)
    nb = u // TILE
    take = plan.when[which]
    schedule = (
        (0, 4, 2, False, self_step),
        (2, 3, 1, True, attend_grads),
        (2, 4, 2, False, enter_back(lambda g: [(d, g * inner) for d in (r.d.at[0], r.d.at[1], r.d.at[2])],
                                    r.w_in, 3)),
        (4, 1, 1, False, second_norm),
        (5, 4, 2, False, slope_step),
        (5, nb, 1, True, weight_grads(of(r.active), r.low_grad, layout.down, u)),
        (5 + nb, nb, 1, True, weight_grads(of(r.dz), r.h1, layout.up, u)),
        (7, 4, 2, False, enter_back(lambda g: [(r.dz, g * u + b * TILE) for b in range(nb)],
                                    r.w_up, nb)),
        (9, 1, 1, False, first_norm),
        (10, 4, 2, False, context_back(r.w_cross_out)),
        (12, 4, 2, False, cross_step),
        (14, 1, 1, False, pair_send),
        (11, 1, 1, True, weight_grads(of(r.context), r.low_grad, layout.cross_out, inner)),
        (15, 1, 1, True, weight_grads(of(r.d.at[0]), r.x, layout.cross_in, inner)),
        (take, 1, 1, False, pair_take),
        (take, 2, 1, True, cross_grads),
        (take + 2, 4, 2, False, enter_back(
            lambda g: [(d, g * inner) for d in (r.d.at[0], r.back.at[0], r.back.at[1])], r.w_in, 3)),
        (take + 4, 1, 1, False, hidden_store),
        (take + 5, 1, 1, False, lambda _: small.middle()),
        (17, 1, 1, False, drain_gather),
        (take + 6, 1, 1, False, lambda _: outputs.drained(0)),
        (take + 12, 1, 1, False, lambda _: small.finish()),
    )
    storing = sorted({start + n for start, steps, per, keeps, _ in schedule if keeps
                      for n in range(steps)})
    assert len(storing) == sum(steps for _, steps, _, keeps, _ in schedule if keeps)
    hidden_at = take + 5

    @pl.loop(0, max(reduce.iterations(), hidden_at + plan.cuts + PACE * groups))
    def _(j):
        flushes = j == 0
        for n in storing:
            flushes = jnp.logical_or(flushes, j == n + 1)
        pl.when(flushes)(flush)
        for start, steps, per, _, step in schedule:
            @pl.when(jnp.logical_and(j >= start, j < start + steps // per))
            def _():
                if per == 1:
                    step(j - start)
                else:
                    pl.loop(0, per)(lambda n: step((j - start) * per + n))
        reduce.iteration(j)
        outputs.step(0, j, True)
        outputs.step(1, j - hidden_at)

    reduce.drained()
    outputs.drained(1)


def place_kernel(layout, groups, copies, layer_in, hidden_in, reduced, small, layer_out, hidden_out,
                 cross_in, attend_in, cross_out, attend_out, up, down,
                 cross_bias, attend_bias, up_bias, out_bias, gains, shifts,
                 held, rows, tall, flat_out, turned, load_sem, store_sem):
    inner = cross_out.shape[0]
    units = down.shape[0]
    copy = lax.axis_index("dp")
    me = lax.axis_index("mp") * copies + copy
    blocks = layout.total // inner
    loads = [pltpu.make_async_copy(
        reduced.at[pl.ds(n * inner, inner)], rows.at[n], load_sem.at[n]) for n in range(blocks)]
    stores = []

    def store(src, dst):
        stores.append(pltpu.make_async_copy(src, dst, store_sem.at[len(stores)]))
        stores[-1].start()

    large = [(pair, z) for pair in ((layer_in, layer_out, 0), (hidden_in, hidden_out, 1))
             for z in range(groups)]
    carries = [pltpu.make_async_copy(source.at[z], held.at[n, z], load_sem.at[blocks + k])
               for k, ((source, _, n), z) in enumerate(large)]
    for item in loads + carries:
        item.start()

    def turn(n, slot):
        loads[n].wait()
        turned[slot] = rows[n].astype(wide).T

    def keep(n, slot):
        loads[n].wait()
        flat_out[slot] = rows[n].astype(wide)

    first = {name: getattr(layout, name) // inner for name in (
        "attend_out", "attend_in", "down", "up", "cross_out", "cross_in")}
    keep(first["attend_out"], 0)
    store(flat_out.at[0], attend_out)
    for k in range(3):
        turn(first["attend_in"] + k, k)
        store(turned.at[k], attend_in.at[k])
    for j in range(units // inner):
        keep(first["down"] + j, 2 + j)
        store(flat_out.at[2 + j], down.at[pl.ds(j * inner, inner)])
    for j in range(units // inner):
        loads[first["up"] + j].wait()
        tall[:, j * inner : (j + 1) * inner] = rows[first["up"] + j].astype(wide).T
    store(tall, up)
    for item, ((_, target, n), z) in zip(carries, large):
        item.wait()
        store(held.at[n, z], target.at[z])
    keep(first["cross_out"], 1)
    store(flat_out.at[1], cross_out)
    for k in range(3):
        turn(first["cross_in"] + k, 3 + k)
        store(turned.at[3 + k], cross_in.at[k])

    def share(value, start, size):
        width = value.shape[1]
        return pltpu.roll(value, lax.rem(width - start, width), 1)[:, :size]

    columns = down.shape[1]
    values = share(small[...], copy * columns, columns)
    for ref, row in ((out_bias, 0), (gains, 3), (shifts, 6)):
        for k in range(3):
            ref[k] = values[row + k : row + k + 1]
    sides = share(small[...], me * (inner // copies), inner // copies)
    attend_bias[...] = sides[12:14]
    cross_bias[...] = sides[14:16]
    flat = jnp.concatenate([small[9:10], small[10:11], small[11:12]], axis=1)
    up_bias[...] = share(flat, me * (units // copies), units // copies)
    for item in stores:
        item.wait()


def shards(
    hidden,
    cotangent,
    segments,
    cross_in,
    cross_bias,
    cross_out,
    up_weight,
    up_bias,
    down_weight,
    attend_in,
    attend_bias,
    attend_out,
    out_bias,
    norm_gains,
    norm_shifts,
):
    groups = lax.axis_size("mp")
    copies = lax.axis_size("dp")
    stride = copies // 4
    side = lax.axis_index("stream")
    member = lax.axis_index("mp")
    copy = lax.axis_index("dp")
    inner = cross_in.shape[3]
    padded = hidden.shape[2]
    units = up_weight.shape[2]
    length = segments.shape[2]
    text = Setting(TEXT_WIDTH, TEXT_HEADS, TEXT_FF, groups)
    image = Setting(IMAGE_WIDTH, IMAGE_HEADS, IMAGE_FF, groups)
    settings = (text, image)
    layout = Layout(inner, units)
    rows_max = layout.total
    rows_dev = segments.shape[1] // groups
    tokens = hidden.shape[1] // groups
    co = groups * inner

    def shape(dims, kind=low):
        return jax.ShapeDtypeStruct(dims, kind)

    seg = lax.dynamic_slice_in_dim(segments, member * rows_dev, rows_dev, 1)
    seg_own = lax.dynamic_index_in_dim(seg, side, 0, keepdims=False)
    seg_other = lax.dynamic_index_in_dim(seg, 1 - side, 0, keepdims=False)
    cross_allowed = (seg_other[:, :, None] == seg_own[:, None, :]).astype(wide)
    self_allowed = (seg_own[:, :, None] == seg_own[:, None, :]).astype(wide)

    dma = pltpu.SemaphoreType.DMA

    def real(*dims):
        return pltpu.VMEM(dims, wide)

    def short(*dims):
        return pltpu.VMEM(dims, low)

    chunk, slots, cuts, ring = 64, 20, 8, 4
    widest = max(s.units for s in settings) * groups
    up_rows = max(groups * s.units * s.width for s in settings) // TILE
    heads = max(groups * s.per_group for s in settings)
    pieces, hops = 8 + 2 * max(s.units for s in settings) // TILE, groups - 1
    peers = groups * copies
    small_width = padded // max(1, peers // 16)
    scratch = Scratch(
        w_in=short(groups * 3 * padded, inner),
        w_cross_out=short(padded // TILE * co, TILE),
        w_attend_out=short(padded // TILE * co, TILE),
        w_up=short(up_rows, TILE),
        w_down=short(up_rows, TILE),
        x=short(tokens, padded),
        grad_out=short(tokens, padded),
        q=short(tokens, co),
        k=short(tokens, co),
        v=short(tokens, co),
        pair_k=short(tokens, co),
        pair_v=short(tokens, co),
        back=short(2, tokens, co),
        cross_prob=real(CO_HEADS * rows_dev, length, length),
        self_prob=real(heads * rows_dev, length, length),
        context=short(tokens, co),
        context2=short(tokens, co),
        acc=real(tokens, padded),
        n1=real(tokens, padded),
        n2=real(tokens, padded),
        n3=real(tokens, padded),
        r1=real(tokens, 1),
        r2=real(tokens, 1),
        r3=real(tokens, 1),
        h1=short(tokens, padded),
        h2=short(tokens, padded),
        slope=real(tokens, widest),
        active=short(tokens, widest),
        dz=short(tokens, widest),
        q2=short(tokens, co),
        k2=short(tokens, co),
        v2=short(tokens, co),
        d=short(3, tokens, co),
        low_grad=short(tokens, padded),
        grad_context=short(tokens, co),
        layer_rows=short(tokens, padded),
        hidden_rows=short(tokens, padded),
        zero=short(tokens, IMAGE_WIDTH - TEXT_WIDTH),
        staged=short(ring, TILE, padded),
        from_core=short(slots, 2, groups, chunk, TILE),
        from_y=short(slots, groups, chunk, TILE),
        from_z=short(slots, groups + 1, chunk, TILE),
        far=short(2, slots, chunk, 128),
        own=short(4, 2, groups, chunk, TILE),
        staged_out=short(2, chunk, TILE),
        small_in=real(16, padded),
        small_got=real(peers, 1, small_width),
        small_sum=real(1, small_width),
        small_sem=dma((2,)),
        a_cross_bias=short(groups, 2, inner),
        a_attend_bias=short(groups, 2, inner),
        a_up_bias=short(groups, 1, units),
        send_gz=dma((pieces,)),
        recv_gz=dma((pieces, groups)),
        send_gy=dma((pieces,)),
        recv_gy=dma((pieces,)),
        send_gc=dma((pieces,)),
        recv_gc=dma((pieces,)),
        weight_sem=dma((pieces,)),
        enter_sem=dma((2,)),
        send_b=dma((3,)),
        recv_b=dma((3,)),
        send_x=dma((4,)),
        recv_x=dma((4,)),
        store_sem=dma((ring,)),
        send_c=dma((slots,)),
        recv_c=dma((slots,)),
        send_y=dma((slots,)),
        recv_y=dma((slots,)),
        send_z=dma((slots,)),
        recv_z=dma((slots, groups + 1)),
        send_f=dma((slots,)),
        recv_f=dma((slots,)),
        own_sem=dma((4,)),
        out_sem=dma((2, 2)),
        send_a=dma((2, 2)),
        recv_a=dma((2, cuts, groups)),
        local_sem=dma((2, groups + 1)),
        send_s=dma((2,)),
        recv_s=dma((2,)),
        free=pltpu.SemaphoreType.REGULAR((5,)),
        zero_sem=dma((4 + rows_max // TILE,)),
    )
    plan = Plan(
        groups=groups, copies=copies, inner=inner, length=length, rows=rows_dev,
        tokens=tokens, units=units, chunk=chunk, slots=slots, cuts=cuts,
        ring=ring, lags=(3, 8, 2, 2),
        when=(26, 24),
        forward=((4, 5, 6, 10, 11, 12, 13, 14), (4, 5, 6, 8, 9, 10, 11, 12)),
    )
    weights = (
        jnp.swapaxes(cross_in[0], 0, 1),
        cross_out[0],
        up_weight[0],
        down_weight[0],
        jnp.swapaxes(attend_in[0], 0, 1),
        attend_out[0],
    )
    line = shape((groups, tokens, padded))
    out = pl.pallas_call(
        partial(layer_kernel, settings, layout, plan),
        out_shape=(
            line, line, shape((rows_max, TILE)), shape((16, padded), wide),
        ) + tuple(shape((groups,) + w.shape) for w in weights)
        + (shape((groups, rows_max, padded)),),
        in_specs=[ANY] * 8 + [VMEM] * 8,
        out_specs=(ANY,) * 3 + (VMEM,) + (ANY,) * 7,
        scratch_shapes=list(scratch),
        compiler_params=pltpu.CompilerParams(
            collective_id=0, has_side_effects=True, vmem_limit_bytes=VMEM_LIMIT),
        name="layer",
    )(*weights, hidden[0], cotangent[0], cross_bias[0], attend_bias[0], up_bias,
      out_bias[0], norm_gains[0], norm_shifts[0],
      cross_allowed.reshape(tokens, length), self_allowed.reshape(tokens, length))
    layer_out, hidden_grad, reduced, small = out[:4]

    if stride > 1:
        teams = [[q * stride + b for b in range(stride)] for q in range(4)]
        reduced = lax.psum_scatter(
            reduced, "dp", scatter_dimension=1, axis_index_groups=teams, tiled=True)

    columns, part = padded // copies, inner // copies
    shapes = (
        line, line, shape((3, columns, inner), wide), shape((3, columns, inner), wide),
        shape((inner, columns), wide), shape((inner, columns), wide),
        shape((columns, units), wide), shape((units, columns), wide),
        shape((2, part), wide), shape((2, part), wide), shape((1, units // copies), wide),
    ) + (shape((3, 1, columns), wide),) * 3
    (layer_out, hidden_grad, g_cross_in, g_attend_in, g_cross_out, g_attend_out, g_up, g_down,
     g_cross_bias, g_attend_bias, g_up_bias, g_out_bias, g_gains, g_shifts) = pl.pallas_call(
        partial(place_kernel, layout, groups, copies),
        out_shape=shapes,
        in_specs=[HBM] * 3 + [VMEM],
        out_specs=(HBM,) * 8 + (VMEM,) * 6,
        scratch_shapes=[
            short(2, groups, tokens, padded), short(rows_max // inner, inner, columns),
            real(columns, units), real(2 + units // inner, inner, columns),
            real(6, columns, inner), dma((rows_max // inner + 2 * groups,)),
            dma((9 + units // inner + 2 * groups,)),
        ],
        compiler_params=pltpu.CompilerParams(vmem_limit_bytes=VMEM_LIMIT),
        name="place",
    )(layer_out, hidden_grad, reduced, small)
    return (
        layer_out.reshape(1, groups * tokens, padded),
        hidden_grad.reshape(1, groups * tokens, padded),
        g_cross_in.transpose(1, 0, 2)[None],
        g_cross_bias[None],
        g_cross_out[None],
        g_up[None],
        g_up_bias,
        g_down[None],
        g_attend_in.transpose(1, 0, 2)[None],
        g_attend_bias[None],
        g_attend_out[None],
        g_out_bias.transpose(1, 0, 2),
        g_gains.transpose(1, 0, 2),
        g_shifts.transpose(1, 0, 2),
    )


def solution(mesh):
    placed = (
        P("stream", "dp", None),
        P("stream", "dp", None),
        P(None, "dp", None),
        P("stream", None, None, "mp"),
        P("stream", None, "mp"),
        P("stream", "mp", None),
        P("stream", None, "mp"),
        P("stream", "mp"),
        P("stream", "mp", None),
        P("stream", None, None, "mp"),
        P("stream", None, "mp"),
        P("stream", "mp", None),
        P("stream", None, None),
        P("stream", None, None),
        P("stream", None, None),
    )
    return jax.shard_map(
        shards,
        mesh=mesh,
        in_specs=placed,
        out_specs=(
            P("stream", "dp", None),
            P("stream", "dp", None),
            P("stream", "dp", None, "mp"),
            P("stream", None, ("mp", "dp")),
            P("stream", "mp", "dp"),
            P("stream", "dp", "mp"),
            P("stream", ("mp", "dp")),
            P("stream", "mp", "dp"),
            P("stream", "dp", None, "mp"),
            P("stream", None, ("mp", "dp")),
            P("stream", "mp", "dp"),
            P("stream", None, "dp"),
            P("stream", None, "dp"),
            P("stream", None, "dp"),
        ),
        check_vma=False,
    )
```

```python
import math
from functools import partial
from typing import Any, NamedTuple

import jax
import jax.numpy as jnp
from jax import lax
from jax.experimental import pallas as pl
from jax.experimental.pallas import tpu as pltpu
from jax.sharding import PartitionSpec as P

TEXT_WIDTH = 768
TEXT_HEADS = 12
TEXT_FF = 3072
IMAGE_WIDTH = 1024
IMAGE_HEADS = 8
IMAGE_FF = 1024
CO_HEADS = 8

norm_eps = 1e-12
masked_score = -1000000000.0
low = jnp.bfloat16
wide = jnp.float32
ANY = pl.BlockSpec(memory_space=pl.ANY)
VMEM = pl.BlockSpec(memory_space=pltpu.VMEM)
HBM = pl.BlockSpec(memory_space=pltpu.HBM)
MESH = pl.DeviceIdType.MESH
VMEM_LIMIT = 65400 * 1024
TILE = 256
PACE = 3


def dot(left, right):
    return jnp.dot(left, right, preferred_element_type=wide)


def dot_nt(left, right):
    return lax.dot_general(left, right, (((1,), (1,)), ((), ())), preferred_element_type=wide)


def dot_tn(left, right):
    return lax.dot_general(left, right, (((0,), (0,)), ((), ())), preferred_element_type=wide)


class Setting:
    def __init__(self, width, count, units, groups):
        self.width = width
        self.head = width // count
        self.units = units // groups
        self.lanes = width // groups
        self.parts = width // TILE
        self.per_group = count // groups


class Layout:
    def __init__(self, inner, units):
        self.units = units
        self.attend_out = 0
        self.attend_in = inner
        self.down = 4 * inner
        self.up = 4 * inner + units
        self.cross_out = 4 * inner + 2 * units
        self.cross_in = 5 * inner + 2 * units
        self.total = 8 * inner + 2 * units


def lane(start, size=TILE):
    return pl.ds(pl.multiple_of(start, 128), size)


def norm_back(normal, inverse, gain, incoming, w):
    scaled = incoming * gain
    first = jnp.sum(scaled, axis=-1, keepdims=True) * (1.0 / w)
    second = jnp.sum(scaled * normal, axis=-1, keepdims=True) * (1.0 / w)
    return inverse * (scaled - first - normal * second)


def down_sum(value):
    return jnp.sum(value, axis=0, keepdims=True)


def softmax_t(scores, allowed, scale):
    scores = jnp.where(allowed, scores, masked_score / scale)
    top = jnp.max(scores, axis=0, keepdims=True)
    exponent = jnp.exp2((scores - top) * (scale * math.log2(math.e)))
    return exponent * (1.0 / jnp.sum(exponent, axis=0, keepdims=True))


def score_grad_t(p, grad):
    return (p * (grad - jnp.sum(grad * p, axis=0, keepdims=True))).astype(low)


def halves(value):
    index = lax.broadcasted_iota(jnp.int32, value.shape, 1)
    zero = jnp.zeros_like(value)
    return jnp.concatenate(
        [jnp.where(index < 64, value, zero), jnp.where(index >= 64, value, zero)], axis=0)


def lower(value):
    index = lax.broadcasted_iota(jnp.int32, value.shape, 1)
    return jnp.where(index < 64, value, jnp.zeros_like(value))


def side_by_side(parts, axis=1):
    return parts[0] if len(parts) == 1 else jnp.concatenate(parts, axis=axis)


def split(value, count):
    size = value.shape[1] // count
    return [value[:, n * size : (n + 1) * size] for n in range(count)]


def block_kinds(head, heads):
    if head == 128:
        return [0] * heads
    return [2] * (heads // 2) + [1] * (heads % 2)


def spread_heads(kind, value):
    return halves(value) if kind == 2 else lower(value) if kind == 1 else value


def attend_forward(group, kinds, scale, length, rows, q, k, v, allowed, prob, context):
    heads = sum(max(kind, 1) for kind in kinds)
    base = group * len(kinds) * 128
    ats = [slice(r * length, (r + 1) * length) for r in range(rows)]
    step = 0
    for b, kind in enumerate(kinds):
        cols = lane(base + b * 128, 128)
        count = max(kind, 1)
        groups = [ats]
        for members in groups:
            scores = side_by_side(
                [dot_nt(k[at, cols], spread_heads(kind, q[at, cols])) for at in members])
            masks = side_by_side([allowed[at, :] for at in members for _ in range(count)])
            p = softmax_t(scores, masks > 0, scale)
            low_p = p.astype(low)
            tiles = split(p, count * len(members))
            low_tiles = split(low_p, count * len(members))
            out = [
                dot_tn(side_by_side(low_tiles[n * count : (n + 1) * count], 0),
                       spread_heads(kind, v[at, cols]))
                for n, at in enumerate(members)]
            for n, at in enumerate(members):
                r = ats.index(at)
                context[at, cols] = out[n].astype(low)
                for c in range(count):
                    prob[group * heads * rows + r * heads + step + c] = tiles[n * count + c]
        step += count


def attend_backward(group, kinds, scale, length, rows, q, k, v, prob, grad, dq, dk, dv):
    heads = sum(max(kind, 1) for kind in kinds)
    base = group * len(kinds) * 128
    ats = [slice(r * length, (r + 1) * length) for r in range(rows)]
    step = 0
    for b, kind in enumerate(kinds):
        cols = lane(base + b * 128, 128)
        count = max(kind, 1)
        groups = [ats]
        for members in groups:
            dcs = [spread_heads(kind, grad[at, cols]) for at in members]
            qs = [spread_heads(kind, q[at, cols]) for at in members]
            gp = side_by_side([dot_nt(v[at, cols], dc) for at, dc in zip(members, dcs)])
            p = side_by_side([
                prob[group * heads * rows + ats.index(at) * heads + step + c]
                for at in members for c in range(count)])
            low_p = split(p.astype(low), len(members))
            ds = split(score_grad_t(p, gp), len(members))
            grad_v = [dot(a, dc) for a, dc in zip(low_p, dcs)]
            grad_k = [dot(a, two) * scale for a, two in zip(ds, qs)]
            grad_q = [dot_tn(a, k[at, cols]) * scale for a, at in zip(ds, members)]
            for n, at in enumerate(members):
                value = grad_q[n]
                if kind:
                    index = lax.broadcasted_iota(jnp.int32, (length, 128), 1)
                    other = value[length:] if kind == 2 else jnp.zeros((length, 128), wide)
                    value = jnp.where(index < 64, value[:length], other)
                dq[at, cols] = value.astype(low)
                dk[at, cols] = grad_k[n].astype(low)
                dv[at, cols] = grad_v[n].astype(low)
        step += count
class Refs:
    def __init__(self, *groups):
        for group in groups:
            self.__dict__.update(group._asdict())


class Inputs(NamedTuple):
    cross_in: Any
    cross_out: Any
    up: Any
    down: Any
    attend_in: Any
    attend_out: Any
    hidden: Any
    cotangent: Any
    cross_bias: Any
    attend_bias: Any
    up_bias: Any
    out_bias: Any
    gains: Any
    shifts: Any
    cross_allowed: Any
    self_allowed: Any


class Results(NamedTuple):
    layer_full: Any
    hidden_full: Any
    reduced: Any
    small_out: Any
    f_cross_in: Any
    f_cross_out: Any
    f_up: Any
    f_down: Any
    f_attend_in: Any
    f_attend_out: Any
    grads: Any


class Scratch(NamedTuple):
    w_in: Any
    w_cross_out: Any
    w_attend_out: Any
    w_up: Any
    w_down: Any
    x: Any
    grad_out: Any
    q: Any
    k: Any
    v: Any
    pair_k: Any
    pair_v: Any
    back: Any
    cross_prob: Any
    self_prob: Any
    context: Any
    context2: Any
    acc: Any
    n1: Any
    n2: Any
    n3: Any
    r1: Any
    r2: Any
    r3: Any
    h1: Any
    h2: Any
    slope: Any
    active: Any
    dz: Any
    q2: Any
    k2: Any
    v2: Any
    d: Any
    low_grad: Any
    grad_context: Any
    layer_rows: Any
    hidden_rows: Any
    zero: Any
    staged: Any
    from_core: Any
    from_y: Any
    from_z: Any
    far: Any
    own: Any
    staged_out: Any
    small_in: Any
    small_got: Any
    small_sum: Any
    small_sem: Any
    a_cross_bias: Any
    a_attend_bias: Any
    a_up_bias: Any
    send_gz: Any
    recv_gz: Any
    send_gy: Any
    recv_gy: Any
    send_gc: Any
    recv_gc: Any
    weight_sem: Any
    enter_sem: Any
    send_b: Any
    recv_b: Any
    send_x: Any
    recv_x: Any
    store_sem: Any
    send_c: Any
    recv_c: Any
    send_y: Any
    recv_y: Any
    send_z: Any
    recv_z: Any
    send_f: Any
    recv_f: Any
    own_sem: Any
    out_sem: Any
    send_a: Any
    recv_a: Any
    local_sem: Any
    send_s: Any
    recv_s: Any
    free: Any
    zero_sem: Any


class Plan(NamedTuple):
    groups: Any
    copies: Any
    inner: Any
    length: Any
    rows: Any
    tokens: Any
    units: Any
    chunk: Any
    slots: Any
    cuts: Any
    ring: Any
    lags: Any
    when: Any
    forward: Any


def layer_kernel(settings, layout, plan, *refs):
    first, second = len(Inputs._fields), len(Inputs._fields) + len(Results._fields)
    r = Refs(Inputs(*refs[:first]), Results(*refs[first:second]), Scratch(*refs[second:]))
    side = lax.axis_index("stream")
    greet(plan, r)
    for which, s in enumerate(settings):
        pl.when(side == which)(partial(run_stream, which, s, layout, plan, r))


def peer_of(plan, offset):
    groups, copies = plan.groups, plan.copies
    me = lax.axis_index("mp") * copies + lax.axis_index("dp")
    index = lax.rem(me + offset, groups * copies)
    return me, index, {"mp": index // copies, "dp": lax.rem(index, copies)}


def greet(plan, r):
    barrier = pltpu.get_barrier_semaphore()
    count = plan.groups * plan.copies

    @pl.loop(1, count)
    def _(offset):
        pl.semaphore_signal(barrier, inc=1, device_id=peer_of(plan, offset)[2], device_id_type=MESH)

    pl.semaphore_signal(barrier, inc=1, device_id={"stream": 1 - lax.axis_index("stream")},
                        device_id_type=MESH)
    pl.semaphore_wait(barrier, count)


class Piece(NamedTuple):
    own: Any
    gathered: Any
    every: Any
    sized: Any
    whole: Any
    ref: Any
    full: Any
    held: Any
    place: Any


def pieces_of(s, plan, r):
    w, u, inner, groups = s.width, s.units, plan.inner, plan.groups
    pieces, named = [], {}

    def add(name, size, ref, full, held, cut, whole, place):
        named.setdefault(name, []).append(len(pieces))
        pieces.append(Piece(
            lambda part: cut(ref, (), part * size, size),
            lambda z, part: cut(full, (z,), part * size, size),
            lambda part: cut(full, (slice(None),), part * size, size),
            lambda n: cut(full, (pl.ds(0, min(n, 2)),), 0, n * size // min(n, 2)), whole, ref, full, held, place))

    def matrix(name, b, ref, full):
        add(name, w // 4, ref, full, r.w_in,
            lambda a, at, start, size: a.at[at + (b, pl.ds(start, size), slice(None))],
            lambda a: [a.at[b, pl.ds(0, w), :]],
            lambda z: [pl.ds(pl.multiple_of((z * 3 + b) * w, TILE), w)])

    def rows(name, j, count, ref, full, held):
        add(name, TILE // 4, ref, full, held,
            lambda a, at, start, size: a.at[at + (pl.ds(j * TILE + start, size), pl.ds(0, w))],
            lambda a: [a.at[pl.ds(j * TILE, TILE), pl.ds(b * TILE, TILE)] for b in range(s.parts)],
            lambda z: [pl.ds(pl.multiple_of((b * groups + z) * count + j * TILE, TILE), TILE)
                       for b in range(s.parts)])

    def columns(name, j, ref, full, held):
        add(name, w // 4, ref, full, held,
            lambda a, at, start, size: a.at[at + (pl.ds(start, size), pl.ds(j * TILE, TILE))],
            lambda a: [a.at[pl.ds(0, w), pl.ds(j * TILE, TILE)]],
            lambda z: [pl.ds(pl.multiple_of((z * (u // TILE) + j) * w, TILE), w)])

    matrix("k", 1, r.cross_in, r.f_cross_in)
    matrix("v", 2, r.cross_in, r.f_cross_in)
    matrix("q", 0, r.cross_in, r.f_cross_in)
    rows("cross_out", 0, inner, r.cross_out, r.f_cross_out, r.w_cross_out)
    for j in range(u // TILE):
        columns("up", j, r.up, r.f_up, r.w_up)
    for j in range(u // TILE):
        rows("down", j, u, r.down, r.f_down, r.w_down)
    for b in range(3):
        matrix("attend_in", b, r.attend_in, r.f_attend_in)
    rows("attend_out", 0, inner, r.attend_out, r.f_attend_out, r.w_attend_out)
    return pieces, named


class Gather:
    def __init__(self, s, plan, r):
        self.groups, self.r = plan.groups, r
        stride, copy = plan.copies // 4, lax.axis_index("dp")
        self.z = lax.axis_index("mp")
        self.quarter = lax.rem(copy // stride, 4)
        base = lax.rem(copy, stride)
        self.to_y = {"dp": (self.quarter ^ 2) * stride + base}
        self.to_c = {"dp": (self.quarter ^ 1) * stride + base}
        self.at_end = jnp.logical_or(self.z == 0, self.z == self.groups - 1)
        self.pieces, self.named = pieces_of(s, plan, r)

    def z_copy(self, p, way, hop):
        step = 1 - 2 * way
        origin = self.z - hop * step
        piece = self.pieces[p]
        dst = piece.gathered(origin, self.quarter)
        src = piece.own(self.quarter) if hop == 0 else dst
        return pltpu.make_async_remote_copy(
            src, dst, self.r.send_gz.at[p], self.r.recv_gz.at[p, origin],
            device_id={"mp": self.z + step}, device_id_type=MESH)

    def block(self, p, way, hop, whose):
        return self.pieces[p].gathered(self.z - (hop + 1) * (1 - 2 * way), whose)

    def z_arrival(self, p, way, hop):
        block = self.block(p, way, hop, self.quarter)
        origin = self.z - (hop + 1) * (1 - 2 * way)
        return pltpu.make_async_remote_copy(
            block, block, self.r.send_gz.at[p], self.r.recv_gz.at[p, origin],
            device_id={"mp": self.z - (1 - 2 * way)}, device_id_type=MESH)

    def y_copy(self, p, way, hop):
        block = self.block(p, way, hop, self.quarter)
        return pltpu.make_async_remote_copy(
            block, block, self.r.send_gy.at[p], self.r.recv_gy.at[p],
            device_id=self.to_y, device_id_type=MESH)

    def c_copy(self, p, which):
        block = self.pieces[p].every(self.quarter ^ (2 * which))
        return pltpu.make_async_remote_copy(
            block, block, self.r.send_gc.at[p], self.r.recv_gc.at[p],
            device_id=self.to_c, device_id_type=MESH)

    def total(self, p, n, send, recv, target):
        block = self.pieces[p].sized(n)
        return pltpu.make_async_remote_copy(
            block, block, send.at[p], recv.at[p], device_id=target, device_id_type=MESH)

    def y_all(self, p):
        return self.total(p, self.groups - 1, self.r.send_gy, self.r.recv_gy, self.to_y)

    def c_all(self, p):
        return self.total(p, 2 * self.groups, self.r.send_gc, self.r.recv_gc, self.to_c)

    def sends(self, way, hop):
        last = self.groups - 1
        if way == 0:
            return jnp.logical_and(self.z >= hop, self.z < last)
        return jnp.logical_and(self.z <= last - hop, self.z > 0)

    def arrives(self, way, hop):
        return self.z >= hop + 1 if way == 0 else self.z <= self.groups - 2 - hop

    def each(self, test, action, hops=None):
        for hop in range(self.groups - 1) if hops is None else hops:
            for way in range(2):
                pl.when(test(way, hop))(partial(action, way, hop))

    def own(self, p):
        for way in range(2):
            pl.when(self.sends(way, 0))(lambda: self.z_copy(p, way, 0).start())

    def begin(self, ahead):
        for p in range(ahead):
            self.own(p)
        for p in range(ahead, len(self.pieces)):
            pl.when(self.at_end)(partial(self.own, p))

    def wave(self, i, ahead):
        count, last = len(self.pieces), self.groups - 2
        for hop in range(self.groups - 1):
            if 0 <= i - hop < count:
                self.received(i - hop, hop)
        if 0 <= i - last < count:
            self.c_copy(i - last, 0).start()
        if i + ahead < count:
            pl.when(jnp.logical_not(self.at_end))(partial(self.own, i + ahead))
        if 0 <= i - last - 1 < count:
            self.y_all(i - last - 1).wait_recv()
            self.c_copy(i - last - 1, 1).start()

    def waves(self):
        return len(self.pieces) + self.groups - 1

    def received(self, p, *hops):
        def action(way, hop):
            self.z_arrival(p, way, hop).wait_recv()
            if hop + 1 < self.groups - 1:
                pl.when(self.sends(way, hop + 1))(lambda: self.z_copy(p, way, hop + 1).start())
            self.y_copy(p, way, hop).start()

        self.each(self.arrives, action, hops or None)

    def settled(self, weights, *names):
        for name in names:
            for p in self.named[name]:
                self.c_all(p).wait_recv()

                def action(way, hop):
                    for item in weights.copies(p, self.z - (hop + 1) * (1 - 2 * way), False):
                        item.start()

                self.each(self.arrives, action)

    def drained(self, p):
        for test, n in ((self.at_end, 1), (jnp.logical_not(self.at_end), self.groups + 1)):
            pl.when(test)(lambda: self.total(
                p, n, self.r.send_gz, self.r.recv_gy, self.to_y).wait_send())
        self.y_all(p).wait_send()
        self.c_all(p).wait_send()


class Weights:
    def __init__(self, s, plan, r):
        self.r, self.groups = r, plan.groups
        self.z = lax.axis_index("mp")
        self.pieces, self.named = pieces_of(s, plan, r)

    def copies(self, p, z, own):
        piece = self.pieces[p]
        blocks = piece.whole(piece.ref if own else piece.full.at[z])
        for src, rows in zip(blocks, piece.place(z)):
            yield pltpu.make_async_copy(src, piece.held.at[rows], self.r.weight_sem.at[p])

    def load_own(self, *names):
        for name in names:
            for p in self.named[name]:
                for item in self.copies(p, self.z, True):
                    item.start()

    def load_rest(self, *names):
        for name in names:
            for p in self.named[name]:
                @pl.loop(0, self.groups)
                def _(z):
                    @pl.when(self.z != z)
                    def _():
                        for item in self.copies(p, z, False):
                            item.start()

    def wait(self, *names):
        for name in names:
            for p in self.named[name]:
                piece = self.pieces[p]
                blocks = piece.whole(piece.ref)
                rows = self.groups * len(blocks) * blocks[0].shape[0]
                held = piece.held.at[pl.ds(0, rows)]
                pltpu.make_async_copy(held, held, self.r.weight_sem.at[p]).wait()


class Outputs:
    def __init__(self, s, plan, r):
        self.s, self.r, self.groups, self.cuts = s, r, plan.groups, plan.cuts
        self.z = lax.axis_index("mp")
        self.last = self.groups - 1
        self.rows = plan.tokens // self.cuts
        self.pairs = ((r.layer_rows, r.layer_full), (r.hidden_rows, r.hidden_full))

    def cut(self, ref, k):
        return ref.at[pl.ds(pl.multiple_of(k * self.rows, self.rows), self.rows),
                      pl.ds(0, self.s.width)]

    def copy(self, which, k, way, hop, arrival=False):
        step = 1 - 2 * way
        origin = self.z - (hop + 1 if arrival else hop) * step
        rows, full = self.pairs[which]
        dst = self.cut(full.at[origin], k)
        src = self.cut(rows, k) if hop == 0 and not arrival else dst
        return pltpu.make_async_remote_copy(
            src, dst, self.r.send_a.at[which, way], self.r.recv_a.at[which, k, origin],
            device_id={"mp": self.z + step}, device_id_type=MESH)

    def sends(self, way, hop):
        if way == 0:
            return jnp.logical_and(self.z >= hop, self.z < self.last)
        return jnp.logical_and(self.z <= self.last - hop, self.z > 0)

    def arrives(self, way, hop):
        return self.z >= hop + 1 if way == 0 else self.z <= self.last - 1 - hop

    def begin(self, which):
        @pl.loop(0, self.cuts)
        def _(k):
            for way in range(2):
                pl.when(self.sends(way, 0))(lambda: self.copy(which, k, way, 0).start())

    def step(self, which, k, begun=False):
        for hop in range(1 if begun else 0, self.groups):
            now = k - PACE * hop

            @pl.when(jnp.logical_and(now >= 0, now < self.cuts))
            def _():
                for way in range(2):
                    if hop:
                        pl.when(self.arrives(way, hop - 1))(
                            lambda: self.copy(which, now, way, hop - 1, True).wait_recv())
                    if hop < self.last:
                        pl.when(self.sends(way, hop))(
                            lambda: self.copy(which, now, way, hop).start())

    def local(self, which):
        rows, full = self.pairs[which]
        width = self.s.width
        items = [pltpu.make_async_copy(rows.at[:, pl.ds(0, width)],
                                       full.at[self.z, :, pl.ds(0, width)],
                                       self.r.local_sem.at[which, self.groups])]
        padded = full.shape[2]
        if width < padded:
            items += [pltpu.make_async_copy(
                self.r.zero, full.at[z, :, pl.ds(width, padded - width)],
                self.r.local_sem.at[which, z]) for z in range(self.groups)]
        return items

    def drained(self, which):
        full = self.pairs[which][1]
        for way in range(2):
            count = self.z + 1 if way == 0 else self.groups - self.z
            for n in range(1, self.groups):
                block = full.at[pl.ds(0, n), :, pl.ds(0, self.s.width)]
                pl.when(jnp.logical_and(self.sends(way, 0), count == n))(
                    lambda: pltpu.make_async_remote_copy(
                        block, block, self.r.send_a.at[which, way], self.r.recv_a.at[which, 0, 0],
                        device_id={"mp": self.z + 1 - 2 * way}, device_id_type=MESH).wait_send())
        for item in self.local(which):
            item.wait()


class Reduce:
    def __init__(self, which, s, layout, plan, r):
        self.text = which == 0
        self.r, self.groups, self.chunk = r, plan.groups, plan.chunk
        self.slots, self.lags = plan.slots, plan.lags
        self.inner, self.used = plan.inner, s.lanes // self.chunk
        self.narrow = 4 * self.used
        self.feed = s.units // self.chunk
        self.layout = layout
        self.count = self.narrow + 2 * self.feed + plan.inner // self.chunk * 4
        stride, copy = plan.copies // 4, lax.axis_index("dp")
        quarter = lax.rem(copy // stride, 4)
        base = lax.rem(copy, stride)
        self.z = lax.axis_index("mp")
        self.y, self.core = quarter // 2, lax.rem(quarter, 2)
        self.to_y = {"dp": (quarter ^ 2) * stride + base}
        self.to_c = {"dp": (quarter ^ 1) * stride + base}
        self.last = self.groups - 1

    def widths(self, action):
        if not self.text:
            action(TILE, TILE, False)
        else:
            pl.when(self.core == 0)(partial(action, TILE, 128, False))
            pl.when(self.core == 1)(partial(action, 128, TILE, True))

    def first_lane(self, core, y):
        if self.text:
            return pl.multiple_of(jnp.where(core == 0, y * 2 * TILE, TILE + y * 128), 128)
        return pl.multiple_of((2 * y + core) * TILE, 128)

    def rows(self, i):
        early = (i // self.used) * self.inner + lax.rem(i, self.used) * self.chunk
        n = i - self.narrow
        late = jnp.where(
            n < self.feed, self.layout.down + n * self.chunk,
            jnp.where(n < 2 * self.feed, self.layout.up + (n - self.feed) * self.chunk,
                      self.layout.cross_out + (n - 2 * self.feed) * self.chunk))
        start = jnp.where(i < self.narrow, early, late)
        return pl.ds(pl.multiple_of(start, self.chunk), self.chunk)

    def slot(self, i):
        return lax.rem(i, self.slots)

    def core_copy(self, i, k, other):
        n = self.slot(i)
        return pltpu.make_async_remote_copy(
            self.r.grads.at[:, self.rows(i), pl.ds(self.first_lane(1 - self.core, k), other)],
            self.r.from_core.at[n, k, :, :, pl.ds(0, other)],
            self.r.send_c.at[n], self.r.recv_c.at[n],
            device_id=self.to_c, device_id_type=MESH)

    def core_both(self, i, size):
        n = self.slot(i)
        block = self.r.from_core.at[n, :, :, :, pl.ds(0, size)]
        return pltpu.make_async_remote_copy(
            block, block, self.r.send_c.at[n], self.r.recv_c.at[n],
            device_id=self.to_c, device_id_type=MESH)

    def own_load(self, i, k, size):
        n = lax.rem(i, 4)
        return pltpu.make_async_copy(
            self.r.grads.at[:, self.rows(i), pl.ds(self.first_lane(self.core, k), size)],
            self.r.own.at[n, k, :, :, pl.ds(0, size)], self.r.own_sem.at[n])

    def own_both(self, i, size):
        n = lax.rem(i, 4)
        block = self.r.own.at[n, :, :, :, pl.ds(0, size)]
        return pltpu.make_async_copy(block, block, self.r.own_sem.at[n])

    def y_copy(self, i, size):
        n = self.slot(i)
        return pltpu.make_async_remote_copy(
            self.r.from_core.at[n, 1 - self.y, :, :, pl.ds(0, size)],
            self.r.from_y.at[n, :, :, pl.ds(0, size)],
            self.r.send_y.at[n], self.r.recv_y.at[n], device_id=self.to_y, device_id_type=MESH)

    def z_copy(self, i, way, t, size, fresh):
        n = self.slot(i)
        place = t + 1 - way
        dst = self.r.from_z.at[n, place, :, pl.ds(0, size)]
        src = self.r.from_core.at[n, self.y, t, :, pl.ds(0, size)] if fresh else dst
        return pltpu.make_async_remote_copy(
            src, dst, self.r.send_z.at[n], self.r.recv_z.at[n, place],
            device_id={"mp": self.z + 1 - 2 * way}, device_id_type=MESH)

    def far_copy(self, i):
        n = self.slot(i)
        return pltpu.make_async_remote_copy(
            self.r.far.at[0, n], self.r.far.at[1, n], self.r.send_f.at[n], self.r.recv_f.at[n],
            device_id=self.to_y, device_id_type=MESH)

    def out_store(self, i, start, size):
        n = lax.rem(i, 2)
        return pltpu.make_async_copy(
            self.r.staged_out.at[n, :, pl.ds(start, size)],
            self.r.reduced.at[self.rows(i), pl.ds(start, size)],
            self.r.out_sem.at[1 if start else 0, n])

    def credit(self, i, sem):
        pl.when(i >= self.slots)(lambda: pl.semaphore_wait(sem, 1))

    def stage_a(self, i):
        self.credit(i, self.r.free.at[0])

        def action(size, other, far):
            for k in range(2):
                self.core_copy(i, k, other).start()
                self.own_load(i, k, size).start()

        self.widths(action)

    def stage_b(self, i):
        n = self.slot(i)

        def action(size, other, far):
            self.core_both(i, size).wait_recv()
            self.own_both(i, size).wait()
            for k in range(2):
                self.r.from_core[n, k, :, :, :size] += self.r.own[lax.rem(i, 4), k, :, :, :size]
            self.credit(i, self.r.free.at[1])
            self.y_copy(i, size).start()

        self.widths(action)

    def z_step(self, hop, i):
        n = self.slot(i)

        def action(size, other, far):
            for way in range(2):
                t = self.z + (1 - 2 * way) * (self.groups - hop)

                @pl.when(t <= self.last if way == 0 else t >= 0)
                def _():
                    first = self.z == (0 if way == 0 else self.last)
                    pl.when(first)(lambda: self.z_copy(i, way, t, size, True).start())

                    @pl.when(jnp.logical_not(first))
                    def _():
                        self.z_copy(i, way, t, size, False).wait_recv()
                        self.r.from_z[n, t + 1 - way, :, :size] += (
                            self.r.from_core[n, self.y, t, :, :size])
                        self.z_copy(i, way, t, size, False).start()

        self.widths(action)

    def stage_c(self, i):
        n = self.slot(i)

        def action(size, other, far):
            self.y_copy(i, size).wait_recv()
            self.r.from_core[n, self.y, :, :, :size] += self.r.from_y[n, :, :, :size]

        self.widths(action)
        pl.when(self.z < self.last)(lambda: self.credit(i, self.r.free.at[2]))
        pl.when(self.z > 0)(lambda: self.credit(i, self.r.free.at[3]))
        self.z_step(1, i)

    def final(self, i):
        n = self.slot(i)

        def action(size, other, far):
            for way in range(2):
                edge = 0 if way == 0 else self.last

                @pl.when(self.z != edge)
                def _():
                    self.z_copy(i, way, self.z, size, False).wait_recv()

                @pl.when(self.z == edge)
                def _():
                    self.r.from_z[n, self.z + 1 - way, :, :size] = jnp.zeros((self.chunk, size), low)

            total = (self.r.from_core[n, self.y, self.z, :, :size].astype(wide)
                     + self.r.from_z[n, self.z + 1, :, :size].astype(wide)
                     + self.r.from_z[n, self.z, :, :size].astype(wide))

            def keep():
                pl.when(i >= 2)(lambda: self.out_store(i - 2, 0, size).wait())
                self.r.staged_out[lax.rem(i, 2), :, :size] = total.astype(low)
                self.out_store(i, 0, size).start()

            if far:
                pl.when(self.y == 0)(keep)

                @pl.when(self.y == 1)
                def _():
                    pl.when(i >= self.slots)(lambda: self.far_copy(i - self.slots).wait_send())
                    self.credit(i, self.r.free.at[4])
                    self.r.far[0, n] = total.astype(low)
                    self.far_copy(i).start()
            else:
                keep()
            self.core_both(i, other).wait_send()
            self.y_copy(i, size).wait_send()
            block = self.r.from_z.at[n, pl.ds(0, self.last), :, pl.ds(0, size)]
            pltpu.make_async_remote_copy(
                block, block, self.r.send_z.at[n], self.r.recv_z.at[n, 0],
                device_id=self.to_y, device_id_type=MESH).wait_send()

        self.widths(action)

        @pl.when(i < self.count - self.slots)
        def _():
            def tell(index, target):
                pl.semaphore_signal(self.r.free.at[index], inc=1, device_id=target,
                                    device_id_type=MESH)

            tell(0, self.to_c)
            tell(1, self.to_y)
            pl.when(self.z > 0)(lambda: tell(2, {"mp": self.z - 1}))
            pl.when(self.z < self.last)(lambda: tell(3, {"mp": self.z + 1}))

    def land(self, i):
        n = self.slot(i)

        def action(size, other, far):
            if not far:
                return

            @pl.when(self.y == 0)
            def _():
                self.far_copy(i).wait_recv()
                pl.when(i >= 2)(lambda: self.out_store(i - 2, size, size).wait())
                self.r.staged_out[lax.rem(i, 2), :, size : 2 * size] = self.r.far[1, n]
                self.out_store(i, size, size).start()

                @pl.when(i < self.count - self.slots)
                def _():
                    pl.semaphore_signal(self.r.free.at[4], inc=1, device_id=self.to_y,
                                        device_id_type=MESH)

        self.widths(action)

    def zeros(self, s, zero):
        blocks = [(4 * self.chunk * n + self.used * self.chunk, self.inner - self.used * self.chunk)
                  for n in range(4)] if self.used * self.chunk < self.inner else []
        for start in (self.layout.down, self.layout.up):
            blocks += [(row, TILE) for row in range(start + s.units, start + self.layout.units, TILE)]
        number = 0
        for always, group in ((True, blocks), (False, [(row, TILE) for row in range(
                0, self.layout.total, TILE)] if self.text else [])):
            test = self.y + self.core == 2
            for row, size in group:
                yield (jnp.logical_not(test) if always and self.text else test if self.text
                       else self.y >= 0, pltpu.make_async_copy(
                    zero.at[pl.ds(0, size), pl.ds(0, TILE)],
                    self.r.reduced.at[pl.ds(row, size)], self.r.zero_sem.at[number]))
                number += 1

    def iteration(self, j):
        lag_b, lag_c, lag_z, lag_f = self.lags

        def at(i, stage):
            pl.when(jnp.logical_and(i >= 0, i < self.count))(lambda: stage(i))

        at(j, self.stage_a)
        at(j - lag_b, self.stage_b)
        at(j - lag_c, self.stage_c)
        for hop in range(2, self.groups):
            at(j - lag_c - lag_z * (hop - 1), partial(self.z_step, hop))
        done = lag_c + lag_z * (self.groups - 1)
        at(j - done, self.final)
        if self.text:
            at(j - done - lag_f, self.land)

    def iterations(self):
        lag_b, lag_c, lag_z, lag_f = self.lags
        return self.count + lag_c + lag_z * (self.groups - 1) + (lag_f if self.text else 0)

    def drained(self):
        def action(size, other, far):
            pair = (self.count - 2, self.count - 1)
            if not far:
                for i in pair:
                    self.out_store(jnp.int32(i), 0, size).wait()
                return

            @pl.when(self.y == 0)
            def _():
                for i in pair:
                    self.out_store(jnp.int32(i), 0, size).wait()
                    self.out_store(jnp.int32(i), size, size).wait()

            @pl.when(self.y == 1)
            def _():
                @pl.loop(self.count - self.slots, self.count)
                def _(i):
                    self.far_copy(i).wait_send()

        self.widths(action)


class Small:
    def __init__(self, plan, r):
        self.plan, self.r = plan, r
        self.count = plan.groups * plan.copies
        self.per_row = max(1, self.count // 16)
        self.width = r.small_in.shape[1] // self.per_row

    def piece(self, ref, index):
        row, part = index // self.per_row, lax.rem(index, self.per_row)
        return ref.at[pl.ds(row, 1), pl.ds(pl.multiple_of(part * self.width, 128), self.width)]

    def copy(self, offset, first):
        me, peer, target = peer_of(self.plan, offset)
        if first:
            src, dst = self.piece(self.r.small_in, peer), self.r.small_got.at[me]
        else:
            src, dst = self.r.small_sum, self.piece(self.r.small_out, me)
        n = 0 if first else 1
        return pltpu.make_async_remote_copy(
            src, dst, self.r.send_s.at[n], self.r.recv_s.at[n],
            device_id=target, device_id_type=MESH)

    def all(self, first):
        n = 0 if first else 1
        block = self.r.small_got.at[pl.ds(0, self.count - 1)]
        return pltpu.make_async_remote_copy(
            block, block, self.r.send_s.at[n], self.r.recv_s.at[n],
            device_id=peer_of(self.plan, 1)[2], device_id_type=MESH)

    def every(self, action):
        @pl.loop(1, self.count)
        def _(offset):
            action(offset)

    def start(self):
        self.every(lambda offset: self.copy(offset, True).start())

    def local(self, first):
        me = peer_of(self.plan, 0)[0]
        pair = ((self.piece(self.r.small_in, me), self.r.small_got.at[me]) if first
                else (self.r.small_sum, self.piece(self.r.small_out, me)))
        return pltpu.make_async_copy(*pair, self.r.small_sem.at[0 if first else 1])

    def middle(self):
        self.local(True).start()
        self.all(True).wait_recv()
        self.local(True).wait()
        self.r.small_sum[...] = jnp.sum(self.r.small_got[...], axis=0)
        self.local(False).start()
        self.every(lambda offset: self.copy(offset, False).start())

    def finish(self):
        self.local(False).wait()
        self.all(False).wait_recv()
        for first in (True, False):
            self.all(first).wait_send()


def run_stream(which, s, layout, plan, r):
    groups, inner, length = plan.groups, plan.inner, plan.length
    rows_dev = plan.rows
    tokens = plan.tokens
    w, u = s.width, s.units
    z = lax.axis_index("mp")
    side = lax.axis_index("stream")
    gather = Gather(s, plan, r)
    weights = Weights(s, plan, r)
    outputs = Outputs(s, plan, r)
    reduce = Reduce(which, s, layout, plan, r)
    small = Small(plan, r)

    gather.begin(2)
    own_rows = pl.ds(pl.multiple_of(z * tokens, tokens), tokens)
    enter = [pltpu.make_async_copy(r.hidden.at[own_rows], r.x, r.enter_sem.at[0]),
             pltpu.make_async_copy(r.cotangent.at[own_rows], r.grad_out, r.enter_sem.at[1])]
    for item in enter:
        item.start()
    weights.load_own("k", "v", "q", "cross_out", "up", "down", "attend_out")

    def bias_copy(step, kind):
        ref, full = ((r.cross_bias, r.a_cross_bias), (r.attend_bias, r.a_attend_bias),
                     (r.up_bias, r.a_up_bias))[kind]
        return pltpu.make_async_remote_copy(
            ref, full.at[z], r.send_b.at[kind], r.recv_b.at[kind],
            device_id={"mp": lax.rem(z + step, groups)}, device_id_type=MESH)

    for kind, (ref, full) in enumerate(((r.cross_bias, r.a_cross_bias),
                                        (r.attend_bias, r.a_attend_bias),
                                        (r.up_bias, r.a_up_bias))):
        for step in range(1, groups):
            bias_copy(step, kind).start()
        full[z] = ref[...]

    r.zero[...] = jnp.zeros_like(r.zero)
    r.low_grad[:, :TILE] = jnp.zeros((tokens, TILE), low)
    for test, item in reduce.zeros(s, r.low_grad):
        pl.when(test)(item.start)

    def swap(source, target, number):
        return pltpu.make_async_remote_copy(
            source, target, r.send_x.at[number], r.recv_x.at[number],
            device_id={"stream": 1 - side}, device_id_type=MESH)

    self_kinds = block_kinds(s.head, s.per_group)
    cross_kinds = block_kinds(128, CO_HEADS // groups)
    self_scale, cross_scale = 1.0 / math.sqrt(s.head), 1.0 / math.sqrt(128)

    def in_block(index):
        return pl.ds(pl.multiple_of(index * w, TILE), w)

    def project(part, source, target, bias_ref, line):
        @pl.loop(0, groups)
        def _(g):
            cols = lane(g * inner, inner)
            value = dot(source[:, :w], r.w_in[in_block(g * 3 + part), :])
            if line is not None:
                value = value + bias_ref[g, line : line + 1].astype(wide)
            target[:, cols] = value.astype(low)

    def vector(ref, line, cols=slice(0, w)):
        return ref[line : line + 1, cols].astype(wide)

    def scaled(normal, line, cols):
        return normal[:, cols] * vector(r.gains, line, cols) + vector(r.shifts, line, cols)

    def leave(source, size, weight, residual, line):
        @pl.loop(0, s.parts)
        def _(j):
            cols = lane(j * TILE)
            at = pl.ds(pl.multiple_of(j * size, TILE), size)
            r.acc[:, cols] = (dot(source[:, :size], weight[at, :]) + residual(cols)
                              + vector(r.out_bias, line, cols))

    strip = 64

    def strips(action):
        @pl.loop(0, tokens // strip)
        def _(k):
            action(pl.ds(pl.multiple_of(k * strip, strip), strip))

    def norm(normal, inverse, line, low_out):
        def action(at):
            summed = r.acc[at, :w]
            mean = jnp.sum(summed, axis=-1, keepdims=True) * (1.0 / w)
            centred = summed - mean
            scale = lax.rsqrt(
                jnp.sum(centred * centred, axis=-1, keepdims=True) * (1.0 / w) + norm_eps)
            normal[at, :w] = centred * scale
            inverse[at, :] = scale
            low_out[at, :w] = (
                centred * scale * vector(r.gains, line) + vector(r.shifts, line)).astype(low)

        strips(action)

    def cross_part(begin, end):
        @pl.loop(begin, end)
        def _(g):
            attend_forward(g, cross_kinds, cross_scale, length, rows_dev, r.q, r.pair_k, r.pair_v,
                           r.cross_allowed, r.cross_prob, r.context)

    def feed_part(begin, end):
        @pl.loop(begin, end)
        def _(g):
            for j in range(u // TILE):
                cols = lane(g * u + j * TILE)
                value = (dot(r.h1[:, :w], r.w_up[in_block(g * (u // TILE) + j), :])
                         + r.a_up_bias[g, 0:1, j * TILE : (j + 1) * TILE].astype(wide))
                bell = 0.5 * (1.0 + lax.erf(value * math.sqrt(0.5)))
                r.active[:, cols] = (value * bell).astype(low)
                r.slope[:, cols] = bell + value * (
                    jnp.exp(-0.5 * value * value) * (1.0 / math.sqrt(2.0 * math.pi)))

    def do_key():
        gather.settled(weights, "k")
        for item in enter:
            item.wait()
        weights.wait("k")
        project(1, r.x, r.k, None, None)
        swap(r.k, r.pair_k, 0).start()

    def do_value():
        gather.settled(weights, "v")
        for kind, full in enumerate((r.a_cross_bias, r.a_attend_bias, r.a_up_bias)):
            block = full.at[pl.ds(0, groups - 1)]
            pltpu.make_async_remote_copy(
                block, block, r.send_b.at[kind], r.recv_b.at[kind],
                device_id={"mp": lax.rem(z + 1, groups)}, device_id_type=MESH).wait()
        weights.wait("v")
        project(2, r.x, r.v, r.a_cross_bias, 1)
        swap(r.v, r.pair_v, 1).start()

    def do_query():
        gather.settled(weights, "q")
        weights.wait("q")
        project(0, r.x, r.q, r.a_cross_bias, 0)
        weights.load_own("attend_in")

    def do_cross_first():
        gather.settled(weights, "cross_out")
        swap(r.k, r.pair_k, 0).wait()
        swap(r.v, r.pair_v, 1).wait()
        cross_part(0, groups // 2)

    def do_cross_second():
        cross_part(groups // 2, groups)
        gather.settled(weights, "up")

    def do_first_norm():
        for test, item in reduce.zeros(s, r.low_grad):
            pl.when(test)(item.wait)
        weights.wait("cross_out")
        leave(r.context, groups * inner, r.w_cross_out, lambda cols: r.x[:, cols].astype(wide), 0)
        norm(r.n1, r.r1, 0, r.h1)

    def do_feed_first():
        weights.wait("up")
        feed_part(0, groups // 2)
        gather.settled(weights, "down")

    def do_feed_second():
        feed_part(groups // 2, groups)

    work = dict(zip(plan.forward[which], (
        do_key, do_value, do_query, do_cross_first, do_cross_second, do_first_norm,
        do_feed_first, do_feed_second)))
    for i in range(gather.waves() + 1):
        gather.wave(i, 2)
        if i in work:
            work[i]()
    weights.wait("down")
    leave(r.active, groups * u, r.w_down, lambda cols: scaled(r.n1, 0, cols), 1)
    norm(r.n2, r.r2, 1, r.h2)
    gather.settled(weights, "attend_in", "attend_out")
    weights.wait("attend_in")
    project(0, r.h2, r.q2, r.a_attend_bias, 0)
    project(1, r.h2, r.k2, None, None)
    project(2, r.h2, r.v2, r.a_attend_bias, 1)

    @pl.loop(0, groups)
    def _(g):
        attend_forward(g, self_kinds, self_scale, length, rows_dev, r.q2, r.k2, r.v2,
                       r.self_allowed, r.self_prob, r.context2)

    weights.wait("attend_out")
    leave(r.context2, groups * inner, r.w_attend_out, lambda cols: scaled(r.n2, 1, cols), 2)
    norm(r.n3, r.r3, 2, r.layer_rows)

    def store(row, g):
        return pltpu.make_async_copy(
            r.staged.at[g, :, pl.ds(0, w)],
            r.grads.at[g, pl.ds(pl.multiple_of(row, TILE), TILE), pl.ds(0, w)],
            r.store_sem.at[g])

    def weight_grads(left, right, row, size):
        def step(k):
            @pl.loop(0, groups)
            def _(g):
                r.staged[g, :, :w] = dot_tn(left(lane(g * size + k * TILE)), right[:, :w]).astype(low)
                store(row + k * TILE, g).start()

        return step

    def flush():
        pl.loop(0, groups)(lambda g: store(0, g).wait())

    def back_norm(source, normal, inverse, line):
        def action(at):
            incoming = source[at, :w].astype(wide)
            r.small_in[3 + line : 4 + line, :w] += down_sum(incoming * normal[at, :w])
            r.small_in[6 + line : 7 + line, :w] += down_sum(incoming)
            out = norm_back(normal[at, :w], inverse[at, :], vector(r.gains, line), incoming, w)
            r.acc[at, :w] = out
            r.low_grad[at, :w] = out.astype(low)
            r.small_in[line : line + 1, :w] += down_sum(out.astype(low).astype(wide))

        strips(action)

    def leave_back(weight, size, row, count):
        total = None
        for j in range(s.parts):
            at = pl.ds(pl.multiple_of(j * size + row, TILE), count)
            part = dot_nt(r.low_grad[:, j * TILE : (j + 1) * TILE], weight[at, :])
            total = part if total is None else total + part
        return total

    def enter_back(d, weight, blocks):
        def step(g):
            total = r.acc[:, :w]
            for b, (ref, start) in enumerate(d(g)):
                total = total + dot_nt(ref[:, lane(start)], weight[in_block(g * blocks + b), :])
            r.acc[:, :w] = total

        return step

    def context_back(weight):
        def step(g):
            r.grad_context[:, lane(g * inner, inner)] = leave_back(
                weight, groups * inner, g * inner, inner).astype(low)

        return step

    def self_step(g):
        attend_backward(g, self_kinds, self_scale, length, rows_dev, r.q2, r.k2, r.v2,
                        r.self_prob, r.grad_context, r.d.at[0], r.d.at[1], r.d.at[2])

    def cross_step(g):
        attend_backward(g, cross_kinds, cross_scale, length, rows_dev, r.q, r.pair_k, r.pair_v,
                        r.cross_prob, r.grad_context, r.d.at[0], r.d.at[1], r.d.at[2])

    def second_norm(_):
        r.small_in[12:13, :] = down_sum(r.d[0].astype(wide))
        r.small_in[13:14, :] = down_sum(r.d[2].astype(wide))
        weights.load_own("q", "k", "v")
        weights.load_rest("q", "k", "v")
        back_norm(r.acc, r.n2, r.r2, 1)

    def slope_step(g):
        for j in range(u // TILE):
            cols = lane(g * u + j * TILE)
            value = leave_back(r.w_down, groups * u, g * u + j * TILE, TILE)
            r.dz[:, cols] = (value * r.slope[:, cols]).astype(low)

    def first_norm(_):
        back_norm(r.acc, r.n1, r.r1, 0)
        units, width = plan.units, r.small_in.shape[1]
        for g in range(groups):
            for j in range(u // TILE):
                start = g * units + j * TILE
                r.small_in[9 + start // width : 10 + start // width,
                           start % width : start % width + TILE] = down_sum(
                    r.dz[:, g * u + j * TILE : g * u + (j + 1) * TILE].astype(wide))

    def pair_send(_):
        r.small_in[14:15, :] = down_sum(r.d[0].astype(wide))
        weights.wait("q", "k", "v")
        swap(r.d.at[1], r.back.at[0], 2).start()
        swap(r.d.at[2], r.back.at[1], 3).start()

    def pair_take(_):
        swap(r.d.at[1], r.back.at[0], 2).wait()
        swap(r.d.at[2], r.back.at[1], 3).wait()
        r.small_in[15:16, :] = down_sum(r.back[1].astype(wide))
        small.start()

    def hidden_store(_):
        r.hidden_rows[:, :w] = r.acc[:, :w].astype(low)
        for item in outputs.local(1):
            item.start()

    def layer_send(_):
        outputs.begin(0)
        for item in outputs.local(0):
            item.start()

    def drain_gather(_):
        for p in range(len(gather.pieces)):
            gather.drained(p)

    def attend_grads(k):
        weight_grads(lambda cols: r.d[k, :, cols], r.h2, layout.attend_in + k * inner, inner)(0)

    def cross_grads(k):
        weight_grads(lambda cols: r.back[k, :, cols], r.x,
                     layout.cross_in + (1 + k) * inner, inner)(0)

    def of(ref):
        return lambda cols: ref[:, cols]

    r.small_in[...] = jnp.zeros_like(r.small_in)
    back_norm(r.grad_out, r.n3, r.r3, 2)
    weight_grads(of(r.context2), r.low_grad, layout.attend_out, inner)(0)
    nb = u // TILE
    take = plan.when[which]
    schedule = (
        (0, 4, 4, False, context_back(r.w_attend_out)),
        (0, 4, 2, False, self_step),
        (1, 1, 1, False, layer_send),
        (2, 3, 1, True, attend_grads),
        (2, 4, 2, False, enter_back(lambda g: [(d, g * inner) for d in (r.d.at[0], r.d.at[1], r.d.at[2])],
                                    r.w_in, 3)),
        (4, 1, 1, False, second_norm),
        (5, 4, 2, False, slope_step),
        (5, nb, 1, True, weight_grads(of(r.active), r.low_grad, layout.down, u)),
        (5 + nb, nb, 1, True, weight_grads(of(r.dz), r.h1, layout.up, u)),
        (7, 4, 2, False, enter_back(lambda g: [(r.dz, g * u + b * TILE) for b in range(nb)],
                                    r.w_up, nb)),
        (9, 1, 1, False, first_norm),
        (10, 4, 2, False, context_back(r.w_cross_out)),
        (12, 4, 2, False, cross_step),
        (14, 1, 1, False, pair_send),
        (11, 1, 1, True, weight_grads(of(r.context), r.low_grad, layout.cross_out, inner)),
        (15, 1, 1, True, weight_grads(of(r.d.at[0]), r.x, layout.cross_in, inner)),
        (take, 1, 1, False, pair_take),
        (take, 2, 1, True, cross_grads),
        (take + 2, 4, 2, False, enter_back(
            lambda g: [(d, g * inner) for d in (r.d.at[0], r.back.at[0], r.back.at[1])], r.w_in, 3)),
        (take + 4, 1, 1, False, hidden_store),
        (take + 5, 1, 1, False, lambda _: small.middle()),
        (17, 1, 1, False, drain_gather),
        (take + 6, 1, 1, False, lambda _: outputs.drained(0)),
        (take + 12, 1, 1, False, lambda _: small.finish()),
    )
    storing = sorted({start + n for start, steps, per, keeps, _ in schedule if keeps
                      for n in range(steps)})
    assert len(storing) == sum(steps for _, steps, _, keeps, _ in schedule if keeps)
    hidden_at = take + 5

    @pl.loop(0, max(reduce.iterations(), hidden_at + plan.cuts + PACE * groups))
    def _(j):
        flushes = j == 0
        for n in storing:
            flushes = jnp.logical_or(flushes, j == n + 1)
        pl.when(flushes)(flush)
        reduce.iteration(j)
        for start, steps, per, _, step in schedule:
            @pl.when(jnp.logical_and(j >= start, j < start + steps // per))
            def _():
                if per == 1:
                    step(j - start)
                else:
                    pl.loop(0, per)(lambda n: step((j - start) * per + n))
        outputs.step(0, j - 1, True)
        outputs.step(1, j - hidden_at)

    reduce.drained()
    outputs.drained(1)


def place_kernel(layout, groups, copies, layer_in, hidden_in, reduced, small, layer_out, hidden_out,
                 cross_in, attend_in, cross_out, attend_out, up, down,
                 cross_bias, attend_bias, up_bias, out_bias, gains, shifts,
                 held, rows, tall, flat_out, turned, load_sem, store_sem):
    inner = cross_out.shape[0]
    units = down.shape[0]
    copy = lax.axis_index("dp")
    me = lax.axis_index("mp") * copies + copy
    blocks = layout.total // inner
    loads = [pltpu.make_async_copy(
        reduced.at[pl.ds(n * inner, inner)], rows.at[n], load_sem.at[n]) for n in range(blocks)]
    stores = []

    def store(src, dst):
        stores.append(pltpu.make_async_copy(src, dst, store_sem.at[len(stores)]))
        stores[-1].start()

    large = [(pair, z) for pair in ((layer_in, layer_out, 0), (hidden_in, hidden_out, 1))
             for z in range(groups)]
    carries = [pltpu.make_async_copy(source.at[z], held.at[n, z], load_sem.at[blocks + k])
               for k, ((source, _, n), z) in enumerate(large)]
    for item in loads + carries:
        item.start()

    def turn(n, slot):
        loads[n].wait()
        turned[slot] = rows[n].astype(wide).T

    def keep(n, slot):
        loads[n].wait()
        flat_out[slot] = rows[n].astype(wide)

    first = {name: getattr(layout, name) // inner for name in (
        "attend_out", "attend_in", "down", "up", "cross_out", "cross_in")}
    keep(first["attend_out"], 0)
    store(flat_out.at[0], attend_out)
    for k in range(3):
        turn(first["attend_in"] + k, k)
        store(turned.at[k], attend_in.at[k])
    for j in range(units // inner):
        keep(first["down"] + j, 2 + j)
        store(flat_out.at[2 + j], down.at[pl.ds(j * inner, inner)])
    for j in range(units // inner):
        loads[first["up"] + j].wait()
        tall[:, j * inner : (j + 1) * inner] = rows[first["up"] + j].astype(wide).T
    store(tall, up)
    for item, ((_, target, n), z) in zip(carries, large):
        item.wait()
        store(held.at[n, z], target.at[z])
    keep(first["cross_out"], 1)
    store(flat_out.at[1], cross_out)
    for k in range(3):
        turn(first["cross_in"] + k, 3 + k)
        store(turned.at[3 + k], cross_in.at[k])

    def share(value, start, size):
        width = value.shape[1]
        return pltpu.roll(value, lax.rem(width - start, width), 1)[:, :size]

    columns = down.shape[1]
    values = share(small[...], copy * columns, columns)
    for ref, row in ((out_bias, 0), (gains, 3), (shifts, 6)):
        for k in range(3):
            ref[k] = values[row + k : row + k + 1]
    sides = share(small[...], me * (inner // copies), inner // copies)
    attend_bias[...] = sides[12:14]
    cross_bias[...] = sides[14:16]
    flat = jnp.concatenate([small[9:10], small[10:11], small[11:12]], axis=1)
    up_bias[...] = share(flat, me * (units // copies), units // copies)
    for item in stores:
        item.wait()


def shards(
    hidden,
    cotangent,
    segments,
    cross_in,
    cross_bias,
    cross_out,
    up_weight,
    up_bias,
    down_weight,
    attend_in,
    attend_bias,
    attend_out,
    out_bias,
    norm_gains,
    norm_shifts,
):
    groups = lax.axis_size("mp")
    copies = lax.axis_size("dp")
    stride = copies // 4
    side = lax.axis_index("stream")
    member = lax.axis_index("mp")
    copy = lax.axis_index("dp")
    inner = cross_in.shape[3]
    padded = hidden.shape[2]
    units = up_weight.shape[2]
    length = segments.shape[2]
    text = Setting(TEXT_WIDTH, TEXT_HEADS, TEXT_FF, groups)
    image = Setting(IMAGE_WIDTH, IMAGE_HEADS, IMAGE_FF, groups)
    settings = (text, image)
    layout = Layout(inner, units)
    rows_max = layout.total
    rows_dev = segments.shape[1] // groups
    tokens = hidden.shape[1] // groups
    co = groups * inner

    def shape(dims, kind=low):
        return jax.ShapeDtypeStruct(dims, kind)

    seg = lax.dynamic_slice_in_dim(segments, member * rows_dev, rows_dev, 1)
    seg_own = lax.dynamic_index_in_dim(seg, side, 0, keepdims=False)
    seg_other = lax.dynamic_index_in_dim(seg, 1 - side, 0, keepdims=False)
    cross_allowed = (seg_other[:, :, None] == seg_own[:, None, :]).astype(wide)
    self_allowed = (seg_own[:, :, None] == seg_own[:, None, :]).astype(wide)

    dma = pltpu.SemaphoreType.DMA

    def real(*dims):
        return pltpu.VMEM(dims, wide)

    def short(*dims):
        return pltpu.VMEM(dims, low)

    chunk, slots, cuts, ring = 64, 20, 8, 4
    widest = max(s.units for s in settings) * groups
    up_rows = max(groups * s.units * s.width for s in settings) // TILE
    heads = max(groups * s.per_group for s in settings)
    pieces, hops = 8 + 2 * max(s.units for s in settings) // TILE, groups - 1
    peers = groups * copies
    small_width = padded // max(1, peers // 16)
    scratch = Scratch(
        w_in=short(groups * 3 * padded, inner),
        w_cross_out=short(padded // TILE * co, TILE),
        w_attend_out=short(padded // TILE * co, TILE),
        w_up=short(up_rows, TILE),
        w_down=short(up_rows, TILE),
        x=short(tokens, padded),
        grad_out=short(tokens, padded),
        q=short(tokens, co),
        k=short(tokens, co),
        v=short(tokens, co),
        pair_k=short(tokens, co),
        pair_v=short(tokens, co),
        back=short(2, tokens, co),
        cross_prob=real(CO_HEADS * rows_dev, length, length),
        self_prob=real(heads * rows_dev, length, length),
        context=short(tokens, co),
        context2=short(tokens, co),
        acc=real(tokens, padded),
        n1=real(tokens, padded),
        n2=real(tokens, padded),
        n3=real(tokens, padded),
        r1=real(tokens, 1),
        r2=real(tokens, 1),
        r3=real(tokens, 1),
        h1=short(tokens, padded),
        h2=short(tokens, padded),
        slope=real(tokens, widest),
        active=short(tokens, widest),
        dz=short(tokens, widest),
        q2=short(tokens, co),
        k2=short(tokens, co),
        v2=short(tokens, co),
        d=short(3, tokens, co),
        low_grad=short(tokens, padded),
        grad_context=short(tokens, co),
        layer_rows=short(tokens, padded),
        hidden_rows=short(tokens, padded),
        zero=short(tokens, IMAGE_WIDTH - TEXT_WIDTH),
        staged=short(ring, TILE, padded),
        from_core=short(slots, 2, groups, chunk, TILE),
        from_y=short(slots, groups, chunk, TILE),
        from_z=short(slots, groups + 1, chunk, TILE),
        far=short(2, slots, chunk, 128),
        own=short(4, 2, groups, chunk, TILE),
        staged_out=short(2, chunk, TILE),
        small_in=real(16, padded),
        small_got=real(peers, 1, small_width),
        small_sum=real(1, small_width),
        small_sem=dma((2,)),
        a_cross_bias=short(groups, 2, inner),
        a_attend_bias=short(groups, 2, inner),
        a_up_bias=short(groups, 1, units),
        send_gz=dma((pieces,)),
        recv_gz=dma((pieces, groups)),
        send_gy=dma((pieces,)),
        recv_gy=dma((pieces,)),
        send_gc=dma((pieces,)),
        recv_gc=dma((pieces,)),
        weight_sem=dma((pieces,)),
        enter_sem=dma((2,)),
        send_b=dma((3,)),
        recv_b=dma((3,)),
        send_x=dma((4,)),
        recv_x=dma((4,)),
        store_sem=dma((ring,)),
        send_c=dma((slots,)),
        recv_c=dma((slots,)),
        send_y=dma((slots,)),
        recv_y=dma((slots,)),
        send_z=dma((slots,)),
        recv_z=dma((slots, groups + 1)),
        send_f=dma((slots,)),
        recv_f=dma((slots,)),
        own_sem=dma((4,)),
        out_sem=dma((2, 2)),
        send_a=dma((2, 2)),
        recv_a=dma((2, cuts, groups)),
        local_sem=dma((2, groups + 1)),
        send_s=dma((2,)),
        recv_s=dma((2,)),
        free=pltpu.SemaphoreType.REGULAR((5,)),
        zero_sem=dma((4 + rows_max // TILE,)),
    )
    plan = Plan(
        groups=groups, copies=copies, inner=inner, length=length, rows=rows_dev,
        tokens=tokens, units=units, chunk=chunk, slots=slots, cuts=cuts,
        ring=ring, lags=(1, 8, 2, 2),
        when=(25, 25),
        forward=((4, 5, 6, 10, 11, 12, 13, 14), (4, 5, 6, 8, 9, 10, 11, 12)),
    )
    weights = (
        jnp.swapaxes(cross_in[0], 0, 1),
        cross_out[0],
        up_weight[0],
        down_weight[0],
        jnp.swapaxes(attend_in[0], 0, 1),
        attend_out[0],
    )
    line = shape((groups, tokens, padded))
    out = pl.pallas_call(
        partial(layer_kernel, settings, layout, plan),
        out_shape=(
            line, line, shape((rows_max, TILE)), shape((16, padded), wide),
        ) + tuple(shape((groups,) + w.shape) for w in weights)
        + (shape((groups, rows_max, padded)),),
        in_specs=[ANY] * 8 + [VMEM] * 8,
        out_specs=(ANY,) * 3 + (VMEM,) + (ANY,) * 7,
        scratch_shapes=list(scratch),
        compiler_params=pltpu.CompilerParams(
            collective_id=0, has_side_effects=True, vmem_limit_bytes=VMEM_LIMIT),
        name="layer",
    )(*weights, hidden[0], cotangent[0], cross_bias[0], attend_bias[0], up_bias,
      out_bias[0], norm_gains[0], norm_shifts[0],
      cross_allowed.reshape(tokens, length), self_allowed.reshape(tokens, length))
    layer_out, hidden_grad, reduced, small = out[:4]

    if stride > 1:
        teams = [[q * stride + b for b in range(stride)] for q in range(4)]
        reduced = lax.psum_scatter(
            reduced, "dp", scatter_dimension=1, axis_index_groups=teams, tiled=True)

    columns, part = padded // copies, inner // copies
    shapes = (
        line, line, shape((3, columns, inner), wide), shape((3, columns, inner), wide),
        shape((inner, columns), wide), shape((inner, columns), wide),
        shape((columns, units), wide), shape((units, columns), wide),
        shape((2, part), wide), shape((2, part), wide), shape((1, units // copies), wide),
    ) + (shape((3, 1, columns), wide),) * 3
    (layer_out, hidden_grad, g_cross_in, g_attend_in, g_cross_out, g_attend_out, g_up, g_down,
     g_cross_bias, g_attend_bias, g_up_bias, g_out_bias, g_gains, g_shifts) = pl.pallas_call(
        partial(place_kernel, layout, groups, copies),
        out_shape=shapes,
        in_specs=[HBM] * 3 + [VMEM],
        out_specs=(HBM,) * 8 + (VMEM,) * 6,
        scratch_shapes=[
            short(2, groups, tokens, padded), short(rows_max // inner, inner, columns),
            real(columns, units), real(2 + units // inner, inner, columns),
            real(6, columns, inner), dma((rows_max // inner + 2 * groups,)),
            dma((9 + units // inner + 2 * groups,)),
        ],
        compiler_params=pltpu.CompilerParams(vmem_limit_bytes=VMEM_LIMIT),
        name="place",
    )(layer_out, hidden_grad, reduced, small)
    return (
        layer_out.reshape(1, groups * tokens, padded),
        hidden_grad.reshape(1, groups * tokens, padded),
        g_cross_in.transpose(1, 0, 2)[None],
        g_cross_bias[None],
        g_cross_out[None],
        g_up[None],
        g_up_bias,
        g_down[None],
        g_attend_in.transpose(1, 0, 2)[None],
        g_attend_bias[None],
        g_attend_out[None],
        g_out_bias.transpose(1, 0, 2),
        g_gains.transpose(1, 0, 2),
        g_shifts.transpose(1, 0, 2),
    )


def solution(mesh):
    placed = (
        P("stream", "dp", None),
        P("stream", "dp", None),
        P(None, "dp", None),
        P("stream", None, None, "mp"),
        P("stream", None, "mp"),
        P("stream", "mp", None),
        P("stream", None, "mp"),
        P("stream", "mp"),
        P("stream", "mp", None),
        P("stream", None, None, "mp"),
        P("stream", None, "mp"),
        P("stream", "mp", None),
        P("stream", None, None),
        P("stream", None, None),
        P("stream", None, None),
    )
    return jax.shard_map(
        shards,
        mesh=mesh,
        in_specs=placed,
        out_specs=(
            P("stream", "dp", None),
            P("stream", "dp", None),
            P("stream", "dp", None, "mp"),
            P("stream", None, ("mp", "dp")),
            P("stream", "mp", "dp"),
            P("stream", "dp", "mp"),
            P("stream", ("mp", "dp")),
            P("stream", "mp", "dp"),
            P("stream", "dp", None, "mp"),
            P("stream", None, ("mp", "dp")),
            P("stream", "mp", "dp"),
            P("stream", None, "dp"),
            P("stream", None, "dp"),
            P("stream", None, "dp"),
        ),
        check_vma=False,
    )
```

```python
import math
from functools import partial
from typing import Any, NamedTuple

import jax
import jax.numpy as jnp
from jax import lax
from jax.experimental import pallas as pl
from jax.experimental.pallas import tpu as pltpu
from jax.sharding import PartitionSpec as P

TEXT_WIDTH = 768
TEXT_HEADS = 12
TEXT_FF = 3072
IMAGE_WIDTH = 1024
IMAGE_HEADS = 8
IMAGE_FF = 1024
CO_HEADS = 8

norm_eps = 1e-12
masked_score = -1000000000.0
low = jnp.bfloat16
wide = jnp.float32
ANY = pl.BlockSpec(memory_space=pl.ANY)
VMEM = pl.BlockSpec(memory_space=pltpu.VMEM)
HBM = pl.BlockSpec(memory_space=pltpu.HBM)
MESH = pl.DeviceIdType.MESH
VMEM_LIMIT = 65400 * 1024
TILE = 256
PACE = 3


def dot(left, right):
    return jnp.dot(left, right, preferred_element_type=wide)


def dot_nt(left, right):
    return lax.dot_general(left, right, (((1,), (1,)), ((), ())), preferred_element_type=wide)


def dot_tn(left, right):
    return lax.dot_general(left, right, (((0,), (0,)), ((), ())), preferred_element_type=wide)


class Setting:
    def __init__(self, width, count, units, groups):
        self.width = width
        self.head = width // count
        self.units = units // groups
        self.lanes = width // groups
        self.parts = width // TILE
        self.per_group = count // groups


class Layout:
    def __init__(self, inner, units):
        self.units = units
        self.attend_out = 0
        self.attend_in = inner
        self.down = 4 * inner
        self.up = 4 * inner + units
        self.cross_out = 4 * inner + 2 * units
        self.cross_in = 5 * inner + 2 * units
        self.total = 8 * inner + 2 * units


def lane(start, size=TILE):
    return pl.ds(pl.multiple_of(start, 128), size)


def norm_back(normal, inverse, gain, incoming, w):
    scaled = incoming * gain
    first = jnp.sum(scaled, axis=-1, keepdims=True) * (1.0 / w)
    second = jnp.sum(scaled * normal, axis=-1, keepdims=True) * (1.0 / w)
    return inverse * (scaled - first - normal * second)


def down_sum(value):
    return jnp.sum(value, axis=0, keepdims=True)


def softmax_t(scores, allowed, scale):
    scores = jnp.where(allowed, scores, masked_score / scale)
    top = jnp.max(scores, axis=0, keepdims=True)
    exponent = jnp.exp2((scores - top) * (scale * math.log2(math.e)))
    return exponent * (1.0 / jnp.sum(exponent, axis=0, keepdims=True))


def score_grad_t(p, grad):
    return (p * (grad - jnp.sum(grad * p, axis=0, keepdims=True))).astype(low)


def halves(value):
    index = lax.broadcasted_iota(jnp.int32, value.shape, 1)
    zero = jnp.zeros_like(value)
    return jnp.concatenate(
        [jnp.where(index < 64, value, zero), jnp.where(index >= 64, value, zero)], axis=0)


def lower(value):
    index = lax.broadcasted_iota(jnp.int32, value.shape, 1)
    return jnp.where(index < 64, value, jnp.zeros_like(value))


def side_by_side(parts, axis=1):
    return parts[0] if len(parts) == 1 else jnp.concatenate(parts, axis=axis)


def split(value, count):
    size = value.shape[1] // count
    return [value[:, n * size : (n + 1) * size] for n in range(count)]


def block_kinds(head, heads):
    if head == 128:
        return [0] * heads
    return [2] * (heads // 2) + [1] * (heads % 2)


def spread_heads(kind, value):
    return halves(value) if kind == 2 else lower(value) if kind == 1 else value


def attend_forward(group, kinds, scale, length, rows, q, k, v, allowed, prob, context):
    heads = sum(max(kind, 1) for kind in kinds)
    base = group * len(kinds) * 128
    ats = [slice(r * length, (r + 1) * length) for r in range(rows)]
    step = 0
    for b, kind in enumerate(kinds):
        cols = lane(base + b * 128, 128)
        count = max(kind, 1)
        groups = [ats]
        for members in groups:
            scores = side_by_side(
                [dot_nt(k[at, cols], spread_heads(kind, q[at, cols])) for at in members])
            masks = side_by_side([allowed[at, :] for at in members for _ in range(count)])
            p = softmax_t(scores, masks > 0, scale)
            low_p = p.astype(low)
            tiles = split(p, count * len(members))
            low_tiles = split(low_p, count * len(members))
            out = [
                dot_tn(side_by_side(low_tiles[n * count : (n + 1) * count], 0),
                       spread_heads(kind, v[at, cols]))
                for n, at in enumerate(members)]
            for n, at in enumerate(members):
                r = ats.index(at)
                context[at, cols] = out[n].astype(low)
                for c in range(count):
                    prob[group * heads * rows + r * heads + step + c] = tiles[n * count + c]
        step += count


def attend_backward(group, kinds, scale, length, rows, q, k, v, prob, grad, dq, dk, dv):
    heads = sum(max(kind, 1) for kind in kinds)
    base = group * len(kinds) * 128
    ats = [slice(r * length, (r + 1) * length) for r in range(rows)]
    step = 0
    for b, kind in enumerate(kinds):
        cols = lane(base + b * 128, 128)
        count = max(kind, 1)
        groups = [ats]
        for members in groups:
            dcs = [spread_heads(kind, grad[at, cols]) for at in members]
            qs = [spread_heads(kind, q[at, cols]) for at in members]
            gp = side_by_side([dot_nt(v[at, cols], dc) for at, dc in zip(members, dcs)])
            p = side_by_side([
                prob[group * heads * rows + ats.index(at) * heads + step + c]
                for at in members for c in range(count)])
            low_p = split(p.astype(low), len(members))
            ds = split(score_grad_t(p, gp), len(members))
            grad_v = [dot(a, dc) for a, dc in zip(low_p, dcs)]
            grad_k = [dot(a, two) * scale for a, two in zip(ds, qs)]
            grad_q = [dot_tn(a, k[at, cols]) * scale for a, at in zip(ds, members)]
            for n, at in enumerate(members):
                value = grad_q[n]
                if kind:
                    index = lax.broadcasted_iota(jnp.int32, (length, 128), 1)
                    other = value[length:] if kind == 2 else jnp.zeros((length, 128), wide)
                    value = jnp.where(index < 64, value[:length], other)
                dq[at, cols] = value.astype(low)
                dk[at, cols] = grad_k[n].astype(low)
                dv[at, cols] = grad_v[n].astype(low)
        step += count
class Refs:
    def __init__(self, *groups):
        for group in groups:
            self.__dict__.update(group._asdict())


class Inputs(NamedTuple):
    cross_in: Any
    cross_out: Any
    up: Any
    down: Any
    attend_in: Any
    attend_out: Any
    hidden: Any
    cotangent: Any
    cross_bias: Any
    attend_bias: Any
    up_bias: Any
    out_bias: Any
    gains: Any
    shifts: Any
    cross_allowed: Any
    self_allowed: Any


class Results(NamedTuple):
    layer_full: Any
    hidden_full: Any
    reduced: Any
    small_out: Any
    f_cross_in: Any
    f_cross_out: Any
    f_up: Any
    f_down: Any
    f_attend_in: Any
    f_attend_out: Any
    grads: Any


class Scratch(NamedTuple):
    w_in: Any
    w_cross_out: Any
    w_attend_out: Any
    w_up: Any
    w_down: Any
    x: Any
    grad_out: Any
    q: Any
    k: Any
    v: Any
    pair_k: Any
    pair_v: Any
    back: Any
    cross_prob: Any
    self_prob: Any
    context: Any
    context2: Any
    acc: Any
    n1: Any
    n2: Any
    n3: Any
    r1: Any
    r2: Any
    r3: Any
    h1: Any
    h2: Any
    slope: Any
    active: Any
    dz: Any
    q2: Any
    k2: Any
    v2: Any
    d: Any
    low_grad: Any
    grad_context: Any
    layer_rows: Any
    hidden_rows: Any
    zero: Any
    staged: Any
    from_core: Any
    from_y: Any
    from_z: Any
    far: Any
    own: Any
    staged_out: Any
    small_in: Any
    small_got: Any
    small_sum: Any
    small_sem: Any
    a_cross_bias: Any
    a_attend_bias: Any
    a_up_bias: Any
    send_gz: Any
    recv_gz: Any
    send_gy: Any
    recv_gy: Any
    send_gc: Any
    recv_gc: Any
    weight_sem: Any
    enter_sem: Any
    send_b: Any
    recv_b: Any
    send_x: Any
    recv_x: Any
    store_sem: Any
    send_c: Any
    recv_c: Any
    send_y: Any
    recv_y: Any
    send_z: Any
    recv_z: Any
    send_f: Any
    recv_f: Any
    own_sem: Any
    out_sem: Any
    send_a: Any
    recv_a: Any
    local_sem: Any
    send_s: Any
    recv_s: Any
    free: Any
    zero_sem: Any


class Plan(NamedTuple):
    groups: Any
    copies: Any
    inner: Any
    length: Any
    rows: Any
    tokens: Any
    units: Any
    chunk: Any
    slots: Any
    cuts: Any
    ring: Any
    lags: Any
    when: Any
    forward: Any


def layer_kernel(settings, layout, plan, *refs):
    first, second = len(Inputs._fields), len(Inputs._fields) + len(Results._fields)
    r = Refs(Inputs(*refs[:first]), Results(*refs[first:second]), Scratch(*refs[second:]))
    side = lax.axis_index("stream")
    greet(plan, r)
    for which, s in enumerate(settings):
        pl.when(side == which)(partial(run_stream, which, s, layout, plan, r))


def peer_of(plan, offset):
    groups, copies = plan.groups, plan.copies
    me = lax.axis_index("mp") * copies + lax.axis_index("dp")
    index = lax.rem(me + offset, groups * copies)
    return me, index, {"mp": index // copies, "dp": lax.rem(index, copies)}


def greet(plan, r):
    barrier = pltpu.get_barrier_semaphore()
    count = plan.groups * plan.copies

    @pl.loop(1, count)
    def _(offset):
        pl.semaphore_signal(barrier, inc=1, device_id=peer_of(plan, offset)[2], device_id_type=MESH)

    pl.semaphore_signal(barrier, inc=1, device_id={"stream": 1 - lax.axis_index("stream")},
                        device_id_type=MESH)
    pl.semaphore_wait(barrier, count)


class Piece(NamedTuple):
    own: Any
    gathered: Any
    every: Any
    sized: Any
    whole: Any
    ref: Any
    full: Any
    held: Any
    place: Any


def pieces_of(s, plan, r):
    w, u, inner, groups = s.width, s.units, plan.inner, plan.groups
    pieces, named = [], {}

    def add(name, size, ref, full, held, cut, whole, place):
        named.setdefault(name, []).append(len(pieces))
        pieces.append(Piece(
            lambda part: cut(ref, (), part * size, size),
            lambda z, part: cut(full, (z,), part * size, size),
            lambda part: cut(full, (slice(None),), part * size, size),
            lambda n: cut(full, (pl.ds(0, min(n, 2)),), 0, n * size // min(n, 2)), whole, ref, full, held, place))

    def matrix(name, b, ref, full):
        add(name, w // 4, ref, full, r.w_in,
            lambda a, at, start, size: a.at[at + (b, pl.ds(start, size), slice(None))],
            lambda a: [a.at[b, pl.ds(0, w), :]],
            lambda z: [pl.ds(pl.multiple_of((z * 3 + b) * w, TILE), w)])

    def rows(name, j, count, ref, full, held):
        add(name, TILE // 4, ref, full, held,
            lambda a, at, start, size: a.at[at + (pl.ds(j * TILE + start, size), pl.ds(0, w))],
            lambda a: [a.at[pl.ds(j * TILE, TILE), pl.ds(b * TILE, TILE)] for b in range(s.parts)],
            lambda z: [pl.ds(pl.multiple_of((b * groups + z) * count + j * TILE, TILE), TILE)
                       for b in range(s.parts)])

    def columns(name, j, ref, full, held):
        add(name, w // 4, ref, full, held,
            lambda a, at, start, size: a.at[at + (pl.ds(start, size), pl.ds(j * TILE, TILE))],
            lambda a: [a.at[pl.ds(0, w), pl.ds(j * TILE, TILE)]],
            lambda z: [pl.ds(pl.multiple_of((z * (u // TILE) + j) * w, TILE), w)])

    matrix("k", 1, r.cross_in, r.f_cross_in)
    matrix("v", 2, r.cross_in, r.f_cross_in)
    matrix("q", 0, r.cross_in, r.f_cross_in)
    rows("cross_out", 0, inner, r.cross_out, r.f_cross_out, r.w_cross_out)
    for j in range(u // TILE):
        columns("up", j, r.up, r.f_up, r.w_up)
    for j in range(u // TILE):
        rows("down", j, u, r.down, r.f_down, r.w_down)
    matrix("attend_q", 0, r.attend_in, r.f_attend_in)
    matrix("attend_k", 1, r.attend_in, r.f_attend_in)
    matrix("attend_v", 2, r.attend_in, r.f_attend_in)
    rows("attend_out", 0, inner, r.attend_out, r.f_attend_out, r.w_attend_out)
    return pieces, named


class Gather:
    def __init__(self, s, plan, r):
        self.groups, self.r = plan.groups, r
        stride, copy = plan.copies // 4, lax.axis_index("dp")
        self.z = lax.axis_index("mp")
        self.quarter = lax.rem(copy // stride, 4)
        base = lax.rem(copy, stride)
        self.to_y = {"dp": (self.quarter ^ 2) * stride + base}
        self.to_c = {"dp": (self.quarter ^ 1) * stride + base}
        self.at_end = jnp.logical_or(self.z == 0, self.z == self.groups - 1)
        self.pieces, self.named = pieces_of(s, plan, r)

    def z_copy(self, p, way, hop):
        step = 1 - 2 * way
        origin = self.z - hop * step
        piece = self.pieces[p]
        dst = piece.gathered(origin, self.quarter)
        src = piece.own(self.quarter) if hop == 0 else dst
        return pltpu.make_async_remote_copy(
            src, dst, self.r.send_gz.at[p], self.r.recv_gz.at[p, origin],
            device_id={"mp": self.z + step}, device_id_type=MESH)

    def block(self, p, way, hop, whose):
        return self.pieces[p].gathered(self.z - (hop + 1) * (1 - 2 * way), whose)

    def z_arrival(self, p, way, hop):
        block = self.block(p, way, hop, self.quarter)
        origin = self.z - (hop + 1) * (1 - 2 * way)
        return pltpu.make_async_remote_copy(
            block, block, self.r.send_gz.at[p], self.r.recv_gz.at[p, origin],
            device_id={"mp": self.z - (1 - 2 * way)}, device_id_type=MESH)

    def y_copy(self, p, way, hop):
        block = self.block(p, way, hop, self.quarter)
        return pltpu.make_async_remote_copy(
            block, block, self.r.send_gy.at[p], self.r.recv_gy.at[p],
            device_id=self.to_y, device_id_type=MESH)

    def c_copy(self, p, which):
        block = self.pieces[p].every(self.quarter ^ (2 * which))
        return pltpu.make_async_remote_copy(
            block, block, self.r.send_gc.at[p], self.r.recv_gc.at[p],
            device_id=self.to_c, device_id_type=MESH)

    def total(self, p, n, send, recv, target):
        block = self.pieces[p].sized(n)
        return pltpu.make_async_remote_copy(
            block, block, send.at[p], recv.at[p], device_id=target, device_id_type=MESH)

    def y_all(self, p):
        return self.total(p, self.groups - 1, self.r.send_gy, self.r.recv_gy, self.to_y)

    def c_all(self, p):
        return self.total(p, 2 * self.groups, self.r.send_gc, self.r.recv_gc, self.to_c)

    def sends(self, way, hop):
        last = self.groups - 1
        if way == 0:
            return jnp.logical_and(self.z >= hop, self.z < last)
        return jnp.logical_and(self.z <= last - hop, self.z > 0)

    def arrives(self, way, hop):
        return self.z >= hop + 1 if way == 0 else self.z <= self.groups - 2 - hop

    def each(self, test, action, hops=None):
        for hop in range(self.groups - 1) if hops is None else hops:
            for way in range(2):
                pl.when(test(way, hop))(partial(action, way, hop))

    def own(self, p):
        for way in range(2):
            pl.when(self.sends(way, 0))(lambda: self.z_copy(p, way, 0).start())

    def begin(self, ahead):
        for p in range(ahead):
            self.own(p)
        for p in range(ahead, len(self.pieces)):
            pl.when(self.at_end)(partial(self.own, p))

    def wave(self, i, ahead):
        count, last = len(self.pieces), self.groups - 2
        for hop in range(self.groups - 1):
            if 0 <= i - hop < count:
                self.received(i - hop, hop)
        if 0 <= i - last < count:
            self.c_copy(i - last, 0).start()
        if i + ahead < count:
            pl.when(jnp.logical_not(self.at_end))(partial(self.own, i + ahead))
        if 0 <= i - last - 1 < count:
            self.y_all(i - last - 1).wait_recv()
            self.c_copy(i - last - 1, 1).start()

    def waves(self):
        return len(self.pieces) + self.groups - 1

    def received(self, p, *hops):
        def action(way, hop):
            self.z_arrival(p, way, hop).wait_recv()
            if hop + 1 < self.groups - 1:
                pl.when(self.sends(way, hop + 1))(lambda: self.z_copy(p, way, hop + 1).start())
            self.y_copy(p, way, hop).start()

        self.each(self.arrives, action, hops or None)

    def settled(self, weights, *names):
        for name in names:
            for p in self.named[name]:
                self.c_all(p).wait_recv()

                def action(way, hop):
                    for item in weights.copies(p, self.z - (hop + 1) * (1 - 2 * way), False):
                        item.start()

                self.each(self.arrives, action)

    def drained(self, p):
        for test, n in ((self.at_end, 1), (jnp.logical_not(self.at_end), self.groups + 1)):
            pl.when(test)(lambda: self.total(
                p, n, self.r.send_gz, self.r.recv_gy, self.to_y).wait_send())
        self.y_all(p).wait_send()
        self.c_all(p).wait_send()


class Weights:
    def __init__(self, s, plan, r):
        self.r, self.groups = r, plan.groups
        self.z = lax.axis_index("mp")
        self.pieces, self.named = pieces_of(s, plan, r)

    def copies(self, p, z, own):
        piece = self.pieces[p]
        blocks = piece.whole(piece.ref if own else piece.full.at[z])
        for src, rows in zip(blocks, piece.place(z)):
            yield pltpu.make_async_copy(src, piece.held.at[rows], self.r.weight_sem.at[p])

    def load_own(self, *names):
        for name in names:
            for p in self.named[name]:
                for item in self.copies(p, self.z, True):
                    item.start()

    def load_rest(self, *names):
        for name in names:
            for p in self.named[name]:
                @pl.loop(0, self.groups)
                def _(z):
                    @pl.when(self.z != z)
                    def _():
                        for item in self.copies(p, z, False):
                            item.start()

    def wait(self, *names):
        for name in names:
            for p in self.named[name]:
                piece = self.pieces[p]
                blocks = piece.whole(piece.ref)
                rows = self.groups * len(blocks) * blocks[0].shape[0]
                held = piece.held.at[pl.ds(0, rows)]
                pltpu.make_async_copy(held, held, self.r.weight_sem.at[p]).wait()


class Outputs:
    def __init__(self, s, plan, r):
        self.s, self.r, self.groups, self.cuts = s, r, plan.groups, plan.cuts
        self.z = lax.axis_index("mp")
        self.last = self.groups - 1
        self.rows = plan.tokens // self.cuts
        self.pairs = ((r.layer_rows, r.layer_full), (r.hidden_rows, r.hidden_full))

    def cut(self, ref, k):
        return ref.at[pl.ds(pl.multiple_of(k * self.rows, self.rows), self.rows),
                      pl.ds(0, self.s.width)]

    def copy(self, which, k, way, hop, arrival=False):
        step = 1 - 2 * way
        origin = self.z - (hop + 1 if arrival else hop) * step
        rows, full = self.pairs[which]
        dst = self.cut(full.at[origin], k)
        src = self.cut(rows, k) if hop == 0 and not arrival else dst
        return pltpu.make_async_remote_copy(
            src, dst, self.r.send_a.at[which, way], self.r.recv_a.at[which, k, origin],
            device_id={"mp": self.z + step}, device_id_type=MESH)

    def sends(self, way, hop):
        if way == 0:
            return jnp.logical_and(self.z >= hop, self.z < self.last)
        return jnp.logical_and(self.z <= self.last - hop, self.z > 0)

    def arrives(self, way, hop):
        return self.z >= hop + 1 if way == 0 else self.z <= self.last - 1 - hop

    def begin(self, which):
        @pl.loop(0, self.cuts)
        def _(k):
            for way in range(2):
                pl.when(self.sends(way, 0))(lambda: self.copy(which, k, way, 0).start())

    def step(self, which, k, begun=False):
        for hop in range(1 if begun else 0, self.groups):
            now = k - PACE * hop

            @pl.when(jnp.logical_and(now >= 0, now < self.cuts))
            def _():
                for way in range(2):
                    if hop:
                        pl.when(self.arrives(way, hop - 1))(
                            lambda: self.copy(which, now, way, hop - 1, True).wait_recv())
                    if hop < self.last:
                        pl.when(self.sends(way, hop))(
                            lambda: self.copy(which, now, way, hop).start())

    def local(self, which):
        rows, full = self.pairs[which]
        width = self.s.width
        items = [pltpu.make_async_copy(rows.at[:, pl.ds(0, width)],
                                       full.at[self.z, :, pl.ds(0, width)],
                                       self.r.local_sem.at[which, self.groups])]
        padded = full.shape[2]
        if width < padded:
            items += [pltpu.make_async_copy(
                self.r.zero, full.at[z, :, pl.ds(width, padded - width)],
                self.r.local_sem.at[which, z]) for z in range(self.groups)]
        return items

    def drained(self, which):
        full = self.pairs[which][1]
        for way in range(2):
            count = self.z + 1 if way == 0 else self.groups - self.z
            for n in range(1, self.groups):
                block = full.at[pl.ds(0, n), :, pl.ds(0, self.s.width)]
                pl.when(jnp.logical_and(self.sends(way, 0), count == n))(
                    lambda: pltpu.make_async_remote_copy(
                        block, block, self.r.send_a.at[which, way], self.r.recv_a.at[which, 0, 0],
                        device_id={"mp": self.z + 1 - 2 * way}, device_id_type=MESH).wait_send())
        for item in self.local(which):
            item.wait()


class Reduce:
    def __init__(self, which, s, layout, plan, r):
        self.text = which == 0
        self.r, self.groups, self.chunk = r, plan.groups, plan.chunk
        self.slots, self.lags = plan.slots, plan.lags
        self.inner, self.used = plan.inner, s.lanes // self.chunk
        self.narrow = 4 * self.used
        self.feed = s.units // self.chunk
        self.layout = layout
        self.count = self.narrow + 2 * self.feed + plan.inner // self.chunk * 4
        stride, copy = plan.copies // 4, lax.axis_index("dp")
        quarter = lax.rem(copy // stride, 4)
        base = lax.rem(copy, stride)
        self.z = lax.axis_index("mp")
        self.y, self.core = quarter // 2, lax.rem(quarter, 2)
        self.to_y = {"dp": (quarter ^ 2) * stride + base}
        self.to_c = {"dp": (quarter ^ 1) * stride + base}
        self.last = self.groups - 1

    def widths(self, action):
        if not self.text:
            action(TILE, TILE, False)
        else:
            pl.when(self.core == 0)(partial(action, TILE, 128, False))
            pl.when(self.core == 1)(partial(action, 128, TILE, True))

    def first_lane(self, core, y):
        if self.text:
            return pl.multiple_of(jnp.where(core == 0, y * 2 * TILE, TILE + y * 128), 128)
        return pl.multiple_of((2 * y + core) * TILE, 128)

    def rows(self, i):
        early = (i // self.used) * self.inner + lax.rem(i, self.used) * self.chunk
        n = i - self.narrow
        late = jnp.where(
            n < self.feed, self.layout.down + n * self.chunk,
            jnp.where(n < 2 * self.feed, self.layout.up + (n - self.feed) * self.chunk,
                      self.layout.cross_out + (n - 2 * self.feed) * self.chunk))
        start = jnp.where(i < self.narrow, early, late)
        return pl.ds(pl.multiple_of(start, self.chunk), self.chunk)

    def slot(self, i):
        return lax.rem(i, self.slots)

    def core_copy(self, i, k, other):
        n = self.slot(i)
        return pltpu.make_async_remote_copy(
            self.r.grads.at[:, self.rows(i), pl.ds(self.first_lane(1 - self.core, k), other)],
            self.r.from_core.at[n, k, :, :, pl.ds(0, other)],
            self.r.send_c.at[n], self.r.recv_c.at[n],
            device_id=self.to_c, device_id_type=MESH)

    def core_both(self, i, size):
        n = self.slot(i)
        block = self.r.from_core.at[n, :, :, :, pl.ds(0, size)]
        return pltpu.make_async_remote_copy(
            block, block, self.r.send_c.at[n], self.r.recv_c.at[n],
            device_id=self.to_c, device_id_type=MESH)

    def own_load(self, i, k, size):
        n = lax.rem(i, 4)
        return pltpu.make_async_copy(
            self.r.grads.at[:, self.rows(i), pl.ds(self.first_lane(self.core, k), size)],
            self.r.own.at[n, k, :, :, pl.ds(0, size)], self.r.own_sem.at[n])

    def own_both(self, i, size):
        n = lax.rem(i, 4)
        block = self.r.own.at[n, :, :, :, pl.ds(0, size)]
        return pltpu.make_async_copy(block, block, self.r.own_sem.at[n])

    def y_copy(self, i, size):
        n = self.slot(i)
        return pltpu.make_async_remote_copy(
            self.r.from_core.at[n, 1 - self.y, :, :, pl.ds(0, size)],
            self.r.from_y.at[n, :, :, pl.ds(0, size)],
            self.r.send_y.at[n], self.r.recv_y.at[n], device_id=self.to_y, device_id_type=MESH)

    def z_copy(self, i, way, t, size, fresh):
        n = self.slot(i)
        place = t + 1 - way
        dst = self.r.from_z.at[n, place, :, pl.ds(0, size)]
        src = self.r.from_core.at[n, self.y, t, :, pl.ds(0, size)] if fresh else dst
        return pltpu.make_async_remote_copy(
            src, dst, self.r.send_z.at[n], self.r.recv_z.at[n, place],
            device_id={"mp": self.z + 1 - 2 * way}, device_id_type=MESH)

    def far_copy(self, i):
        n = self.slot(i)
        return pltpu.make_async_remote_copy(
            self.r.far.at[0, n], self.r.far.at[1, n], self.r.send_f.at[n], self.r.recv_f.at[n],
            device_id=self.to_y, device_id_type=MESH)

    def out_store(self, i, start, size):
        n = lax.rem(i, 2)
        return pltpu.make_async_copy(
            self.r.staged_out.at[n, :, pl.ds(start, size)],
            self.r.reduced.at[self.rows(i), pl.ds(start, size)],
            self.r.out_sem.at[1 if start else 0, n])

    def credit(self, i, sem):
        pl.when(i >= self.slots)(lambda: pl.semaphore_wait(sem, 1))

    def stage_a(self, i):
        self.credit(i, self.r.free.at[0])

        def action(size, other, far):
            for k in range(2):
                self.core_copy(i, k, other).start()
                self.own_load(i, k, size).start()

        self.widths(action)

    def stage_b(self, i):
        n = self.slot(i)

        def action(size, other, far):
            self.core_both(i, size).wait_recv()
            self.own_both(i, size).wait()
            for k in range(2):
                self.r.from_core[n, k, :, :, :size] += self.r.own[lax.rem(i, 4), k, :, :, :size]
            self.credit(i, self.r.free.at[1])
            self.y_copy(i, size).start()

        self.widths(action)

    def z_step(self, hop, i):
        n = self.slot(i)

        def action(size, other, far):
            for way in range(2):
                t = self.z + (1 - 2 * way) * (self.groups - hop)

                @pl.when(t <= self.last if way == 0 else t >= 0)
                def _():
                    first = self.z == (0 if way == 0 else self.last)
                    pl.when(first)(lambda: self.z_copy(i, way, t, size, True).start())

                    @pl.when(jnp.logical_not(first))
                    def _():
                        self.z_copy(i, way, t, size, False).wait_recv()
                        self.r.from_z[n, t + 1 - way, :, :size] += (
                            self.r.from_core[n, self.y, t, :, :size])
                        self.z_copy(i, way, t, size, False).start()

        self.widths(action)

    def stage_c(self, i):
        n = self.slot(i)

        def action(size, other, far):
            self.y_copy(i, size).wait_recv()
            self.r.from_core[n, self.y, :, :, :size] += self.r.from_y[n, :, :, :size]

        self.widths(action)
        pl.when(self.z < self.last)(lambda: self.credit(i, self.r.free.at[2]))
        pl.when(self.z > 0)(lambda: self.credit(i, self.r.free.at[3]))
        self.z_step(1, i)

    def final(self, i):
        n = self.slot(i)

        def action(size, other, far):
            for way in range(2):
                edge = 0 if way == 0 else self.last

                @pl.when(self.z != edge)
                def _():
                    self.z_copy(i, way, self.z, size, False).wait_recv()

                @pl.when(self.z == edge)
                def _():
                    self.r.from_z[n, self.z + 1 - way, :, :size] = jnp.zeros((self.chunk, size), low)

            total = (self.r.from_core[n, self.y, self.z, :, :size].astype(wide)
                     + self.r.from_z[n, self.z + 1, :, :size].astype(wide)
                     + self.r.from_z[n, self.z, :, :size].astype(wide))

            def keep():
                pl.when(i >= 2)(lambda: self.out_store(i - 2, 0, size).wait())
                self.r.staged_out[lax.rem(i, 2), :, :size] = total.astype(low)
                self.out_store(i, 0, size).start()

            if far:
                pl.when(self.y == 0)(keep)

                @pl.when(self.y == 1)
                def _():
                    pl.when(i >= self.slots)(lambda: self.far_copy(i - self.slots).wait_send())
                    self.credit(i, self.r.free.at[4])
                    self.r.far[0, n] = total.astype(low)
                    self.far_copy(i).start()
            else:
                keep()
            self.core_both(i, other).wait_send()
            self.y_copy(i, size).wait_send()
            block = self.r.from_z.at[n, pl.ds(0, self.last), :, pl.ds(0, size)]
            pltpu.make_async_remote_copy(
                block, block, self.r.send_z.at[n], self.r.recv_z.at[n, 0],
                device_id=self.to_y, device_id_type=MESH).wait_send()

        self.widths(action)

        @pl.when(i < self.count - self.slots)
        def _():
            def tell(index, target):
                pl.semaphore_signal(self.r.free.at[index], inc=1, device_id=target,
                                    device_id_type=MESH)

            tell(0, self.to_c)
            tell(1, self.to_y)
            pl.when(self.z > 0)(lambda: tell(2, {"mp": self.z - 1}))
            pl.when(self.z < self.last)(lambda: tell(3, {"mp": self.z + 1}))

    def land(self, i):
        n = self.slot(i)

        def action(size, other, far):
            if not far:
                return

            @pl.when(self.y == 0)
            def _():
                self.far_copy(i).wait_recv()
                pl.when(i >= 2)(lambda: self.out_store(i - 2, size, size).wait())
                self.r.staged_out[lax.rem(i, 2), :, size : 2 * size] = self.r.far[1, n]
                self.out_store(i, size, size).start()

                @pl.when(i < self.count - self.slots)
                def _():
                    pl.semaphore_signal(self.r.free.at[4], inc=1, device_id=self.to_y,
                                        device_id_type=MESH)

        self.widths(action)

    def zeros(self, s, zero):
        blocks = [(4 * self.chunk * n + self.used * self.chunk, self.inner - self.used * self.chunk)
                  for n in range(4)] if self.used * self.chunk < self.inner else []
        for start in (self.layout.down, self.layout.up):
            blocks += [(row, TILE) for row in range(start + s.units, start + self.layout.units, TILE)]
        number = 0
        for always, group in ((True, blocks), (False, [(row, TILE) for row in range(
                0, self.layout.total, TILE)] if self.text else [])):
            test = self.y + self.core == 2
            for row, size in group:
                yield (jnp.logical_not(test) if always and self.text else test if self.text
                       else self.y >= 0, pltpu.make_async_copy(
                    zero.at[pl.ds(0, size), pl.ds(0, TILE)],
                    self.r.reduced.at[pl.ds(row, size)], self.r.zero_sem.at[number]))
                number += 1

    def iteration(self, j):
        lag_b, lag_c, lag_z, lag_f = self.lags

        def at(i, stage):
            pl.when(jnp.logical_and(i >= 0, i < self.count))(lambda: stage(i))

        at(j, self.stage_a)
        at(j - lag_b, self.stage_b)
        at(j - lag_c, self.stage_c)
        for hop in range(2, self.groups):
            at(j - lag_c - lag_z * (hop - 1), partial(self.z_step, hop))
        done = lag_c + lag_z * (self.groups - 1)
        at(j - done, self.final)
        if self.text:
            at(j - done - lag_f, self.land)

    def iterations(self):
        lag_b, lag_c, lag_z, lag_f = self.lags
        return self.count + lag_c + lag_z * (self.groups - 1) + (lag_f if self.text else 0)

    def drained(self):
        def action(size, other, far):
            pair = (self.count - 2, self.count - 1)
            if not far:
                for i in pair:
                    self.out_store(jnp.int32(i), 0, size).wait()
                return

            @pl.when(self.y == 0)
            def _():
                for i in pair:
                    self.out_store(jnp.int32(i), 0, size).wait()
                    self.out_store(jnp.int32(i), size, size).wait()

            @pl.when(self.y == 1)
            def _():
                @pl.loop(self.count - self.slots, self.count)
                def _(i):
                    self.far_copy(i).wait_send()

        self.widths(action)


class Small:
    def __init__(self, plan, r):
        self.plan, self.r = plan, r
        self.count = plan.groups * plan.copies
        self.per_row = max(1, self.count // 16)
        self.width = r.small_in.shape[1] // self.per_row

    def piece(self, ref, index):
        row, part = index // self.per_row, lax.rem(index, self.per_row)
        return ref.at[pl.ds(row, 1), pl.ds(pl.multiple_of(part * self.width, 128), self.width)]

    def copy(self, offset, first):
        me, peer, target = peer_of(self.plan, offset)
        if first:
            src, dst = self.piece(self.r.small_in, peer), self.r.small_got.at[me]
        else:
            src, dst = self.r.small_sum, self.piece(self.r.small_out, me)
        n = 0 if first else 1
        return pltpu.make_async_remote_copy(
            src, dst, self.r.send_s.at[n], self.r.recv_s.at[n],
            device_id=target, device_id_type=MESH)

    def all(self, first):
        n = 0 if first else 1
        block = self.r.small_got.at[pl.ds(0, self.count - 1)]
        return pltpu.make_async_remote_copy(
            block, block, self.r.send_s.at[n], self.r.recv_s.at[n],
            device_id=peer_of(self.plan, 1)[2], device_id_type=MESH)

    def every(self, action):
        @pl.loop(1, self.count)
        def _(offset):
            action(offset)

    def start(self):
        self.every(lambda offset: self.copy(offset, True).start())

    def local(self, first):
        me = peer_of(self.plan, 0)[0]
        pair = ((self.piece(self.r.small_in, me), self.r.small_got.at[me]) if first
                else (self.r.small_sum, self.piece(self.r.small_out, me)))
        return pltpu.make_async_copy(*pair, self.r.small_sem.at[0 if first else 1])

    def middle(self):
        self.local(True).start()
        self.all(True).wait_recv()
        self.local(True).wait()
        self.r.small_sum[...] = jnp.sum(self.r.small_got[...], axis=0)
        self.local(False).start()
        self.every(lambda offset: self.copy(offset, False).start())

    def finish(self):
        self.local(False).wait()
        self.all(False).wait_recv()
        for first in (True, False):
            self.all(first).wait_send()


def run_stream(which, s, layout, plan, r):
    groups, inner, length = plan.groups, plan.inner, plan.length
    rows_dev = plan.rows
    tokens = plan.tokens
    w, u = s.width, s.units
    z = lax.axis_index("mp")
    side = lax.axis_index("stream")
    gather = Gather(s, plan, r)
    weights = Weights(s, plan, r)
    outputs = Outputs(s, plan, r)
    reduce = Reduce(which, s, layout, plan, r)
    small = Small(plan, r)

    gather.begin(2)
    own_rows = pl.ds(pl.multiple_of(z * tokens, tokens), tokens)
    enter = [pltpu.make_async_copy(r.hidden.at[own_rows], r.x, r.enter_sem.at[0]),
             pltpu.make_async_copy(r.cotangent.at[own_rows], r.grad_out, r.enter_sem.at[1])]
    for item in enter:
        item.start()
    weights.load_own("k", "v", "q", "cross_out", "up", "down", "attend_out")

    def bias_copy(step, kind):
        ref, full = ((r.cross_bias, r.a_cross_bias), (r.attend_bias, r.a_attend_bias),
                     (r.up_bias, r.a_up_bias))[kind]
        return pltpu.make_async_remote_copy(
            ref, full.at[z], r.send_b.at[kind], r.recv_b.at[kind],
            device_id={"mp": lax.rem(z + step, groups)}, device_id_type=MESH)

    for kind, (ref, full) in enumerate(((r.cross_bias, r.a_cross_bias),
                                        (r.attend_bias, r.a_attend_bias),
                                        (r.up_bias, r.a_up_bias))):
        for step in range(1, groups):
            bias_copy(step, kind).start()
        full[z] = ref[...]

    r.zero[...] = jnp.zeros_like(r.zero)
    r.low_grad[:, :TILE] = jnp.zeros((tokens, TILE), low)
    for test, item in reduce.zeros(s, r.low_grad):
        pl.when(test)(item.start)

    def swap(source, target, number):
        return pltpu.make_async_remote_copy(
            source, target, r.send_x.at[number], r.recv_x.at[number],
            device_id={"stream": 1 - side}, device_id_type=MESH)

    self_kinds = block_kinds(s.head, s.per_group)
    cross_kinds = block_kinds(128, CO_HEADS // groups)
    self_scale, cross_scale = 1.0 / math.sqrt(s.head), 1.0 / math.sqrt(128)

    def in_block(index):
        return pl.ds(pl.multiple_of(index * w, TILE), w)

    def project(part, source, target, bias_ref, line):
        @pl.loop(0, groups)
        def _(g):
            cols = lane(g * inner, inner)
            value = dot(source[:, :w], r.w_in[in_block(g * 3 + part), :])
            if line is not None:
                value = value + bias_ref[g, line : line + 1].astype(wide)
            target[:, cols] = value.astype(low)

    def vector(ref, line, cols=slice(0, w)):
        return ref[line : line + 1, cols].astype(wide)

    def scaled(normal, line, cols):
        return normal[:, cols] * vector(r.gains, line, cols) + vector(r.shifts, line, cols)

    def leave(source, size, weight, residual, line):
        @pl.loop(0, s.parts)
        def _(j):
            cols = lane(j * TILE)
            at = pl.ds(pl.multiple_of(j * size, TILE), size)
            r.acc[:, cols] = (dot(source[:, :size], weight[at, :]) + residual(cols)
                              + vector(r.out_bias, line, cols))

    strip = 64

    def strips(action):
        @pl.loop(0, tokens // strip)
        def _(k):
            action(pl.ds(pl.multiple_of(k * strip, strip), strip))

    def norm(normal, inverse, line, low_out):
        def action(at):
            summed = r.acc[at, :w]
            mean = jnp.sum(summed, axis=-1, keepdims=True) * (1.0 / w)
            centred = summed - mean
            scale = lax.rsqrt(
                jnp.sum(centred * centred, axis=-1, keepdims=True) * (1.0 / w) + norm_eps)
            normal[at, :w] = centred * scale
            inverse[at, :] = scale
            low_out[at, :w] = (
                centred * scale * vector(r.gains, line) + vector(r.shifts, line)).astype(low)

        strips(action)

    def cross_part(begin, end):
        @pl.loop(begin, end)
        def _(g):
            attend_forward(g, cross_kinds, cross_scale, length, rows_dev, r.q, r.pair_k, r.pair_v,
                           r.cross_allowed, r.cross_prob, r.context)

    def feed_part(begin, end):
        @pl.loop(begin, end)
        def _(g):
            for j in range(u // TILE):
                cols = lane(g * u + j * TILE)
                value = (dot(r.h1[:, :w], r.w_up[in_block(g * (u // TILE) + j), :])
                         + r.a_up_bias[g, 0:1, j * TILE : (j + 1) * TILE].astype(wide))
                bell = 0.5 * (1.0 + lax.erf(value * math.sqrt(0.5)))
                r.active[:, cols] = (value * bell).astype(low)
                r.slope[:, cols] = bell + value * (
                    jnp.exp(-0.5 * value * value) * (1.0 / math.sqrt(2.0 * math.pi)))

    def do_key():
        gather.settled(weights, "k")
        for item in enter:
            item.wait()
        weights.wait("k")
        project(1, r.x, r.k, None, None)
        swap(r.k, r.pair_k, 0).start()

    def do_value():
        gather.settled(weights, "v")
        for kind, full in enumerate((r.a_cross_bias, r.a_attend_bias, r.a_up_bias)):
            block = full.at[pl.ds(0, groups - 1)]
            pltpu.make_async_remote_copy(
                block, block, r.send_b.at[kind], r.recv_b.at[kind],
                device_id={"mp": lax.rem(z + 1, groups)}, device_id_type=MESH).wait()
        weights.wait("v")
        project(2, r.x, r.v, r.a_cross_bias, 1)
        swap(r.v, r.pair_v, 1).start()

    def do_query():
        gather.settled(weights, "q")
        weights.wait("q")
        project(0, r.x, r.q, r.a_cross_bias, 0)
        weights.load_own("attend_q", "attend_k", "attend_v")

    def do_cross_first():
        gather.settled(weights, "cross_out")
        swap(r.k, r.pair_k, 0).wait()
        swap(r.v, r.pair_v, 1).wait()
        cross_part(0, groups // 2)

    def do_cross_second():
        cross_part(groups // 2, groups)
        gather.settled(weights, "up")

    def do_first_norm():
        for test, item in reduce.zeros(s, r.low_grad):
            pl.when(test)(item.wait)
        weights.wait("cross_out")
        leave(r.context, groups * inner, r.w_cross_out, lambda cols: r.x[:, cols].astype(wide), 0)
        norm(r.n1, r.r1, 0, r.h1)

    def do_feed_first():
        weights.wait("up")
        feed_part(0, groups // 2)
        gather.settled(weights, "down")

    def do_feed_second():
        feed_part(groups // 2, groups)

    def do_second_norm():
        weights.wait("down")
        leave(r.active, groups * u, r.w_down, lambda cols: scaled(r.n1, 0, cols), 1)
        norm(r.n2, r.r2, 1, r.h2)

    work = dict(zip(plan.forward[which], (
        do_key, do_value, do_query, do_cross_first, do_cross_second, do_first_norm,
        do_feed_first, do_feed_second, do_second_norm)))
    for i in range(gather.waves() + 1):
        gather.wave(i, 2)
        if i in work:
            work[i]()
    if len(plan.forward[which]) < 9:
        do_second_norm()
    for name, part, target, bias_ref, line in (
            ("attend_q", 0, r.q2, r.a_attend_bias, 0), ("attend_k", 1, r.k2, None, None),
            ("attend_v", 2, r.v2, r.a_attend_bias, 1)):
        gather.settled(weights, name)
        weights.wait(name)
        project(part, r.h2, target, bias_ref, line)
    gather.settled(weights, "attend_out")

    @pl.loop(0, groups)
    def _(g):
        attend_forward(g, self_kinds, self_scale, length, rows_dev, r.q2, r.k2, r.v2,
                       r.self_allowed, r.self_prob, r.context2)

    weights.wait("attend_out")
    leave(r.context2, groups * inner, r.w_attend_out, lambda cols: scaled(r.n2, 1, cols), 2)
    norm(r.n3, r.r3, 2, r.layer_rows)

    def store(row, g):
        return pltpu.make_async_copy(
            r.staged.at[g, :, pl.ds(0, w)],
            r.grads.at[g, pl.ds(pl.multiple_of(row, TILE), TILE), pl.ds(0, w)],
            r.store_sem.at[g])

    def weight_grads(left, right, row, size):
        def step(k):
            @pl.loop(0, groups)
            def _(g):
                r.staged[g, :, :w] = dot_tn(left(lane(g * size + k * TILE)), right[:, :w]).astype(low)
                store(row + k * TILE, g).start()

        return step

    def flush():
        pl.loop(0, groups)(lambda g: store(0, g).wait())

    def back_norm(source, normal, inverse, line):
        def action(at):
            incoming = source[at, :w].astype(wide)
            r.small_in[3 + line : 4 + line, :w] += down_sum(incoming * normal[at, :w])
            r.small_in[6 + line : 7 + line, :w] += down_sum(incoming)
            out = norm_back(normal[at, :w], inverse[at, :], vector(r.gains, line), incoming, w)
            r.acc[at, :w] = out
            r.low_grad[at, :w] = out.astype(low)
            r.small_in[line : line + 1, :w] += down_sum(out.astype(low).astype(wide))

        strips(action)

    def leave_back(weight, size, row, count):
        total = None
        for j in range(s.parts):
            at = pl.ds(pl.multiple_of(j * size + row, TILE), count)
            part = dot_nt(r.low_grad[:, j * TILE : (j + 1) * TILE], weight[at, :])
            total = part if total is None else total + part
        return total

    def enter_back(d, weight, blocks):
        def step(g):
            total = r.acc[:, :w]
            for b, (ref, start) in enumerate(d(g)):
                total = total + dot_nt(ref[:, lane(start)], weight[in_block(g * blocks + b), :])
            r.acc[:, :w] = total

        return step

    def context_back(weight):
        def step(g):
            r.grad_context[:, lane(g * inner, inner)] = leave_back(
                weight, groups * inner, g * inner, inner).astype(low)

        return step

    def self_step(g):
        attend_backward(g, self_kinds, self_scale, length, rows_dev, r.q2, r.k2, r.v2,
                        r.self_prob, r.grad_context, r.d.at[0], r.d.at[1], r.d.at[2])

    def cross_step(g):
        attend_backward(g, cross_kinds, cross_scale, length, rows_dev, r.q, r.pair_k, r.pair_v,
                        r.cross_prob, r.grad_context, r.d.at[0], r.d.at[1], r.d.at[2])

    def second_norm(_):
        r.small_in[12:13, :] = down_sum(r.d[0].astype(wide))
        r.small_in[13:14, :] = down_sum(r.d[2].astype(wide))
        weights.load_own("q", "k", "v")
        weights.load_rest("q", "k", "v")
        back_norm(r.acc, r.n2, r.r2, 1)

    def slope_step(g):
        for j in range(u // TILE):
            cols = lane(g * u + j * TILE)
            value = leave_back(r.w_down, groups * u, g * u + j * TILE, TILE)
            r.dz[:, cols] = (value * r.slope[:, cols]).astype(low)

    def first_norm(_):
        back_norm(r.acc, r.n1, r.r1, 0)
        units, width = plan.units, r.small_in.shape[1]
        for g in range(groups):
            for j in range(u // TILE):
                start = g * units + j * TILE
                r.small_in[9 + start // width : 10 + start // width,
                           start % width : start % width + TILE] = down_sum(
                    r.dz[:, g * u + j * TILE : g * u + (j + 1) * TILE].astype(wide))

    def pair_send(_):
        r.small_in[14:15, :] = down_sum(r.d[0].astype(wide))
        weights.wait("q", "k", "v")
        swap(r.d.at[1], r.back.at[0], 2).start()
        swap(r.d.at[2], r.back.at[1], 3).start()

    def pair_take(_):
        swap(r.d.at[1], r.back.at[0], 2).wait()
        swap(r.d.at[2], r.back.at[1], 3).wait()
        r.small_in[15:16, :] = down_sum(r.back[1].astype(wide))
        small.start()

    def hidden_store(_):
        r.hidden_rows[:, :w] = r.acc[:, :w].astype(low)
        for item in outputs.local(1):
            item.start()

    def layer_send(_):
        outputs.begin(0)
        for item in outputs.local(0):
            item.start()

    def drain_gather(_):
        for p in range(len(gather.pieces)):
            gather.drained(p)

    def attend_grads(k):
        weight_grads(lambda cols: r.d[k, :, cols], r.h2, layout.attend_in + k * inner, inner)(0)

    def cross_grads(k):
        weight_grads(lambda cols: r.back[k, :, cols], r.x,
                     layout.cross_in + (1 + k) * inner, inner)(0)

    def of(ref):
        return lambda cols: ref[:, cols]

    r.small_in[...] = jnp.zeros_like(r.small_in)
    back_norm(r.grad_out, r.n3, r.r3, 2)
    weight_grads(of(r.context2), r.low_grad, layout.attend_out, inner)(0)
    nb = u // TILE
    take = plan.when[which]
    schedule = (
        (0, 4, 4, False, context_back(r.w_attend_out)),
        (0, 4, 2, False, self_step),
        (1, 1, 1, False, layer_send),
        (2, 3, 1, True, attend_grads),
        (2, 4, 2, False, enter_back(lambda g: [(d, g * inner) for d in (r.d.at[0], r.d.at[1], r.d.at[2])],
                                    r.w_in, 3)),
        (4, 1, 1, False, second_norm),
        (5, 4, 2, False, slope_step),
        (5, nb, 1, True, weight_grads(of(r.active), r.low_grad, layout.down, u)),
        (5 + nb, nb, 1, True, weight_grads(of(r.dz), r.h1, layout.up, u)),
        (7, 4, 2, False, enter_back(lambda g: [(r.dz, g * u + b * TILE) for b in range(nb)],
                                    r.w_up, nb)),
        (9, 1, 1, False, first_norm),
        (10, 4, 2, False, context_back(r.w_cross_out)),
        (12, 4, 2, False, cross_step),
        (14, 1, 1, False, pair_send),
        (11, 1, 1, True, weight_grads(of(r.context), r.low_grad, layout.cross_out, inner)),
        (15, 1, 1, True, weight_grads(of(r.d.at[0]), r.x, layout.cross_in, inner)),
        (take, 1, 1, False, pair_take),
        (take, 2, 1, True, cross_grads),
        (take + 2, 4, 2, False, enter_back(
            lambda g: [(d, g * inner) for d in (r.d.at[0], r.back.at[0], r.back.at[1])], r.w_in, 3)),
        (take + 4, 1, 1, False, hidden_store),
        (take + 5, 1, 1, False, lambda _: small.middle()),
        (17, 1, 1, False, drain_gather),
        (take + 6, 1, 1, False, lambda _: outputs.drained(0)),
        (take + 12, 1, 1, False, lambda _: small.finish()),
    )
    storing = sorted({start + n for start, steps, per, keeps, _ in schedule if keeps
                      for n in range(steps)})
    assert len(storing) == sum(steps for _, steps, _, keeps, _ in schedule if keeps)
    hidden_at = take + 5

    @pl.loop(0, max(reduce.iterations(), hidden_at + plan.cuts + PACE * groups))
    def _(j):
        flushes = j == 0
        for n in storing:
            flushes = jnp.logical_or(flushes, j == n + 1)
        pl.when(flushes)(flush)
        reduce.iteration(j)
        for start, steps, per, _, step in schedule:
            @pl.when(jnp.logical_and(j >= start, j < start + steps // per))
            def _():
                if per == 1:
                    step(j - start)
                else:
                    pl.loop(0, per)(lambda n: step((j - start) * per + n))
        outputs.step(0, j - 1, True)
        outputs.step(1, j - hidden_at)

    reduce.drained()
    outputs.drained(1)


def place_kernel(layout, groups, copies, layer_in, hidden_in, reduced, small, layer_out, hidden_out,
                 cross_in, attend_in, cross_out, attend_out, up, down,
                 cross_bias, attend_bias, up_bias, out_bias, gains, shifts,
                 held, rows, tall, flat_out, turned, load_sem, store_sem):
    inner = cross_out.shape[0]
    units = down.shape[0]
    copy = lax.axis_index("dp")
    me = lax.axis_index("mp") * copies + copy
    blocks = layout.total // inner
    loads = [pltpu.make_async_copy(
        reduced.at[pl.ds(n * inner, inner)], rows.at[n], load_sem.at[n]) for n in range(blocks)]
    stores = []

    def store(src, dst):
        stores.append(pltpu.make_async_copy(src, dst, store_sem.at[len(stores)]))
        stores[-1].start()

    large = [(pair, z) for pair in ((layer_in, layer_out, 0), (hidden_in, hidden_out, 1))
             for z in range(groups)]
    carries = [pltpu.make_async_copy(source.at[z], held.at[n, z], load_sem.at[blocks + k])
               for k, ((source, _, n), z) in enumerate(large)]
    for item in loads[:1] + carries + loads[1:]:
        item.start()

    def turn(n, slot):
        loads[n].wait()
        turned[slot] = rows[n].astype(wide).T

    def keep(n, slot):
        loads[n].wait()
        flat_out[slot] = rows[n].astype(wide)

    first = {name: getattr(layout, name) // inner for name in (
        "attend_out", "attend_in", "down", "up", "cross_out", "cross_in")}
    keep(first["attend_out"], 0)
    store(flat_out.at[0], attend_out)
    for item, ((_, target, n), z) in zip(carries, large):
        item.wait()
        store(held.at[n, z], target.at[z])
    for k in range(3):
        turn(first["attend_in"] + k, k)
        store(turned.at[k], attend_in.at[k])
    for j in range(units // inner):
        keep(first["down"] + j, 2 + j)
        store(flat_out.at[2 + j], down.at[pl.ds(j * inner, inner)])
    for j in range(units // inner):
        loads[first["up"] + j].wait()
        tall[:, j * inner : (j + 1) * inner] = rows[first["up"] + j].astype(wide).T
    store(tall, up)
    keep(first["cross_out"], 1)
    store(flat_out.at[1], cross_out)
    for k in range(3):
        turn(first["cross_in"] + k, 3 + k)
        store(turned.at[3 + k], cross_in.at[k])

    def share(value, start, size):
        width = value.shape[1]
        return pltpu.roll(value, lax.rem(width - start, width), 1)[:, :size]

    columns = down.shape[1]
    values = share(small[...], copy * columns, columns)
    for ref, row in ((out_bias, 0), (gains, 3), (shifts, 6)):
        for k in range(3):
            ref[k] = values[row + k : row + k + 1]
    sides = share(small[...], me * (inner // copies), inner // copies)
    attend_bias[...] = sides[12:14]
    cross_bias[...] = sides[14:16]
    flat = jnp.concatenate([small[9:10], small[10:11], small[11:12]], axis=1)
    up_bias[...] = share(flat, me * (units // copies), units // copies)
    for item in stores:
        item.wait()


def shards(
    hidden,
    cotangent,
    segments,
    cross_in,
    cross_bias,
    cross_out,
    up_weight,
    up_bias,
    down_weight,
    attend_in,
    attend_bias,
    attend_out,
    out_bias,
    norm_gains,
    norm_shifts,
):
    groups = lax.axis_size("mp")
    copies = lax.axis_size("dp")
    stride = copies // 4
    side = lax.axis_index("stream")
    member = lax.axis_index("mp")
    copy = lax.axis_index("dp")
    inner = cross_in.shape[3]
    padded = hidden.shape[2]
    units = up_weight.shape[2]
    length = segments.shape[2]
    text = Setting(TEXT_WIDTH, TEXT_HEADS, TEXT_FF, groups)
    image = Setting(IMAGE_WIDTH, IMAGE_HEADS, IMAGE_FF, groups)
    settings = (text, image)
    layout = Layout(inner, units)
    rows_max = layout.total
    rows_dev = segments.shape[1] // groups
    tokens = hidden.shape[1] // groups
    co = groups * inner

    def shape(dims, kind=low):
        return jax.ShapeDtypeStruct(dims, kind)

    seg = lax.dynamic_slice_in_dim(segments, member * rows_dev, rows_dev, 1)
    seg_own = lax.dynamic_index_in_dim(seg, side, 0, keepdims=False)
    seg_other = lax.dynamic_index_in_dim(seg, 1 - side, 0, keepdims=False)
    cross_allowed = (seg_other[:, :, None] == seg_own[:, None, :]).astype(wide)
    self_allowed = (seg_own[:, :, None] == seg_own[:, None, :]).astype(wide)

    dma = pltpu.SemaphoreType.DMA

    def real(*dims):
        return pltpu.VMEM(dims, wide)

    def short(*dims):
        return pltpu.VMEM(dims, low)

    chunk, slots, cuts, ring = 64, 20, 8, 4
    widest = max(s.units for s in settings) * groups
    up_rows = max(groups * s.units * s.width for s in settings) // TILE
    heads = max(groups * s.per_group for s in settings)
    pieces, hops = 8 + 2 * max(s.units for s in settings) // TILE, groups - 1
    peers = groups * copies
    small_width = padded // max(1, peers // 16)
    scratch = Scratch(
        w_in=short(groups * 3 * padded, inner),
        w_cross_out=short(padded // TILE * co, TILE),
        w_attend_out=short(padded // TILE * co, TILE),
        w_up=short(up_rows, TILE),
        w_down=short(up_rows, TILE),
        x=short(tokens, padded),
        grad_out=short(tokens, padded),
        q=short(tokens, co),
        k=short(tokens, co),
        v=short(tokens, co),
        pair_k=short(tokens, co),
        pair_v=short(tokens, co),
        back=short(2, tokens, co),
        cross_prob=real(CO_HEADS * rows_dev, length, length),
        self_prob=real(heads * rows_dev, length, length),
        context=short(tokens, co),
        context2=short(tokens, co),
        acc=real(tokens, padded),
        n1=real(tokens, padded),
        n2=real(tokens, padded),
        n3=real(tokens, padded),
        r1=real(tokens, 1),
        r2=real(tokens, 1),
        r3=real(tokens, 1),
        h1=short(tokens, padded),
        h2=short(tokens, padded),
        slope=real(tokens, widest),
        active=short(tokens, widest),
        dz=short(tokens, widest),
        q2=short(tokens, co),
        k2=short(tokens, co),
        v2=short(tokens, co),
        d=short(3, tokens, co),
        low_grad=short(tokens, padded),
        grad_context=short(tokens, co),
        layer_rows=short(tokens, padded),
        hidden_rows=short(tokens, padded),
        zero=short(tokens, IMAGE_WIDTH - TEXT_WIDTH),
        staged=short(ring, TILE, padded),
        from_core=short(slots, 2, groups, chunk, TILE),
        from_y=short(slots, groups, chunk, TILE),
        from_z=short(slots, groups + 1, chunk, TILE),
        far=short(2, slots, chunk, 128),
        own=short(4, 2, groups, chunk, TILE),
        staged_out=short(2, chunk, TILE),
        small_in=real(16, padded),
        small_got=real(peers, 1, small_width),
        small_sum=real(1, small_width),
        small_sem=dma((2,)),
        a_cross_bias=short(groups, 2, inner),
        a_attend_bias=short(groups, 2, inner),
        a_up_bias=short(groups, 1, units),
        send_gz=dma((pieces,)),
        recv_gz=dma((pieces, groups)),
        send_gy=dma((pieces,)),
        recv_gy=dma((pieces,)),
        send_gc=dma((pieces,)),
        recv_gc=dma((pieces,)),
        weight_sem=dma((pieces,)),
        enter_sem=dma((2,)),
        send_b=dma((3,)),
        recv_b=dma((3,)),
        send_x=dma((4,)),
        recv_x=dma((4,)),
        store_sem=dma((ring,)),
        send_c=dma((slots,)),
        recv_c=dma((slots,)),
        send_y=dma((slots,)),
        recv_y=dma((slots,)),
        send_z=dma((slots,)),
        recv_z=dma((slots, groups + 1)),
        send_f=dma((slots,)),
        recv_f=dma((slots,)),
        own_sem=dma((4,)),
        out_sem=dma((2, 2)),
        send_a=dma((2, 2)),
        recv_a=dma((2, cuts, groups)),
        local_sem=dma((2, groups + 1)),
        send_s=dma((2,)),
        recv_s=dma((2,)),
        free=pltpu.SemaphoreType.REGULAR((5,)),
        zero_sem=dma((4 + rows_max // TILE,)),
    )
    plan = Plan(
        groups=groups, copies=copies, inner=inner, length=length, rows=rows_dev,
        tokens=tokens, units=units, chunk=chunk, slots=slots, cuts=cuts,
        ring=ring, lags=(1, 8, 2, 2),
        when=(25, 25),
        forward=((4, 5, 6, 10, 11, 12, 13, 14, 15), (4, 5, 6, 8, 9, 10, 11, 12)),
    )
    weights = (
        jnp.swapaxes(cross_in[0], 0, 1),
        cross_out[0],
        up_weight[0],
        down_weight[0],
        jnp.swapaxes(attend_in[0], 0, 1),
        attend_out[0],
    )
    line = shape((groups, tokens, padded))
    out = pl.pallas_call(
        partial(layer_kernel, settings, layout, plan),
        out_shape=(
            line, line, shape((rows_max, TILE)), shape((16, padded), wide),
        ) + tuple(shape((groups,) + w.shape) for w in weights)
        + (shape((groups, rows_max, padded)),),
        in_specs=[ANY] * 8 + [VMEM] * 8,
        out_specs=(ANY,) * 3 + (VMEM,) + (ANY,) * 7,
        scratch_shapes=list(scratch),
        compiler_params=pltpu.CompilerParams(
            collective_id=0, has_side_effects=True, vmem_limit_bytes=VMEM_LIMIT),
        name="layer",
    )(*weights, hidden[0], cotangent[0], cross_bias[0], attend_bias[0], up_bias,
      out_bias[0], norm_gains[0], norm_shifts[0],
      cross_allowed.reshape(tokens, length), self_allowed.reshape(tokens, length))
    layer_out, hidden_grad, reduced, small = out[:4]

    if stride > 1:
        teams = [[q * stride + b for b in range(stride)] for q in range(4)]
        reduced = lax.psum_scatter(
            reduced, "dp", scatter_dimension=1, axis_index_groups=teams, tiled=True)

    columns, part = padded // copies, inner // copies
    shapes = (
        line, line, shape((3, columns, inner), wide), shape((3, columns, inner), wide),
        shape((inner, columns), wide), shape((inner, columns), wide),
        shape((columns, units), wide), shape((units, columns), wide),
        shape((2, part), wide), shape((2, part), wide), shape((1, units // copies), wide),
    ) + (shape((3, 1, columns), wide),) * 3
    (layer_out, hidden_grad, g_cross_in, g_attend_in, g_cross_out, g_attend_out, g_up, g_down,
     g_cross_bias, g_attend_bias, g_up_bias, g_out_bias, g_gains, g_shifts) = pl.pallas_call(
        partial(place_kernel, layout, groups, copies),
        out_shape=shapes,
        in_specs=[HBM] * 3 + [VMEM],
        out_specs=(HBM,) * 8 + (VMEM,) * 6,
        scratch_shapes=[
            short(2, groups, tokens, padded), short(rows_max // inner, inner, columns),
            real(columns, units), real(2 + units // inner, inner, columns),
            real(6, columns, inner), dma((rows_max // inner + 2 * groups,)),
            dma((9 + units // inner + 2 * groups,)),
        ],
        compiler_params=pltpu.CompilerParams(vmem_limit_bytes=VMEM_LIMIT),
        name="place",
    )(layer_out, hidden_grad, reduced, small)
    return (
        layer_out.reshape(1, groups * tokens, padded),
        hidden_grad.reshape(1, groups * tokens, padded),
        g_cross_in.transpose(1, 0, 2)[None],
        g_cross_bias[None],
        g_cross_out[None],
        g_up[None],
        g_up_bias,
        g_down[None],
        g_attend_in.transpose(1, 0, 2)[None],
        g_attend_bias[None],
        g_attend_out[None],
        g_out_bias.transpose(1, 0, 2),
        g_gains.transpose(1, 0, 2),
        g_shifts.transpose(1, 0, 2),
    )


def solution(mesh):
    placed = (
        P("stream", "dp", None),
        P("stream", "dp", None),
        P(None, "dp", None),
        P("stream", None, None, "mp"),
        P("stream", None, "mp"),
        P("stream", "mp", None),
        P("stream", None, "mp"),
        P("stream", "mp"),
        P("stream", "mp", None),
        P("stream", None, None, "mp"),
        P("stream", None, "mp"),
        P("stream", "mp", None),
        P("stream", None, None),
        P("stream", None, None),
        P("stream", None, None),
    )
    return jax.shard_map(
        shards,
        mesh=mesh,
        in_specs=placed,
        out_specs=(
            P("stream", "dp", None),
            P("stream", "dp", None),
            P("stream", "dp", None, "mp"),
            P("stream", None, ("mp", "dp")),
            P("stream", "mp", "dp"),
            P("stream", "dp", "mp"),
            P("stream", ("mp", "dp")),
            P("stream", "mp", "dp"),
            P("stream", "dp", None, "mp"),
            P("stream", None, ("mp", "dp")),
            P("stream", "mp", "dp"),
            P("stream", None, "dp"),
            P("stream", None, "dp"),
            P("stream", None, "dp"),
        ),
        check_vma=False,
    )
```
